32 devices in a mesh: dp: 4 (over y, core), fsdp: 8 (over z, x).
Axes of the slice: x: 2, y: 2, z: 4, core: 2. Of those that a mesh axis runs over, the one named last changes fastest.
Arguments:
- latents: int32 [256, 64, 32], P(('dp', 'fsdp')), may hold values from 0 to 31
- actions: int32 [256, 64], P(('dp', 'fsdp')), may hold values from 0 to 17, as said below
- game_ids: int32 [256], P(('dp', 'fsdp')), may hold values from 0 to 25
- action_masks: int32 [26, 18], replicated, may hold values from 0 to 1, as said below
- valid_steps: int32 [256, 64], P(('dp', 'fsdp')), may hold values from 0 to 1, as said below
- target_bins: int32 [256, 64, 2], P(('dp', 'fsdp')), may hold values from 0 to 253
- target_fracs: float32 [256, 64, 2], P(('dp', 'fsdp')), may hold values from 0 to 1
- continues: int32 [256, 64], P(('dp', 'fsdp')), may hold values 0 or 1
- owner_order: int32 [192], replicated, may hold values from 0 to 191, each once
- blocks: float32 [192, 128, 128], P('fsdp'), may hold values from -0.25 to 0.25
- block_first: float32 [192, 128, 128], P('fsdp'), may hold values from -1.5258789e-05 to 1.5258789e-05
- block_second: float32 [192, 128, 128], P('fsdp'), may hold values from 5.649883e-12 to 2.2554868e-11
- left_stat: float32 [192, 128, 128], P('fsdp'), may hold values from -2.85843873e-09 to 2.9156075e-09, as said below
- right_stat: float32 [192, 128, 128], P('fsdp'), may hold values from -2.85843873e-09 to 2.9156075e-09, as said below
- left_basis: float32 [192, 128, 128], P('fsdp'), may hold values from -1 to 1, as said below
- right_basis: float32 [192, 128, 128], P('fsdp'), may hold values from -1 to 1, as said below
- latent_maps: float32 [2048, 512], P('fsdp'), may hold values from -0.625 to 0.625
- latent_first: float32 [2048, 512], P('fsdp'), may hold values from -1.5258789e-05 to 1.5258789e-05
- latent_second: float32 [2048, 512], P('fsdp'), may hold values from 5.649883e-12 to 2.2554868e-11
- head_weights: float32 [513, 529], replicated, may hold values from -0.625 to 0.625
- head_first: float32 [513, 529], replicated, may hold values from -1.5258789e-05 to 1.5258789e-05
- head_second: float32 [513, 529], replicated, may hold values from 5.649883e-12 to 2.2554868e-11
- small_params: float32 [24, 512], replicated
- small_first: float32 [24, 512], replicated, may hold values from -1.5258789e-05 to 1.5258789e-05
- small_second: float32 [24, 512], replicated, may hold values from 5.649883e-12 to 2.2554868e-11
- ema_critic: float32 [513, 255], replicated, may hold values from -0.15625 to 0.15625
Outputs:
- loss: float32 [], replicated
- grad_norm: float32 [], replicated
- blocks_new: float32 [192, 128, 128], P('fsdp')
- block_first_new: float32 [192, 128, 128], P('fsdp')
- block_second_new: float32 [192, 128, 128], P('fsdp')
- left_stat_new: float32 [192, 128, 128], P('fsdp')
- right_stat_new: float32 [192, 128, 128], P('fsdp')
- left_basis_new: float32 [192, 128, 128], P('fsdp')
- right_basis_new: float32 [192, 128, 128], P('fsdp')
- latent_maps_new: float32 [2048, 512], P('fsdp')
- latent_first_new: float32 [2048, 512], P('fsdp')
- latent_second_new: float32 [2048, 512], P('fsdp')
- head_weights_new: float32 [513, 529], replicated
- head_first_new: float32 [513, 529], replicated
- head_second_new: float32 [513, 529], replicated
- small_params_new: float32 [24, 512], replicated
- small_first_new: float32 [24, 512], replicated
- small_second_new: float32 [24, 512], replicated
- ema_critic_new: float32 [513, 255], replicated
The draws below stay inside these ranges and needn't reach their ends.
Inputs may be any that keep to these rules, and one draw needn't show every extreme that they name: `actions`: every action is legal in its sequence's game. `action_masks`: every game allows action 0. `valid_steps`: each sequence is 1 on a prefix of 16 frames or more and 0 after it. `owner_order`: a permutation of the blocks. `left_stat`: symmetric positive definite. `right_stat`: symmetric positive definite. `left_basis`: orthogonal. `right_basis`: orthogonal.
All inputs are finite; a program needn't handle non-finite values. Where the reference program divides by a largest or mean magnitude, that divisor is 1e-20 or more. No bound on the sum of `continues` on one device may be relied on, other than what follows from the above.
Results may differ from the reference program's by a relative error of at most 0.0053.
Values may be sent and summed in bfloat16 or wider, within the bound.
No kernel may reach another device: no remote copies, remote signals or barrier semaphores. Data moves between devices by JAX's collectives and lax.ppermute only.
A program may use at most 192 MiB of HBM per device.

```python
import math
import jax
import jax.numpy as jnp
from jax import lax

D = 512
NH = 8
DH = 64
FF = 2048
GROUPS = 32
CLASSES = 32
LAT = 1024
BINS = 255
NA = 18
LAYERS = 1
F = 64
SEQS = 256
NGAME = 26
BS = 128
STEP = 10
NB = 192
OUTS = 529
SR = 24
PARAMS = 4477969


def game_table(key):
    coin_bits = jax.random.randint(jax.random.fold_in(key, 11), (NGAME, NA), 0, 5) < 3
    column_zero = jnp.arange(NA)[None, :] == 0
    return jnp.where(coin_bits | column_zero, 1, 0).astype(jnp.int32)


def game_list(key):
    return jax.random.randint(jax.random.fold_in(key, 12), (SEQS,), 0, NGAME).astype(jnp.int32)


def draw_action_masks(key, part):
    return game_table(key)


def draw_game_ids(key, part):
    return game_list(key)


def draw_actions(key, part):
    table = game_table(key)
    chosen_games = game_list(key)
    proposed = jax.random.randint(jax.random.fold_in(key, 13), (SEQS, F), 0, NA).astype(jnp.int32)
    legal = jnp.take_along_axis(table[chosen_games], proposed, 1)
    return jnp.where(legal > 0, proposed, 0).astype(jnp.int32)


def draw_valid_steps(key, part):
    seq_index = jnp.arange(SEQS)
    shortest = F // 4 + 5 * F // 8 * seq_index // SEQS
    length = shortest + jax.random.randint(jax.random.fold_in(key, 14), (SEQS,), 0, F // 8 + 1)
    return (jnp.arange(F)[None, :] < length[:, None]).astype(jnp.int32)


def make_stat(key, salt):
    subkey = jax.random.fold_in(key, salt)
    base_level = 0.0101 * BS * 0.0025 / PARAMS
    level = base_level * jnp.exp(jax.random.uniform(jax.random.fold_in(subkey, 1), (NB, 1, 1), jnp.float32, 0.0, 1.3863))
    noise = jax.random.uniform(jax.random.fold_in(subkey, 2), (NB, BS, BS), jnp.float32, -1.0, 1.0)
    symmetric = (noise + jnp.swapaxes(noise, 1, 2)) * (0.37 / BS ** 0.5)
    identity = jnp.eye(BS, dtype=jnp.float32)[None]
    return level * (identity + symmetric * (1.0 - identity))


def make_basis(key, salt):
    subkey = jax.random.fold_in(key, salt)
    first_vec = jax.random.normal(jax.random.fold_in(subkey, 1), (NB, BS), jnp.float32)
    second_vec = jax.random.normal(jax.random.fold_in(subkey, 2), (NB, BS), jnp.float32)
    first_len = jnp.sum(first_vec * first_vec, -1)[:, None, None]
    second_len = jnp.sum(second_vec * second_vec, -1)[:, None, None]
    cross = jnp.sum(first_vec * second_vec, -1)[:, None, None]
    identity = jnp.eye(BS, dtype=jnp.float32)[None]
    outer_first = first_vec[:, :, None] * first_vec[:, None, :]
    outer_second = second_vec[:, :, None] * second_vec[:, None, :]
    outer_mixed = first_vec[:, :, None] * second_vec[:, None, :]
    return identity - 2.0 * outer_first / first_len - 2.0 * outer_second / second_len + 4.0 * cross * outer_mixed / (first_len * second_len)


def draw_left_stat(key, part):
    return make_stat(key, 21)


def draw_right_stat(key, part):
    return make_stat(key, 22)


def draw_left_basis(key, part):
    return make_basis(key, 23)


def draw_right_basis(key, part):
    return make_basis(key, 24)


def draw_small_params(key, part):
    row_index = jnp.arange(SR)[:, None]
    gauss = jax.random.normal(jax.random.fold_in(key, 31), (SR, D), jnp.float32)
    spread = jax.random.uniform(jax.random.fold_in(key, 32), (SR, D), jnp.float32, -1.0, 1.0)
    gain_rows = (row_index < 4 * LAYERS + 2) & (row_index % 2 == 0)
    bias_rows = (row_index < 4 * LAYERS + 2) & (row_index % 2 == 1)
    return jnp.where(gain_rows, 1.0 + 0.3 * spread, jnp.where(bias_rows, 0.2 * gauss, gauss))


def touch_ends(result, key, smallest, high):
    index_at = [jax.random.randint(jax.random.fold_in(key, axis), (), 0, length) for axis, length in enumerate(result.shape)]
    widest = result.shape.index(max(result.shape))
    next_to = index_at[:widest] + [(index_at[widest] + 1) % result.shape[widest]] + index_at[widest + 1:]
    return result.at[tuple(index_at)].set(smallest).at[tuple(next_to)].set(high)


def block_levels(stream_key, extent, shards, least, largest):
    def one(position, blocks):
        draws = jax.random.uniform(jax.random.fold_in(jax.random.fold_in(stream_key, 6), position), (blocks,), jnp.float32, least / len(shards), largest / len(shards))
        return jnp.repeat(jnp.exp(draws), extent[position] // blocks).reshape((-1,) + (1,) * (len(extent) - position - 1))

    gain = one(*shards[0])
    for cut in shards[1:]:
        gain = gain * one(*cut)
    return gain


def gaussian(stream_key, dims, scale, limit, cuts=(), kind=jnp.bfloat16):
    drawn = jax.random.normal(stream_key, dims, jnp.float32) * scale
    if len(cuts) > 0:
        drawn = block_levels(stream_key, dims, cuts, -0.22, 0.18) * drawn
    return jnp.clip(drawn, min=-limit, max=limit).astype(kind)


def setup_inputs(seed: int = 0) -> dict:
    key_list = jax.random.split(jax.random.key(seed), 27)
    return {
        "latents": touch_ends(jax.random.randint(key_list[0], (SEQS, F, GROUPS), 0, CLASSES), jax.random.fold_in(key_list[0], 1), 0, CLASSES - 1).astype(jnp.int32),
        "actions": draw_actions(jax.random.fold_in(key_list[26], 71), 0),
        "game_ids": draw_game_ids(jax.random.fold_in(key_list[26], 71), 0),
        "action_masks": draw_action_masks(jax.random.fold_in(key_list[26], 71), 0),
        "valid_steps": draw_valid_steps(jax.random.fold_in(key_list[26], 71), 0),
        "target_bins": touch_ends(jax.random.randint(key_list[5], (SEQS, F, 2), 0, BINS - 1), jax.random.fold_in(key_list[5], 1), 0, (BINS - 1) - 1).astype(jnp.int32),
        "target_fracs": jnp.clip(1.0 * jax.random.uniform(key_list[6], (SEQS, F, 2), jnp.float32) ** block_levels(key_list[6], (SEQS, F, 2), ((0, 32),), -0.2, 0.2), 0.0, 1.0),
        "continues": touch_ends((jax.random.randint(key_list[7], (SEQS, F), 0, 16) < 15).astype(jnp.int32), jax.random.fold_in(key_list[7], 1), 0, 1),
        "owner_order": jax.random.permutation(key_list[8], NB).astype(jnp.int32),
        "blocks": gaussian(key_list[9], (NB, BS, BS), D ** -0.5, 0.25, ((0, 8),), jnp.float32),
        "block_first": gaussian(key_list[10], (NB, BS, BS), (0.0056 / PARAMS ** 0.5), 1.52587890625e-05, ((0, 8),), jnp.float32),
        "block_second": jnp.clip(jnp.exp(math.log(2.2554867695756542e-11) - 1.3843161 * jax.random.uniform(key_list[11], (NB, BS, BS), jnp.float32) ** block_levels(key_list[11], (NB, BS, BS), ((0, 8),), -0.2, 0.2)), 5.649882905273129e-12, 2.2554867695756542e-11),
        "left_stat": draw_left_stat(jax.random.fold_in(key_list[26], 71), 0),
        "right_stat": draw_right_stat(jax.random.fold_in(key_list[26], 71), 0),
        "left_basis": draw_left_basis(jax.random.fold_in(key_list[26], 71), 0),
        "right_basis": draw_right_basis(jax.random.fold_in(key_list[26], 71), 0),
        "latent_maps": gaussian(key_list[16], (2 * LAT, D), 0.1, 0.625, ((0, 8),), jnp.float32),
        "latent_first": gaussian(key_list[17], (2 * LAT, D), (0.0056 / PARAMS ** 0.5), 1.52587890625e-05, ((0, 8),), jnp.float32),
        "latent_second": jnp.clip(jnp.exp(math.log(2.2554867695756542e-11) - 1.3843161 * jax.random.uniform(key_list[18], (2 * LAT, D), jnp.float32) ** block_levels(key_list[18], (2 * LAT, D), ((0, 8),), -0.2, 0.2)), 5.649882905273129e-12, 2.2554867695756542e-11),
        "head_weights": gaussian(key_list[19], (D + 1, OUTS), 0.1, 0.625, (), jnp.float32),
        "head_first": gaussian(key_list[20], (D + 1, OUTS), (0.0056 / PARAMS ** 0.5), 1.52587890625e-05, (), jnp.float32),
        "head_second": jnp.clip(jnp.exp(jax.random.uniform(key_list[21], (D + 1, OUTS), jnp.float32, math.log(5.649882905273129e-12), math.log(2.2554867695756542e-11))), 5.649882905273129e-12, 2.2554867695756542e-11),
        "small_params": draw_small_params(jax.random.fold_in(key_list[26], 71), 0),
        "small_first": gaussian(key_list[23], (SR, D), (0.0056 / PARAMS ** 0.5), 1.52587890625e-05, (), jnp.float32),
        "small_second": jnp.clip(jnp.exp(jax.random.uniform(key_list[24], (SR, D), jnp.float32, math.log(5.649882905273129e-12), math.log(2.2554867695756542e-11))), 5.649882905273129e-12, 2.2554867695756542e-11),
        "ema_critic": gaussian(key_list[25], (D + 1, BINS), 0.025, 0.15625, (), jnp.float32),
    }


HIGHEST = lax.Precision.HIGHEST
beta_one = 0.9
beta_two = 0.99
epsilon = 1e-08
learn_rate = 0.03
small_rate = 0.15
weight_decay = 0.01
clip_norm = 0.05
ema_rate = 0.98
norm_eps = 1e-05

@jax.custom_vjp
def low(v):
    return lax.optimization_barrier(v.astype(jnp.bfloat16)).astype(jnp.float32)

@jax.custom_vjp
def low_back(v):
    return v

def low_keep(v):
    return (low(v), None)

def low_pass(kept, grad):
    return (grad,)

def back_keep(v):
    return (v, None)

def back_low(kept, grad):
    return (low(grad),)
low.defvjp(low_keep, low_pass)
low_back.defvjp(back_keep, back_low)

def from_blocks(pieces, block_rows, block_cols):
    side = pieces.shape[-1]
    return pieces.reshape(block_rows, block_cols, side, side).transpose(0, 2, 1, 3).reshape(block_rows * side, block_cols * side)

def layer_mats(block_ids, layer_index):
    per_layer = block_ids.shape[0] // LAYERS
    segment = block_ids[layer_index * per_layer:(layer_index + 1) * per_layer]
    tile_count = D // BS
    wide_count = FF // BS
    first_end = 3 * tile_count * tile_count
    second_end = first_end + tile_count * tile_count
    third_end = second_end + tile_count * wide_count
    joint_map = from_blocks(segment[:first_end], tile_count, 3 * tile_count)
    output_map = from_blocks(segment[first_end:second_end], tile_count, tile_count)
    expand = from_blocks(segment[second_end:third_end], tile_count, wide_count)
    contract = from_blocks(segment[third_end:], wide_count, tile_count)
    return (joint_map, output_map, expand, contract)

def layer_norm(inputs, gain_row, bias_row):
    center = inputs - lax.optimization_barrier(jnp.mean(inputs, -1, keepdims=True))
    spread = lax.optimization_barrier(jnp.mean(center * center, -1, keepdims=True))
    return center * lax.rsqrt(spread + norm_eps) * gain_row + bias_row

def positions(frames, width):
    frame_index = jnp.arange(frames).astype(jnp.float32)[:, None]
    feature = jnp.arange(width)
    freq = jnp.exp(-(feature // 2 * 2).astype(jnp.float32) * (math.log(10000.0) / width))
    angle = frame_index * freq[None, :]
    return jnp.where(feature % 2 == 0, jnp.sin(angle), jnp.cos(angle))

def attend(normed, joint_map, output_map):
    seqs_here = normed.shape[0]
    qkv_all = low(low_back(jnp.einsum('nfd,de->nfe', normed, joint_map, precision=HIGHEST)))
    qkv_all = qkv_all.reshape(seqs_here, F, 3, NH, DH)
    scores = low_back(jnp.einsum('nqhd,nkhd->nhqk', qkv_all[:, :, 0], qkv_all[:, :, 1], precision=HIGHEST) * DH ** (-0.5))
    causal = jnp.arange(F)[:, None] >= jnp.arange(F)[None, :]
    attn_probs = jax.nn.softmax(jnp.where(causal, scores, -1e+30), axis=-1)
    mixed_out = low(low_back(jnp.einsum('nhqk,nkhd->nqhd', low(attn_probs), qkv_all[:, :, 2], precision=HIGHEST)))
    return low_back(jnp.einsum('nfe,ed->nfd', mixed_out.reshape(seqs_here, F, D), output_map, precision=HIGHEST))

def feed_forward(normed, expand, contract):
    pre_act = low_back(jnp.einsum('nfd,de->nfe', normed, expand, precision=HIGHEST))
    return low_back(jnp.einsum('nfe,ed->nfd', low(jax.nn.gelu(pre_act, approximate=True)), contract, precision=HIGHEST))

def two_hot(logits, lower_bin, upper_frac):
    bin_index = jnp.arange(logits.shape[-1])
    weights = jnp.where(bin_index == lower_bin[..., None], 1.0 - upper_frac[..., None], 0.0)
    weights = weights + jnp.where(bin_index == lower_bin[..., None] + 1, upper_frac[..., None], 0.0)
    return -lax.optimization_barrier(jnp.sum(jax.nn.log_softmax(logits, -1) * weights, -1))

def group_loss(params, batches):
    block_ids, maps_low, head_weights, small_params = params
    latents, actions, legal_rows, valid_steps, target_bins, target_fracs, continues = batches
    seqs_here = latents.shape[0]
    latent_hot = (jnp.repeat(latents, CLASSES, axis=-1) == jnp.tile(jnp.arange(CLASSES), GROUPS)).astype(jnp.float32)
    action_hot = (actions[..., None] == jnp.arange(NA)).astype(jnp.float32)
    hidden = low_back(jnp.einsum('nfl,ld->nfd', latent_hot, maps_low[:LAT], precision=HIGHEST))
    hidden = hidden + jnp.einsum('nfa,ad->nfd', action_hot, small_params[4 * LAYERS + 2:], precision=HIGHEST) + positions(F, D)[None]
    for layer_index in range(LAYERS):
        joint_map, output_map, expand, contract = layer_mats(block_ids, layer_index)
        gains = small_params[4 * layer_index:4 * layer_index + 4]
        hidden = hidden + attend(low(layer_norm(hidden, gains[0], gains[1])), joint_map, output_map)
        hidden = hidden + feed_forward(low(layer_norm(hidden, gains[2], gains[3])), expand, contract)
    final_low = low(layer_norm(hidden, small_params[4 * LAYERS], small_params[4 * LAYERS + 1]))
    dyn_logits = low_back(jnp.einsum('nfd,ld->nfl', final_low, maps_low[LAT:], precision=HIGHEST))
    dyn_logits = dyn_logits.reshape(seqs_here, F, GROUPS, CLASSES)
    later = valid_steps[:, 1:].astype(jnp.float32)
    now = valid_steps.astype(jnp.float32)
    dyn_target = (latents[:, 1:, :, None] == jnp.arange(CLASSES)).astype(jnp.float32)
    dyn_loss = -jnp.sum(lax.optimization_barrier(jnp.sum(jax.nn.log_softmax(dyn_logits, -1)[:, :-1] * dyn_target, (-1, -2))) * later)
    head_out = low_back(jnp.einsum('nfd,dc->nfc', final_low, low(head_weights[:D]), precision=HIGHEST) + head_weights[D])
    reward_loss = two_hot(head_out[..., :BINS], target_bins[..., 0], target_fracs[..., 0])
    critic_loss = two_hot(head_out[..., BINS:2 * BINS], target_bins[..., 1], target_fracs[..., 1])
    cont_logit = head_out[..., 2 * BINS]
    cont_loss = jax.nn.softplus(cont_logit) - continues.astype(jnp.float32) * cont_logit
    masked = jnp.where(legal_rows[:, None, :] > 0, head_out[..., 2 * BINS + 1:], -1e+30)
    actor_loss = -jnp.sum(lax.optimization_barrier(jnp.sum(jax.nn.log_softmax(masked, -1)[:, :-1] * action_hot[:, 1:], -1)) * later)
    return dyn_loss + actor_loss + jnp.sum((reward_loss + critic_loss + cont_loss) * now)

def renew(stat, basis):
    scale = lax.optimization_barrier(jnp.max(lax.optimization_barrier(jnp.sum(jnp.abs(stat), -1)), -1))[:, None, None]
    iterate = jnp.einsum('bij,bjk->bik', stat, basis, precision=HIGHEST) / scale
    gram = jnp.einsum('bji,bjk->bik', iterate, iterate, precision=HIGHEST)
    lower_factor = jnp.linalg.cholesky(gram)
    solved = jax.scipy.linalg.solve_triangular(lower_factor, jnp.swapaxes(iterate, 1, 2), lower=True)
    return jnp.swapaxes(solved, 1, 2)

def soap_update(weight, first_moment, second_moment, left, right, left_rot, right_rot, grad):
    left = beta_two * left + (1.0 - beta_two) * jnp.einsum('bij,bkj->bik', grad, grad, precision=HIGHEST)
    right = beta_two * right + (1.0 - beta_two) * jnp.einsum('bji,bjk->bik', grad, grad, precision=HIGHEST)
    rotated = jnp.einsum('bji,bjk->bik', left_rot, grad, precision=HIGHEST)
    rotated = jnp.einsum('bij,bjk->bik', rotated, right_rot, precision=HIGHEST)
    first_moment = beta_one * first_moment + (1.0 - beta_one) * rotated
    second_moment = beta_two * second_moment + (1.0 - beta_two) * rotated * rotated
    direction = first_moment / (1.0 - beta_one ** STEP) / (jnp.sqrt(second_moment / (1.0 - beta_two ** STEP)) + epsilon)
    direction = jnp.einsum('bij,bjk->bik', left_rot, direction, precision=HIGHEST)
    direction = jnp.einsum('bij,bkj->bik', direction, right_rot, precision=HIGHEST)
    weight = weight - learn_rate * (direction + weight_decay * weight)
    return (weight, first_moment, second_moment, left, right, renew(left, left_rot), renew(right, right_rot))

def adam_update(weight, first_moment, second_moment, grad, decay_rate, rate):
    first_moment = beta_one * first_moment + (1.0 - beta_one) * grad
    second_moment = beta_two * second_moment + (1.0 - beta_two) * grad * grad
    direction = first_moment / (1.0 - beta_one ** STEP) / (jnp.sqrt(second_moment / (1.0 - beta_two ** STEP)) + epsilon)
    return (weight - rate * (direction + decay_rate * weight), first_moment, second_moment)

def reference(latents, actions, game_ids, action_masks, valid_steps, target_bins, target_fracs, continues, owner_order, blocks, block_first, block_second, left_stat, right_stat, left_basis, right_basis, latent_maps, latent_first, latent_second, head_weights, head_first, head_second, small_params, small_first, small_second, ema_critic):
    inverse = jnp.argsort(owner_order).astype(jnp.int32)
    counted = jnp.sum(valid_steps.astype(jnp.float32))
    legal_rows = action_masks[game_ids]
    group_size = math.gcd(latents.shape[0], 64)

    def regroup(array):
        return array.reshape((array.shape[0] // group_size, group_size) + array.shape[1:])
    batches = tuple((regroup(array) for array in (latents, actions, legal_rows, valid_steps, target_bins, target_fracs, continues)))

    def total_loss(params):
        low_params = (low(params[0])[inverse], low(params[1]), params[2], params[3])

        def scan_step(carry, batch_group):
            return (carry + jax.checkpoint(group_loss)(low_params, batch_group), None)
        summed, _ = lax.scan(scan_step, jnp.zeros((), jnp.float32), batches)
        return summed / counted
    loss_value, backward = jax.vjp(total_loss, (blocks, latent_maps, head_weights, small_params))
    gradients, = backward(jnp.ones((), jnp.float32))
    grad_blocks, grad_maps, grad_heads, grad_small = gradients
    squares = jnp.sum(grad_blocks * grad_blocks) + jnp.sum(grad_maps * grad_maps) + jnp.sum(grad_heads * grad_heads) + jnp.sum(grad_small * grad_small)
    grad_norm = jnp.sqrt(squares)
    factor = jnp.minimum(1.0, clip_norm / grad_norm)
    soap_out = soap_update(blocks, block_first, block_second, left_stat, right_stat, left_basis, right_basis, grad_blocks * factor)
    maps_out = adam_update(latent_maps, latent_first, latent_second, grad_maps * factor, weight_decay, learn_rate)
    heads_out = adam_update(head_weights, head_first, head_second, grad_heads * factor, weight_decay, learn_rate)
    small_out = adam_update(small_params, small_first, small_second, grad_small * factor, 0.0, small_rate)
    ema_new = ema_rate * ema_critic + (1.0 - ema_rate) * heads_out[0][:, BINS:2 * BINS]
    return (loss_value, grad_norm, soap_out[0], soap_out[1], soap_out[2], soap_out[3], soap_out[4], soap_out[5], soap_out[6], maps_out[0], maps_out[1], maps_out[2], heads_out[0], heads_out[1], heads_out[2], small_out[0], small_out[1], small_out[2], ema_new)
```

```python
import functools
import math

import jax
import jax.numpy as jnp
from jax import lax
from jax.experimental import pallas as pl
from jax.experimental.pallas import tpu as pltpu
from jax.sharding import PartitionSpec as P

D = 512
NH = 8
DH = 64
FF = 2048
GROUPS = 32
CLASSES = 32
LAT = 1024
BINS = 255
NA = 18
LAYERS = 1
F = 64
NGAME = 26
BS = 128
STEP = 10
PAN = 16
PACK = 8


HIGHEST = lax.Precision.HIGHEST
beta_one = 0.9
beta_two = 0.99
epsilon = 1e-08
learn_rate = 0.03
small_rate = 0.15
weight_decay = 0.01
clip_norm = 0.05
ema_rate = 0.98
norm_eps = 1e-05


def dot_rows(left_op, right_op):
    return lax.dot_general(
        left_op, right_op, (((1,), (1,)), ((), ())), preferred_element_type=jnp.float32
    )


def dot_cols(left_op, right_op):
    return lax.dot_general(
        left_op, right_op, (((0,), (0,)), ((), ())), preferred_element_type=jnp.float32
    )


def from_blocks(pieces, block_rows, block_cols):
    side = pieces.shape[-1]
    return (
        pieces.reshape(block_rows, block_cols, side, side)
        .transpose(0, 2, 1, 3)
        .reshape(block_rows * side, block_cols * side)
    )


def to_blocks(matrix):
    block_rows = matrix.shape[0] // BS
    block_cols = matrix.shape[1] // BS
    return (
        matrix.reshape(block_rows, BS, block_cols, BS)
        .transpose(0, 2, 1, 3)
        .reshape(block_rows * block_cols, BS, BS)
    )


def layer_mats(block_ids):
    tile_count = D // BS
    wide_count = FF // BS
    first_end = 3 * tile_count * tile_count
    second_end = first_end + tile_count * tile_count
    third_end = second_end + tile_count * wide_count
    joint_map = from_blocks(block_ids[:first_end], tile_count, 3 * tile_count)
    output_map = from_blocks(block_ids[first_end:second_end], tile_count, tile_count)
    expand = from_blocks(block_ids[second_end:third_end], tile_count, wide_count)
    contract = from_blocks(block_ids[third_end:], wide_count, tile_count)
    return (joint_map, output_map, expand, contract)


def positions(frames, width):
    frame_index = jnp.arange(frames).astype(jnp.float32)[:, None]
    feature = jnp.arange(width)
    freq = jnp.exp(-(feature // 2 * 2).astype(jnp.float32) * (math.log(10000.0) / width))
    angle = frame_index * freq[None, :]
    return jnp.where(feature % 2 == 0, jnp.sin(angle), jnp.cos(angle))


def norm_forward(inputs, gain_row, bias_row):
    center = inputs - jnp.mean(inputs, -1, keepdims=True)
    rstd_value = lax.rsqrt(jnp.mean(center * center, -1, keepdims=True) + norm_eps)
    scaled = center * rstd_value
    return (scaled * gain_row + bias_row, scaled, rstd_value)


def norm_backward(grad_out, scaled, rstd_value, gain_row):
    grad_scaled = grad_out * gain_row
    grad_in = rstd_value * (
        grad_scaled
        - jnp.mean(grad_scaled, -1, keepdims=True)
        - scaled * jnp.mean(grad_scaled * scaled, -1, keepdims=True)
    )
    return (grad_in, jnp.sum(grad_out * scaled, 0), jnp.sum(grad_out, 0))


def split_heads(qkv_low, seqs_here):
    shaped = qkv_low.reshape(seqs_here, F, 3, NH, DH)
    return (shaped[:, :, 0], shaped[:, :, 1], shaped[:, :, 2])


def attention_scores(queries, keys_all):
    scores = jnp.einsum(
        "sqhd,skhd->shqk", queries, keys_all, preferred_element_type=jnp.float32
    ) * DH ** (-0.5)
    causal = jnp.arange(F)[:, None] >= jnp.arange(F)[None, :]
    return jnp.where(causal, scores, -1e30)


def layer_forward(hidden, matrices, gains, seqs_here):
    joint_map, output_map, expand, contract = matrices
    normed, scaled_one, rstd_one = norm_forward(hidden, gains[0], gains[1])
    normed_low = normed.astype(jnp.bfloat16)
    qkv_low = jnp.dot(normed_low, joint_map, preferred_element_type=jnp.float32).astype(
        jnp.bfloat16
    )
    queries, keys_all, values_all = split_heads(qkv_low, seqs_here)
    scores = attention_scores(queries, keys_all)
    lse_value = jax.nn.logsumexp(scores, -1, keepdims=True)
    attn_probs = jnp.exp(scores - lse_value)
    mixed_out = jnp.einsum(
        "shqk,skhd->sqhd",
        attn_probs.astype(jnp.bfloat16),
        values_all,
        preferred_element_type=jnp.float32,
    )
    mixed_low = mixed_out.astype(jnp.bfloat16).reshape(-1, D)
    middle = hidden + jnp.dot(mixed_low, output_map, preferred_element_type=jnp.float32)
    normed_two, scaled_two, rstd_two = norm_forward(middle, gains[2], gains[3])
    normed_two_low = normed_two.astype(jnp.bfloat16)
    pre_act = jnp.dot(normed_two_low, expand, preferred_element_type=jnp.float32)
    act_low = jax.nn.gelu(pre_act, approximate=True).astype(jnp.bfloat16)
    output = middle + jnp.dot(act_low, contract, preferred_element_type=jnp.float32)
    kept_state = (
        scaled_one,
        rstd_one,
        normed_low,
        qkv_low,
        lse_value,
        mixed_low,
        scaled_two,
        rstd_two,
        normed_two_low,
        pre_act,
        act_low,
    )
    return (output, kept_state)


def layer_backward(grad_out, matrices, gains, kept_state, seqs_here):
    joint_map, output_map, expand, contract = matrices
    (
        scaled_one,
        rstd_one,
        normed_low,
        qkv_low,
        lse_value,
        mixed_low,
        scaled_two,
        rstd_two,
        normed_two_low,
        pre_act,
        act_low,
    ) = kept_state
    grad_low = grad_out.astype(jnp.bfloat16)
    grad_contract = dot_cols(act_low, grad_low)
    grad_act = dot_rows(grad_low, contract)
    _, gelu_pull = jax.vjp(lambda value: jax.nn.gelu(value, approximate=True), pre_act)
    grad_pre = gelu_pull(grad_act)[0].astype(jnp.bfloat16)
    grad_expand = dot_cols(normed_two_low, grad_pre)
    grad_normed_two = dot_rows(grad_pre, expand)
    grad_from_two, gain_two, bias_two = norm_backward(
        grad_normed_two, scaled_two, rstd_two, gains[2]
    )
    grad_middle = grad_out + grad_from_two
    grad_mid_low = grad_middle.astype(jnp.bfloat16)
    grad_output_map = dot_cols(mixed_low, grad_mid_low)
    grad_mixed = (
        dot_rows(grad_mid_low, output_map).astype(jnp.bfloat16).reshape(seqs_here, F, NH, DH)
    )
    queries, keys_all, values_all = split_heads(qkv_low, seqs_here)
    attn_probs = jnp.exp(attention_scores(queries, keys_all) - lse_value)
    grad_values = jnp.einsum(
        "shqk,sqhd->skhd",
        attn_probs.astype(jnp.bfloat16),
        grad_mixed,
        preferred_element_type=jnp.float32,
    )
    grad_probs = jnp.einsum(
        "sqhd,skhd->shqk", grad_mixed, values_all, preferred_element_type=jnp.float32
    )
    grad_scores = (
        attn_probs * (grad_probs - jnp.sum(grad_probs * attn_probs, -1, keepdims=True))
    ).astype(jnp.bfloat16)
    grad_queries = jnp.einsum(
        "shqk,skhd->sqhd", grad_scores, keys_all, preferred_element_type=jnp.float32
    ) * DH ** (-0.5)
    grad_keys = jnp.einsum(
        "shqk,sqhd->skhd", grad_scores, queries, preferred_element_type=jnp.float32
    ) * DH ** (-0.5)
    grad_qkv = (
        jnp.stack([grad_queries, grad_keys, grad_values], 2).reshape(-1, 3 * D).astype(jnp.bfloat16)
    )
    grad_joint = dot_cols(normed_low, grad_qkv)
    grad_normed = dot_rows(grad_qkv, joint_map)
    grad_from_one, gain_one, bias_one = norm_backward(grad_normed, scaled_one, rstd_one, gains[0])
    gain_grads = jnp.stack([gain_one, bias_one, gain_two, bias_two], 0)
    return (
        grad_middle + grad_from_one,
        (grad_joint, grad_output_map, grad_expand, grad_contract),
        gain_grads,
    )


def two_hot_terms(logits, lower_bin, upper_frac):
    bin_index = jnp.arange(logits.shape[-1])
    weights = jnp.where(bin_index == lower_bin[:, None], 1.0 - upper_frac[:, None], 0.0)
    weights = weights + jnp.where(bin_index == lower_bin[:, None] + 1, upper_frac[:, None], 0.0)
    log_probs = jax.nn.log_softmax(logits, -1)
    return (-jnp.sum(log_probs * weights, -1), jnp.exp(log_probs) - weights)


def hdot(a, b, ca, cb):
    return lax.dot_general(a, b, (((ca,), (cb,)), ((), ())), precision=HIGHEST, preferred_element_type=jnp.float32)

def qr_kernel(count, stat_ref, basis_ref, out_ref, work):
    tiles = -(-count // PACK)
    rows = PACK * PAN
    panels = BS // PAN

    def start(b, _):
        stat = stat_ref[b]
        scale = jnp.max(jnp.sum(jnp.abs(stat), -1, keepdims=True), 0, keepdims=True)
        xt = hdot(basis_ref[b], stat, 0, 0) / scale
        gram = hdot(xt, xt, 1, 1)
        for p in range(panels):
            work[p, pl.ds(b * PAN, PAN), :BS] = gram[p * PAN : (p + 1) * PAN]
            work[p, pl.ds(b * PAN, PAN), BS:] = xt[p * PAN : (p + 1) * PAN]
        return _

    lax.fori_loop(0, count, start, 0, unroll=2)
    row_id = lax.broadcasted_iota(jnp.int32, (PAN, BS), 0)
    lane_id = lax.broadcasted_iota(jnp.int32, (PAN, BS), 1)
    group = lane_id // PAN
    for p in range(panels):
        packed = []
        for t in range(tiles):
            tile = jnp.zeros((PAN, BS), jnp.float32)
            for c in range(PACK):
                b = t * PACK + c
                if b < count:
                    diag = work[p, b * PAN : (b + 1) * PAN, :BS]
                    shift = (c - p) * PAN % BS
                    if shift:
                        diag = pltpu.roll(diag, shift, 1)
                    tile = jnp.where(group == c, diag, tile)
                else:
                    tile = jnp.where((group == c) & (lane_id % PAN == row_id), 1.0, tile)
            packed.append(tile)
        inverse = [jnp.where(lane_id % PAN == row_id, 1.0, 0.0) for _ in range(tiles)]
        scales = [jnp.ones((PAN, BS), jnp.float32) for _ in range(tiles)]
        for k in range(PAN):
            index = group * PAN + k
            for t in range(tiles):
                tile = packed[t]
                column = jnp.take_along_axis(tile, index, axis=1, mode="promise_in_bounds")
                pivot = column[k : k + 1]
                scales[t] = jnp.where(row_id == k, lax.rsqrt(pivot), scales[t])
                if k < PAN - 1:
                    factor = jnp.where(row_id > k, column * (1.0 / pivot), 0.0)
                    packed[t] = tile - factor * tile[k : k + 1]
                    inverse[t] = inverse[t] - factor * inverse[t][k : k + 1]
        for t in range(tiles):
            low = inverse[t] * scales[t]
            spread = jnp.concatenate([jnp.where(group == c, low, 0.0) for c in range(PACK)], 0)
            here = min(rows, (count - t * PACK) * PAN)
            spread = spread[:here]
            if here < rows:
                spread = spread[:, :here]
            span = slice(t * rows, t * rows + here)
            work[p, span, :] = hdot(spread, work[p, span, :], 1, 0)
        if p < panels - 1:

            def trail(b, _, p=p):
                upper = work[p, pl.ds(b * PAN, PAN), :]
                lower = upper[:, :BS].T[(p + 1) * PAN :]
                change = hdot(lower, upper, 1, 0)
                for q in range(p + 1, panels):
                    span = slice((q - p - 1) * PAN, (q - p) * PAN)
                    work[q, pl.ds(b * PAN, PAN), :] -= change[span]
                return _

            lax.fori_loop(0, count, trail, 0, unroll=4 if count % 4 == 0 else 1)

    def finish(b, _):
        rows_q = jnp.concatenate([work[p, pl.ds(b * PAN, PAN), BS:] for p in range(panels)], 0)
        out_ref[b] = rows_q.T
        return _

    lax.fori_loop(0, count, finish, 0, unroll=2)


def renew_all(stats, bases):
    count = stats.shape[0]
    return pl.pallas_call(
        functools.partial(qr_kernel, count),
        out_shape=jax.ShapeDtypeStruct((count, BS, BS), jnp.float32),
        in_specs=[pl.BlockSpec(memory_space=pltpu.VMEM)] * 2,
        out_specs=pl.BlockSpec(memory_space=pltpu.VMEM),
        scratch_shapes=[pltpu.VMEM((BS // PAN, count * PAN, 2 * BS), jnp.float32)],
        name="renew",
    )(stats, bases)


def soap_update(weight, first_moment, second_moment, left, right, left_rot, right_rot, grad):
    left = beta_two * left + (1.0 - beta_two) * jnp.einsum(
        "bij,bkj->bik", grad, grad, precision=HIGHEST
    )
    right = beta_two * right + (1.0 - beta_two) * jnp.einsum(
        "bji,bjk->bik", grad, grad, precision=HIGHEST
    )
    rotated = jnp.einsum("bji,bjk->bik", left_rot, grad, precision=HIGHEST)
    rotated = jnp.einsum("bij,bjk->bik", rotated, right_rot, precision=HIGHEST)
    first_moment = beta_one * first_moment + (1.0 - beta_one) * rotated
    second_moment = beta_two * second_moment + (1.0 - beta_two) * rotated * rotated
    direction = (
        first_moment
        / (1.0 - beta_one**STEP)
        / (jnp.sqrt(second_moment / (1.0 - beta_two**STEP)) + epsilon)
    )
    direction = jnp.einsum("bij,bjk->bik", left_rot, direction, precision=HIGHEST)
    direction = jnp.einsum("bij,bkj->bik", direction, right_rot, precision=HIGHEST)
    weight = weight - learn_rate * (direction + weight_decay * weight)
    count = weight.shape[0]
    renewed = renew_all(
        jnp.concatenate([left, right], 0), jnp.concatenate([left_rot, right_rot], 0)
    )
    return (
        weight,
        first_moment,
        second_moment,
        left,
        right,
        renewed[:count],
        renewed[count:],
    )


def adam_update(weight, first_moment, second_moment, grad, decay_rate, rate):
    first_moment = beta_one * first_moment + (1.0 - beta_one) * grad
    second_moment = beta_two * second_moment + (1.0 - beta_two) * grad * grad
    direction = (
        first_moment
        / (1.0 - beta_one**STEP)
        / (jnp.sqrt(second_moment / (1.0 - beta_two**STEP)) + epsilon)
    )
    return (weight - rate * (direction + decay_rate * weight), first_moment, second_moment)


def shards(
    latents,
    actions,
    game_ids,
    action_masks,
    valid_steps,
    target_bins,
    target_fracs,
    continues,
    owner_order,
    blocks,
    block_first,
    block_second,
    left_stat,
    right_stat,
    left_basis,
    right_basis,
    latent_maps,
    latent_first,
    latent_second,
    head_weights,
    head_first,
    head_second,
    small_params,
    small_first,
    small_second,
    ema_critic,
):
    seqs_here = latents.shape[0]
    tokens = seqs_here * F
    counted = lax.psum(jnp.sum(valid_steps.astype(jnp.float32)), ("dp", "fsdp"))
    shard_low = (blocks.astype(jnp.bfloat16), latent_maps.astype(jnp.bfloat16))
    slots_all, maps_all = (
        lax.all_gather(shard_low[0], "fsdp", axis=0, tiled=True),
        lax.all_gather(shard_low[1], "fsdp", axis=0, tiled=True),
    )
    inverse = jnp.argsort(owner_order)
    ids_all = slots_all[inverse]
    latent_hot = (
        jnp.repeat(latents.reshape(tokens, GROUPS), CLASSES, axis=1)
        == jnp.tile(jnp.arange(CLASSES), GROUPS)[None, :]
    ).astype(jnp.bfloat16)
    action_hot = (actions.reshape(tokens, 1) == jnp.arange(NA)[None, :]).astype(jnp.float32)
    hidden = jnp.dot(latent_hot, maps_all[:LAT], preferred_element_type=jnp.float32)
    hidden = hidden + jnp.dot(action_hot, small_params[4 * LAYERS + 2 :], precision=HIGHEST)
    hidden = (hidden.reshape(seqs_here, F, D) + positions(F, D)[None]).reshape(tokens, D)
    layer_index = 0
    matrices = layer_mats(ids_all)
    hidden, kept_state = layer_forward(
        hidden, matrices, small_params[4 * layer_index : 4 * layer_index + 4], seqs_here
    )
    states_kept = [kept_state]
    final_norm, final_scaled, final_rstd = norm_forward(
        hidden, small_params[4 * LAYERS], small_params[4 * LAYERS + 1]
    )
    final_low = final_norm.astype(jnp.bfloat16)
    dyn_logits = dot_rows(final_low, maps_all[LAT:]).reshape(tokens, GROUPS, CLASSES)
    head_low = head_weights[:D].astype(jnp.bfloat16)
    head_out = jnp.dot(final_low, head_low, preferred_element_type=jnp.float32) + head_weights[D]
    frame_last = (jnp.arange(F) < F - 1).astype(jnp.float32)[None, :]
    later = (jnp.roll(valid_steps, -1, axis=1).astype(jnp.float32) * frame_last).reshape(tokens)
    now = valid_steps.astype(jnp.float32).reshape(tokens)
    next_latent = jnp.roll(latents, -1, axis=1).reshape(tokens, GROUPS, 1)
    dyn_target = (next_latent == jnp.arange(CLASSES)).astype(jnp.float32)
    dyn_log = jax.nn.log_softmax(dyn_logits, -1)
    dyn_loss = -jnp.sum(jnp.sum(dyn_log * dyn_target, (1, 2)) * later)
    grad_dyn = (
        ((jnp.exp(dyn_log) - dyn_target) * (later / counted)[:, None, None])
        .reshape(tokens, LAT)
        .astype(jnp.bfloat16)
    )
    bins_flat = target_bins.reshape(tokens, 2)
    fracs_flat = target_fracs.reshape(tokens, 2)
    reward_loss, reward_grad = two_hot_terms(head_out[:, :BINS], bins_flat[:, 0], fracs_flat[:, 0])
    critic_loss, critic_grad = two_hot_terms(
        head_out[:, BINS : 2 * BINS], bins_flat[:, 1], fracs_flat[:, 1]
    )
    cont_logit = head_out[:, 2 * BINS]
    cont_target = continues.reshape(tokens).astype(jnp.float32)
    cont_loss = jax.nn.softplus(cont_logit) - cont_target * cont_logit
    cont_grad = jax.nn.sigmoid(cont_logit) - cont_target
    game_hot = (game_ids[:, None] == jnp.arange(NGAME)[None, :]).astype(jnp.float32)
    legal_rows = jnp.dot(game_hot, action_masks.astype(jnp.float32), precision=HIGHEST)
    legal_tok = (
        jnp.broadcast_to(legal_rows[:, None, :], (seqs_here, F, NA)).reshape(tokens, NA) > 0.5
    )
    masked = jnp.where(legal_tok, head_out[:, 2 * BINS + 1 :], -1e30)
    actor_log = jax.nn.log_softmax(masked, -1)
    next_action = (
        jnp.roll(actions, -1, axis=1).reshape(tokens, 1) == jnp.arange(NA)[None, :]
    ).astype(jnp.float32)
    actor_loss = -jnp.sum(jnp.sum(actor_log * next_action, -1) * later)
    loss_local = (
        dyn_loss + actor_loss + jnp.sum((reward_loss + critic_loss + cont_loss) * now)
    ) / counted
    grad_head = jnp.concatenate(
        [
            reward_grad * now[:, None],
            critic_grad * now[:, None],
            (cont_grad * now)[:, None],
            (jnp.exp(actor_log) - next_action) * later[:, None],
        ],
        1,
    )
    grad_head = (grad_head / counted).astype(jnp.bfloat16)
    back_slots, back_maps = (
        lax.all_gather(shard_low[0], "fsdp", axis=0, tiled=True),
        lax.all_gather(shard_low[1], "fsdp", axis=0, tiled=True),
    )
    back_ids = back_slots[inverse]
    grad_dyn_table = dot_cols(grad_dyn, final_low)
    grad_head_matrix = dot_cols(final_low, grad_head)
    grad_head_bias = jnp.sum(grad_head.astype(jnp.float32), 0)
    grad_final = jnp.dot(grad_dyn, back_maps[LAT:], preferred_element_type=jnp.float32) + dot_rows(
        grad_head, head_low
    )
    grad_hidden, final_gain, final_bias = norm_backward(
        grad_final, final_scaled, final_rstd, small_params[4 * LAYERS]
    )
    block_parts = [None] * LAYERS
    small_parts = [None] * LAYERS
    for layer_index in reversed(range(LAYERS)):
        matrices = layer_mats(back_ids)
        grad_hidden, matrix_grads, gain_grads = layer_backward(
            grad_hidden,
            matrices,
            small_params[4 * layer_index : 4 * layer_index + 4],
            states_kept[layer_index],
            seqs_here,
        )
        block_parts[layer_index] = jnp.concatenate([to_blocks(piece) for piece in matrix_grads], 0)
        small_parts[layer_index] = gain_grads
    grad_lat_table = dot_cols(latent_hot, grad_hidden.astype(jnp.bfloat16))
    grad_act_table = lax.dot_general(
        action_hot, grad_hidden, (((0,), (0,)), ((), ())), precision=HIGHEST
    )
    grad_ids = block_parts[0]
    grad_slots = grad_ids[owner_order]
    grad_maps = jnp.concatenate([grad_lat_table, grad_dyn_table], 0)
    small_local = jnp.concatenate(
        small_parts + [final_gain[None], final_bias[None], grad_act_table], 0
    )
    head_local = jnp.concatenate([grad_head_matrix, grad_head_bias[None]], 0)
    shard_grads = (
        lax.psum_scatter(grad_slots, "fsdp", scatter_dimension=0, tiled=True),
        lax.psum_scatter(grad_maps, "fsdp", scatter_dimension=0, tiled=True),
    )
    block_grad, maps_grad = lax.psum((shard_grads[0], shard_grads[1]), "dp")
    head_grad, small_grad, loss_value = lax.psum(
        (head_local, small_local, loss_local), ("dp", "fsdp")
    )
    held_square = lax.psum(
        jnp.sum(block_grad * block_grad) + jnp.sum(maps_grad * maps_grad), "fsdp"
    )
    grad_norm = jnp.sqrt(
        held_square + jnp.sum(head_grad * head_grad) + jnp.sum(small_grad * small_grad)
    )
    factor = jnp.minimum(1.0, clip_norm / grad_norm)
    soap_out = soap_update(
        blocks,
        block_first,
        block_second,
        left_stat,
        right_stat,
        left_basis,
        right_basis,
        block_grad * factor,
    )
    maps_out = adam_update(
        latent_maps, latent_first, latent_second, maps_grad * factor, weight_decay, learn_rate
    )
    heads_out = adam_update(
        head_weights, head_first, head_second, head_grad * factor, weight_decay, learn_rate
    )
    small_out = adam_update(
        small_params, small_first, small_second, small_grad * factor, 0.0, small_rate
    )
    ema_new = ema_rate * ema_critic + (1.0 - ema_rate) * heads_out[0][:, BINS : 2 * BINS]
    return (
        loss_value,
        grad_norm,
        soap_out[0],
        soap_out[1],
        soap_out[2],
        soap_out[3],
        soap_out[4],
        soap_out[5],
        soap_out[6],
        maps_out[0],
        maps_out[1],
        maps_out[2],
        heads_out[0],
        heads_out[1],
        heads_out[2],
        small_out[0],
        small_out[1],
        small_out[2],
        ema_new,
    )


def solution(mesh):
    placed = (
        P(("dp", "fsdp"), None, None),
        P(("dp", "fsdp"), None),
        P(("dp", "fsdp")),
        P(),
        P(("dp", "fsdp"), None),
        P(("dp", "fsdp"), None, None),
        P(("dp", "fsdp"), None, None),
        P(("dp", "fsdp"), None),
        P(),
        P("fsdp", None, None),
        P("fsdp", None, None),
        P("fsdp", None, None),
        P("fsdp", None, None),
        P("fsdp", None, None),
        P("fsdp", None, None),
        P("fsdp", None, None),
        P("fsdp", None),
        P("fsdp", None),
        P("fsdp", None),
        P(),
        P(),
        P(),
        P(),
        P(),
        P(),
        P(),
    )
    return jax.shard_map(
        shards,
        mesh=mesh,
        in_specs=placed,
        out_specs=(
            P(),
            P(),
            P("fsdp", None, None),
            P("fsdp", None, None),
            P("fsdp", None, None),
            P("fsdp", None, None),
            P("fsdp", None, None),
            P("fsdp", None, None),
            P("fsdp", None, None),
            P("fsdp", None),
            P("fsdp", None),
            P("fsdp", None),
            P(),
            P(),
            P(),
            P(),
            P(),
            P(),
            P(),
        ),
        check_vma=False,
    )
```

```python
import functools
import math

import jax
import jax.numpy as jnp
from jax import lax
from jax.experimental import pallas as pl
from jax.experimental.pallas import tpu as pltpu
from jax.sharding import PartitionSpec as P

D = 512
NH = 8
DH = 64
FF = 2048
GROUPS = 32
CLASSES = 32
LAT = 1024
BINS = 255
NA = 18
LAYERS = 1
F = 64
NGAME = 26
BS = 128
STEP = 10
PAN = 16
PACK = 8
HEAD_ROWS = 520
HEAD_COLS = 640
PACK_ROWS = 3072
MAPS_CUTS = ((0, 96), (96, 176), (176, 256))
REST_CUTS = ((0, 128), (128, 240), (240, 352))


HIGHEST = lax.Precision.HIGHEST
beta_one = 0.9
beta_two = 0.99
epsilon = 1e-08
learn_rate = 0.03
small_rate = 0.15
weight_decay = 0.01
clip_norm = 0.05
ema_rate = 0.98
norm_eps = 1e-05


def dot_rows(left_op, right_op):
    return lax.dot_general(
        left_op, right_op, (((1,), (1,)), ((), ())), preferred_element_type=jnp.float32
    )


def dot_cols(left_op, right_op):
    return lax.dot_general(
        left_op, right_op, (((0,), (0,)), ((), ())), preferred_element_type=jnp.float32
    )


def from_blocks(pieces, block_rows, block_cols):
    side = pieces.shape[-1]
    return (
        pieces.reshape(block_rows, block_cols, side, side)
        .transpose(0, 2, 1, 3)
        .reshape(block_rows * side, block_cols * side)
    )


def to_blocks(matrix):
    block_rows = matrix.shape[0] // BS
    block_cols = matrix.shape[1] // BS
    return (
        matrix.reshape(block_rows, BS, block_cols, BS)
        .transpose(0, 2, 1, 3)
        .reshape(block_rows * block_cols, BS, BS)
    )


def layer_mats(block_ids):
    tile_count = D // BS
    wide_count = FF // BS
    first_end = 3 * tile_count * tile_count
    second_end = first_end + tile_count * tile_count
    third_end = second_end + tile_count * wide_count
    joint_map = from_blocks(block_ids[:first_end], tile_count, 3 * tile_count)
    output_map = from_blocks(block_ids[first_end:second_end], tile_count, tile_count)
    expand = from_blocks(block_ids[second_end:third_end], tile_count, wide_count)
    contract = from_blocks(block_ids[third_end:], wide_count, tile_count)
    return (joint_map, output_map, expand, contract)


def positions(frames, width):
    frame_index = jnp.arange(frames).astype(jnp.float32)[:, None]
    feature = jnp.arange(width)
    freq = jnp.exp(-(feature // 2 * 2).astype(jnp.float32) * (math.log(10000.0) / width))
    angle = frame_index * freq[None, :]
    return jnp.where(feature % 2 == 0, jnp.sin(angle), jnp.cos(angle))


def norm_forward(inputs, gain_row, bias_row):
    center = inputs - jnp.mean(inputs, -1, keepdims=True)
    rstd_value = lax.rsqrt(jnp.mean(center * center, -1, keepdims=True) + norm_eps)
    scaled = center * rstd_value
    return (scaled * gain_row + bias_row, scaled, rstd_value)


def norm_backward(grad_out, scaled, rstd_value, gain_row):
    grad_scaled = grad_out * gain_row
    grad_in = rstd_value * (
        grad_scaled
        - jnp.mean(grad_scaled, -1, keepdims=True)
        - scaled * jnp.mean(grad_scaled * scaled, -1, keepdims=True)
    )
    return (grad_in, jnp.sum(grad_out * scaled, 0), jnp.sum(grad_out, 0))


def split_heads(qkv_low, seqs_here):
    shaped = qkv_low.reshape(seqs_here, F, 3, NH, DH)
    return (shaped[:, :, 0], shaped[:, :, 1], shaped[:, :, 2])


def attention_scores(queries, keys_all):
    scores = jnp.einsum(
        "sqhd,skhd->shqk", queries, keys_all, preferred_element_type=jnp.float32
    ) * DH ** (-0.5)
    causal = jnp.arange(F)[:, None] >= jnp.arange(F)[None, :]
    return jnp.where(causal, scores, -1e30)


def layer_forward(hidden, matrices, gains, seqs_here):
    joint_map, output_map, expand, contract = matrices
    normed, scaled_one, rstd_one = norm_forward(hidden, gains[0], gains[1])
    normed_low = normed.astype(jnp.bfloat16)
    qkv_low = jnp.dot(normed_low, joint_map, preferred_element_type=jnp.float32).astype(
        jnp.bfloat16
    )
    queries, keys_all, values_all = split_heads(qkv_low, seqs_here)
    scores = attention_scores(queries, keys_all)
    lse_value = jax.nn.logsumexp(scores, -1, keepdims=True)
    attn_probs = jnp.exp(scores - lse_value)
    mixed_out = jnp.einsum(
        "shqk,skhd->sqhd",
        attn_probs.astype(jnp.bfloat16),
        values_all,
        preferred_element_type=jnp.float32,
    )
    mixed_low = mixed_out.astype(jnp.bfloat16).reshape(-1, D)
    middle = hidden + jnp.dot(mixed_low, output_map, preferred_element_type=jnp.float32)
    normed_two, scaled_two, rstd_two = norm_forward(middle, gains[2], gains[3])
    normed_two_low = normed_two.astype(jnp.bfloat16)
    pre_act = jnp.dot(normed_two_low, expand, preferred_element_type=jnp.float32)
    act_low = jax.nn.gelu(pre_act, approximate=True).astype(jnp.bfloat16)
    output = middle + jnp.dot(act_low, contract, preferred_element_type=jnp.float32)
    kept_state = (
        scaled_one,
        rstd_one,
        normed_low,
        qkv_low,
        lse_value,
        mixed_low,
        scaled_two,
        rstd_two,
        normed_two_low,
        pre_act,
        act_low,
    )
    return (output, kept_state)


def layer_backward(grad_out, matrices, gains, kept_state, seqs_here):
    joint_map, output_map, expand, contract = matrices
    (
        scaled_one,
        rstd_one,
        normed_low,
        qkv_low,
        lse_value,
        mixed_low,
        scaled_two,
        rstd_two,
        normed_two_low,
        pre_act,
        act_low,
    ) = kept_state
    grad_low = grad_out.astype(jnp.bfloat16)
    grad_contract = dot_cols(act_low, grad_low)
    grad_act = dot_rows(grad_low, contract)
    _, gelu_pull = jax.vjp(lambda value: jax.nn.gelu(value, approximate=True), pre_act)
    grad_pre = gelu_pull(grad_act)[0].astype(jnp.bfloat16)
    grad_expand = dot_cols(normed_two_low, grad_pre)
    grad_normed_two = dot_rows(grad_pre, expand)
    grad_from_two, gain_two, bias_two = norm_backward(
        grad_normed_two, scaled_two, rstd_two, gains[2]
    )
    grad_middle = grad_out + grad_from_two
    grad_mid_low = grad_middle.astype(jnp.bfloat16)
    grad_output_map = dot_cols(mixed_low, grad_mid_low)
    grad_mixed = (
        dot_rows(grad_mid_low, output_map).astype(jnp.bfloat16).reshape(seqs_here, F, NH, DH)
    )
    queries, keys_all, values_all = split_heads(qkv_low, seqs_here)
    attn_probs = jnp.exp(attention_scores(queries, keys_all) - lse_value)
    grad_values = jnp.einsum(
        "shqk,sqhd->skhd",
        attn_probs.astype(jnp.bfloat16),
        grad_mixed,
        preferred_element_type=jnp.float32,
    )
    grad_probs = jnp.einsum(
        "sqhd,skhd->shqk", grad_mixed, values_all, preferred_element_type=jnp.float32
    )
    grad_scores = (
        attn_probs * (grad_probs - jnp.sum(grad_probs * attn_probs, -1, keepdims=True))
    ).astype(jnp.bfloat16)
    grad_queries = jnp.einsum(
        "shqk,skhd->sqhd", grad_scores, keys_all, preferred_element_type=jnp.float32
    ) * DH ** (-0.5)
    grad_keys = jnp.einsum(
        "shqk,sqhd->skhd", grad_scores, queries, preferred_element_type=jnp.float32
    ) * DH ** (-0.5)
    grad_qkv = (
        jnp.stack([grad_queries, grad_keys, grad_values], 2).reshape(-1, 3 * D).astype(jnp.bfloat16)
    )
    grad_joint = dot_cols(normed_low, grad_qkv)
    grad_normed = dot_rows(grad_qkv, joint_map)
    grad_from_one, gain_one, bias_one = norm_backward(grad_normed, scaled_one, rstd_one, gains[0])
    gain_grads = jnp.stack([gain_one, bias_one, gain_two, bias_two], 0)
    return (
        grad_middle + grad_from_one,
        (grad_joint, grad_output_map, grad_expand, grad_contract),
        gain_grads,
    )


def halves(size):
    return [1 << bit for bit in reversed(range(size.bit_length() - 1))]


def swap(value, axis, size, bit):
    return lax.ppermute(value, axis, [(i, i ^ bit) for i in range(size)])


def sum_small(value, dp, fsdp):
    for axis, size in (("dp", dp), ("fsdp", fsdp)):
        for bit in reversed(halves(size)):
            value = value + swap(value, axis, size, bit)
    return value


def part_orders(dp, fsdp):
    core, tall = [("dp", dp, bit) for bit in reversed(halves(dp))]
    deep, near, side = [("fsdp", fsdp, bit) for bit in halves(fsdp)]
    return (
        (core, tall, side, near, deep),
        (core, side, near, deep, tall),
        (core, near, tall, side, deep),
    )


def order_index(order, dp_here, fsdp_here):
    dp_index = jnp.zeros((), jnp.int32)
    fsdp_index = jnp.zeros((), jnp.int32)
    spot = jnp.arange(1 << len(order))
    for place, (axis, _, bit) in enumerate(order):
        flag = (spot >> (len(order) - 1 - place)) & 1
        if axis == "dp":
            dp_index = dp_index + flag * bit
        else:
            fsdp_index = fsdp_index + flag * bit
    return dp_index ^ dp_here, fsdp_index ^ fsdp_here


def scatter_sum(value, order, wide_stages):
    held = value
    for place, (axis, size, bit) in enumerate(order):
        half = held.shape[0] // 2
        sent = held[half:]
        if place < len(order) - wide_stages:
            sent = sent.astype(jnp.bfloat16)
        got = swap(sent, axis, size, bit)
        held = held[:half].astype(jnp.float32) + got.astype(jnp.float32)
    return held[0]


def gather_doubling(value, order):
    held = value[None]
    for axis, size, bit in reversed(order):
        held = jnp.concatenate([held, swap(held, axis, size, bit)], 0)
    return held


def inverse_place(order, dp, fsdp, dp_here, fsdp_here):
    dp_id = jnp.arange(dp)[None, :] ^ dp_here
    fsdp_id = jnp.arange(fsdp)[:, None] ^ fsdp_here
    spot = jnp.zeros((fsdp, dp), jnp.int32)
    for place, (axis, _, bit) in enumerate(order):
        source = dp_id if axis == "dp" else fsdp_id
        flag = (source & bit) // bit
        spot = spot + flag * (1 << (len(order) - 1 - place))
    return spot


def reduced_grads(grad_ids, grad_maps, heads, owner_order, sums, dp, fsdp):
    slots = owner_order.shape[0] // fsdp
    map_rows = grad_maps.shape[0] // fsdp
    if (dp, fsdp) != (4, 8):
        both = ("dp", "fsdp")
        block_grad = lax.psum(
            lax.psum_scatter(grad_ids[owner_order], "fsdp", scatter_dimension=0, tiled=True), "dp"
        )
        maps_grad = lax.psum(
            lax.psum_scatter(grad_maps, "fsdp", scatter_dimension=0, tiled=True), "dp"
        )
        heads = lax.psum(heads, both)
        sums = lax.psum(sums, both)
        held = lax.psum(jnp.sum(block_grad * block_grad) + jnp.sum(maps_grad * maps_grad), "fsdp")
        return block_grad, maps_grad, heads, held + jnp.sum(heads * heads), sums
    dp_here = lax.axis_index("dp")
    fsdp_here = lax.axis_index("fsdp")
    devices = dp * fsdp
    per_piece = slots // dp // 3
    piece_rows = map_rows // dp
    maps_split = (
        grad_maps.reshape(devices, piece_rows, D // BS, BS)
        .transpose(0, 2, 1, 3)
        .reshape(devices, piece_rows * D // BS, BS)
    )
    rest = jnp.concatenate([maps_split, heads.reshape(devices, -1, BS)], 1)
    parts = []
    for part, order in enumerate(part_orders(dp, fsdp)):
        dp_index, fsdp_index = order_index(order, dp_here, fsdp_here)
        first = fsdp_index * slots + dp_index * (slots // dp) + part * per_piece
        ids = owner_order[(first[:, None] + jnp.arange(per_piece)[None, :]).reshape(-1)]
        low_row, high_row = REST_CUTS[part]
        piece = jnp.concatenate(
            [
                grad_ids[ids].reshape(devices, per_piece * BS, BS),
                rest[fsdp_index * dp + dp_index, low_row:high_row],
            ],
            1,
        )
        parts.append(scatter_sum(piece, order, 2))
    cut = per_piece * BS
    own_blocks = jnp.concatenate([part[:cut] for part in parts], 0)
    own_rest = jnp.concatenate([part[cut:] for part in parts], 0)
    maps_count = piece_rows * D // BS
    own_square = jnp.sum(own_blocks * own_blocks) + jnp.sum(own_rest * own_rest)
    sums = sum_small(jnp.concatenate([sums, own_square[None]]), dp, fsdp)
    dp_order = [("dp", dp, bit) for bit in reversed(halves(dp))]
    spot = inverse_place(dp_order, dp, 1, dp_here, 0).reshape(-1)
    shard = gather_doubling(jnp.concatenate([own_blocks, own_rest[:maps_count]], 0), dp_order)
    shard = shard[spot]
    count = slots // dp * BS
    block_grad = shard[:, :count].reshape(slots, BS, BS)
    maps_grad = (
        shard[:, count:]
        .reshape(dp, D // BS, piece_rows, BS)
        .transpose(0, 2, 1, 3)
        .reshape(map_rows, D)
    )
    full_order = part_orders(dp, fsdp)[0]
    all_heads = gather_doubling(own_rest[maps_count:], full_order)
    spot = inverse_place(full_order, dp, fsdp, dp_here, fsdp_here).reshape(-1)
    return block_grad, maps_grad, all_heads[spot].reshape(-1, BS), sums[-1], sums[:-1]


def gathered_weights(blocks_low, maps_low, inverse, dp, fsdp):
    if (dp, fsdp) != (4, 8):
        return (
            lax.all_gather(blocks_low, "fsdp", axis=0, tiled=True)[inverse],
            lax.all_gather(maps_low, "fsdp", axis=0, tiled=True),
        )
    dp_here = lax.axis_index("dp")
    fsdp_here = lax.axis_index("fsdp")
    slots = blocks_low.shape[0]
    quarter = slots // dp
    per_piece = quarter // 3
    piece_rows = maps_low.shape[0] // dp
    own_blocks = lax.dynamic_slice_in_dim(blocks_low, dp_here * quarter, quarter, 0)
    own_maps = (
        lax.dynamic_slice_in_dim(maps_low, dp_here * piece_rows, piece_rows, 0)
        .reshape(piece_rows, D // BS, BS)
        .transpose(1, 0, 2)
        .reshape(-1, BS)
    )
    cut = per_piece * BS
    blocks_got = []
    maps_got = []
    places = []
    for part, order in enumerate(part_orders(dp, fsdp)):
        low_row, high_row = MAPS_CUTS[part]
        piece = jnp.concatenate(
            [
                own_blocks[part * per_piece : (part + 1) * per_piece].reshape(cut, BS),
                own_maps[low_row:high_row],
            ],
            0,
        )
        got = gather_doubling(piece, order)
        place = inverse_place(order, dp, fsdp, dp_here, fsdp_here)
        blocks_got.append(got[:, :cut].reshape(-1, BS, BS))
        maps_got.append(got[place.reshape(-1), cut:])
        places.append(place)
    maps_all = jnp.concatenate(maps_got, 1)
    maps_all = (
        maps_all.reshape(fsdp * dp, D // BS, piece_rows, BS)
        .transpose(0, 2, 1, 3)
        .reshape(-1, D)
    )
    local = inverse % slots
    part = local % quarter // per_piece
    spot = jnp.stack(places)[part, inverse // slots, local // quarter]
    index = (part * dp * fsdp + spot) * per_piece + local % per_piece
    return jnp.concatenate(blocks_got, 0)[index], maps_all


def pack_heads(head, small):
    head = jnp.pad(head, ((0, HEAD_ROWS - head.shape[0]), (0, HEAD_COLS - head.shape[1])))
    chunks = [head[:, c : c + BS] for c in range(0, HEAD_COLS, BS)]
    chunks += [small[:, c : c + BS] for c in range(0, D, BS)]
    packed = jnp.concatenate(chunks, 0)
    return jnp.pad(packed, ((0, PACK_ROWS - packed.shape[0]), (0, 0)))


def unpack_heads(packed, head_shape, small_rows):
    count = HEAD_COLS // BS
    head = jnp.concatenate(
        [packed[c * HEAD_ROWS : (c + 1) * HEAD_ROWS] for c in range(count)], 1
    )
    start = count * HEAD_ROWS
    small = jnp.concatenate(
        [packed[start + c * small_rows : start + (c + 1) * small_rows] for c in range(D // BS)], 1
    )
    return head[: head_shape[0], : head_shape[1]], small


def two_hot_terms(logits, lower_bin, upper_frac):
    bin_index = jnp.arange(logits.shape[-1])
    weights = jnp.where(bin_index == lower_bin[:, None], 1.0 - upper_frac[:, None], 0.0)
    weights = weights + jnp.where(bin_index == lower_bin[:, None] + 1, upper_frac[:, None], 0.0)
    log_probs = jax.nn.log_softmax(logits, -1)
    return (-jnp.sum(log_probs * weights, -1), jnp.exp(log_probs) - weights)


def thirds(value):
    first = value.astype(jnp.bfloat16)
    rest = value - first.astype(jnp.float32)
    second = rest.astype(jnp.bfloat16)
    third = (rest - second.astype(jnp.float32)).astype(jnp.bfloat16)
    return first, second, third


def stack_left(value, axis):
    a, b, c = thirds(value)
    return jnp.concatenate([a, a, b, a, b, c], axis)


def stack_right(value, axis):
    a, b, c = thirds(value)
    return jnp.concatenate([a, b, a, c, b, a], axis)


def fdot(left, right, ca, cb):
    return lax.dot_general(
        stack_left(left, ca),
        stack_right(right, cb),
        (((ca,), (cb,)), ((), ())),
        preferred_element_type=jnp.float32,
    )


def qr_kernel(count, stat_ref, basis_ref, out_ref, work):
    tiles = -(-count // PACK)
    rows = PACK * PAN
    panels = BS // PAN

    batch = next(size for size in (8, 6, 4, 3, 2, 1) if count % size == 0)

    def start(step, _):
        ids = [step * batch + c for c in range(batch)]
        stats = [stat_ref[b] for b in ids]
        bases = [basis_ref[b] for b in ids]
        scales = [
            1.0 / jnp.max(jnp.sum(jnp.abs(stat), -1, keepdims=True), 0, keepdims=True)
            for stat in stats
        ]
        xts = [fdot(base, stat, 0, 0) * scale for base, stat, scale in zip(bases, stats, scales)]
        grams = [fdot(xt, xt, 1, 1) for xt in xts]
        for b, xt, gram in zip(ids, xts, grams):
            for p in range(panels):
                work[p, pl.ds(b * PAN, PAN), :BS] = gram[p * PAN : (p + 1) * PAN]
                work[p, pl.ds(b * PAN, PAN), BS:] = xt[p * PAN : (p + 1) * PAN]
        return _

    lax.fori_loop(0, count // batch, start, 0)
    row_id = lax.broadcasted_iota(jnp.int32, (PAN, BS), 0)
    lane_id = lax.broadcasted_iota(jnp.int32, (PAN, BS), 1)
    group = lane_id // PAN
    for p in range(panels):
        packed = []
        for t in range(tiles):
            tile = jnp.zeros((PAN, BS), jnp.float32)
            for c in range(PACK):
                b = t * PACK + c
                if b < count:
                    diag = work[p, b * PAN : (b + 1) * PAN, :BS]
                    shift = (c - p) * PAN % BS
                    if shift:
                        diag = pltpu.roll(diag, shift, 1)
                    tile = jnp.where(group == c, diag, tile)
                else:
                    tile = jnp.where((group == c) & (lane_id % PAN == row_id), 1.0, tile)
            packed.append(tile)
        inverse = [jnp.where(lane_id % PAN == row_id, 1.0, 0.0) for _ in range(tiles)]
        scales = [jnp.ones((PAN, BS), jnp.float32) for _ in range(tiles)]
        for k in range(PAN):
            index = group * PAN + k
            for t in range(tiles):
                tile = packed[t]
                column = jnp.take_along_axis(tile, index, axis=1, mode="promise_in_bounds")
                pivot = column[k : k + 1]
                scales[t] = jnp.where(row_id == k, lax.rsqrt(pivot), scales[t])
                if k < PAN - 1:
                    factor = jnp.where(row_id > k, column * (1.0 / pivot), 0.0)
                    packed[t] = tile - factor * tile[k : k + 1]
                    inverse[t] = inverse[t] - factor * inverse[t][k : k + 1]
        for t in range(tiles):
            low = inverse[t] * scales[t]
            spread = jnp.concatenate([jnp.where(group == c, low, 0.0) for c in range(PACK)], 0)
            here = min(rows, (count - t * PACK) * PAN)
            spread = spread[:here]
            if here < rows:
                spread = spread[:, :here]
            span = slice(t * rows, t * rows + here)
            work[p, span, :] = fdot(spread, work[p, span, :], 1, 0)
        if p < panels - 1:

            def trail(step, _, p=p):
                ids = [step * batch + c for c in range(batch)]
                uppers = [work[p, pl.ds(b * PAN, PAN), :] for b in ids]
                changes = [fdot(upper[:, :BS], upper, 0, 0) for upper in uppers]
                for b, change in zip(ids, changes):
                    for q in range(p + 1, panels):
                        work[q, pl.ds(b * PAN, PAN), :] -= change[q * PAN : (q + 1) * PAN]
                return _

            lax.fori_loop(0, count // batch, trail, 0)

    def finish(b, _):
        rows_q = jnp.concatenate([work[p, pl.ds(b * PAN, PAN), BS:] for p in range(panels)], 0)
        out_ref[b] = rows_q.T
        return _

    lax.fori_loop(0, count, finish, 0, unroll=2)


def renew_all(stats, bases):
    count = stats.shape[0]
    return pl.pallas_call(
        functools.partial(qr_kernel, count),
        out_shape=jax.ShapeDtypeStruct((count, BS, BS), jnp.float32),
        in_specs=[pl.BlockSpec(memory_space=pltpu.VMEM)] * 2,
        out_specs=pl.BlockSpec(memory_space=pltpu.VMEM),
        scratch_shapes=[pltpu.VMEM((BS // PAN, count * PAN, 2 * BS), jnp.float32)],
        name="renew",
    )(stats, bases)


def soap_update(weight, first_moment, second_moment, left, right, left_rot, right_rot, grad):
    left = beta_two * left + (1.0 - beta_two) * jnp.einsum(
        "bij,bkj->bik", grad, grad, precision=HIGHEST
    )
    right = beta_two * right + (1.0 - beta_two) * jnp.einsum(
        "bji,bjk->bik", grad, grad, precision=HIGHEST
    )
    rotated = jnp.einsum("bji,bjk->bik", left_rot, grad, precision=HIGHEST)
    rotated = jnp.einsum("bij,bjk->bik", rotated, right_rot, precision=HIGHEST)
    first_moment = beta_one * first_moment + (1.0 - beta_one) * rotated
    second_moment = beta_two * second_moment + (1.0 - beta_two) * rotated * rotated
    direction = (
        first_moment
        / (1.0 - beta_one**STEP)
        / (jnp.sqrt(second_moment / (1.0 - beta_two**STEP)) + epsilon)
    )
    direction = jnp.einsum("bij,bjk->bik", left_rot, direction, precision=HIGHEST)
    direction = jnp.einsum("bij,bkj->bik", direction, right_rot, precision=HIGHEST)
    weight = weight - learn_rate * (direction + weight_decay * weight)
    count = weight.shape[0]
    renewed = renew_all(
        jnp.concatenate([left, right], 0), jnp.concatenate([left_rot, right_rot], 0)
    )
    return (
        weight,
        first_moment,
        second_moment,
        left,
        right,
        renewed[:count],
        renewed[count:],
    )


def adam_update(weight, first_moment, second_moment, grad, decay_rate, rate):
    first_moment = beta_one * first_moment + (1.0 - beta_one) * grad
    second_moment = beta_two * second_moment + (1.0 - beta_two) * grad * grad
    direction = (
        first_moment
        / (1.0 - beta_one**STEP)
        / (jnp.sqrt(second_moment / (1.0 - beta_two**STEP)) + epsilon)
    )
    return (weight - rate * (direction + decay_rate * weight), first_moment, second_moment)


def shards(
    latents,
    actions,
    game_ids,
    action_masks,
    valid_steps,
    target_bins,
    target_fracs,
    continues,
    owner_order,
    blocks,
    block_first,
    block_second,
    left_stat,
    right_stat,
    left_basis,
    right_basis,
    latent_maps,
    latent_first,
    latent_second,
    head_weights,
    head_first,
    head_second,
    small_params,
    small_first,
    small_second,
    ema_critic,
    dp,
    fsdp,
):
    seqs_here = latents.shape[0]
    tokens = seqs_here * F
    inverse = jnp.argsort(owner_order)
    ids_all, maps_all = gathered_weights(
        blocks.astype(jnp.bfloat16), latent_maps.astype(jnp.bfloat16), inverse, dp, fsdp
    )
    latent_hot = (
        jnp.repeat(latents.reshape(tokens, GROUPS), CLASSES, axis=1)
        == jnp.tile(jnp.arange(CLASSES), GROUPS)[None, :]
    ).astype(jnp.bfloat16)
    action_hot = (actions.reshape(tokens, 1) == jnp.arange(NA)[None, :]).astype(jnp.float32)
    hidden = jnp.dot(latent_hot, maps_all[:LAT], preferred_element_type=jnp.float32)
    hidden = hidden + jnp.dot(action_hot, small_params[4 * LAYERS + 2 :], precision=HIGHEST)
    hidden = (hidden.reshape(seqs_here, F, D) + positions(F, D)[None]).reshape(tokens, D)
    layer_index = 0
    matrices = layer_mats(ids_all)
    hidden, kept_state = layer_forward(
        hidden, matrices, small_params[4 * layer_index : 4 * layer_index + 4], seqs_here
    )
    states_kept = [kept_state]
    final_norm, final_scaled, final_rstd = norm_forward(
        hidden, small_params[4 * LAYERS], small_params[4 * LAYERS + 1]
    )
    final_low = final_norm.astype(jnp.bfloat16)
    dyn_logits = dot_rows(final_low, maps_all[LAT:]).reshape(tokens, GROUPS, CLASSES)
    head_low = head_weights[:D].astype(jnp.bfloat16)
    head_out = jnp.dot(final_low, head_low, preferred_element_type=jnp.float32) + head_weights[D]
    frame_last = (jnp.arange(F) < F - 1).astype(jnp.float32)[None, :]
    later = (jnp.roll(valid_steps, -1, axis=1).astype(jnp.float32) * frame_last).reshape(tokens)
    now = valid_steps.astype(jnp.float32).reshape(tokens)
    next_latent = jnp.roll(latents, -1, axis=1).reshape(tokens, GROUPS, 1)
    dyn_target = (next_latent == jnp.arange(CLASSES)).astype(jnp.float32)
    dyn_log = jax.nn.log_softmax(dyn_logits, -1)
    dyn_loss = -jnp.sum(jnp.sum(dyn_log * dyn_target, (1, 2)) * later)
    grad_dyn = (
        ((jnp.exp(dyn_log) - dyn_target) * later[:, None, None])
        .reshape(tokens, LAT)
        .astype(jnp.bfloat16)
    )
    bins_flat = target_bins.reshape(tokens, 2)
    fracs_flat = target_fracs.reshape(tokens, 2)
    reward_loss, reward_grad = two_hot_terms(head_out[:, :BINS], bins_flat[:, 0], fracs_flat[:, 0])
    critic_loss, critic_grad = two_hot_terms(
        head_out[:, BINS : 2 * BINS], bins_flat[:, 1], fracs_flat[:, 1]
    )
    cont_logit = head_out[:, 2 * BINS]
    cont_target = continues.reshape(tokens).astype(jnp.float32)
    cont_loss = jax.nn.softplus(cont_logit) - cont_target * cont_logit
    cont_grad = jax.nn.sigmoid(cont_logit) - cont_target
    game_hot = (game_ids[:, None] == jnp.arange(NGAME)[None, :]).astype(jnp.float32)
    legal_rows = jnp.dot(game_hot, action_masks.astype(jnp.float32), precision=HIGHEST)
    legal_tok = (
        jnp.broadcast_to(legal_rows[:, None, :], (seqs_here, F, NA)).reshape(tokens, NA) > 0.5
    )
    masked = jnp.where(legal_tok, head_out[:, 2 * BINS + 1 :], -1e30)
    actor_log = jax.nn.log_softmax(masked, -1)
    next_action = (
        jnp.roll(actions, -1, axis=1).reshape(tokens, 1) == jnp.arange(NA)[None, :]
    ).astype(jnp.float32)
    actor_loss = -jnp.sum(jnp.sum(actor_log * next_action, -1) * later)
    loss_local = dyn_loss + actor_loss + jnp.sum((reward_loss + critic_loss + cont_loss) * now)
    grad_head = jnp.concatenate(
        [
            reward_grad * now[:, None],
            critic_grad * now[:, None],
            (cont_grad * now)[:, None],
            (jnp.exp(actor_log) - next_action) * later[:, None],
        ],
        1,
    )
    grad_head = grad_head.astype(jnp.bfloat16)
    grad_dyn_table = dot_cols(grad_dyn, final_low)
    grad_head_matrix = dot_cols(final_low, grad_head)
    grad_head_bias = jnp.sum(grad_head.astype(jnp.float32), 0)
    grad_final = jnp.dot(grad_dyn, maps_all[LAT:], preferred_element_type=jnp.float32) + dot_rows(
        grad_head, head_low
    )
    grad_hidden, final_gain, final_bias = norm_backward(
        grad_final, final_scaled, final_rstd, small_params[4 * LAYERS]
    )
    block_parts = [None] * LAYERS
    small_parts = [None] * LAYERS
    for layer_index in reversed(range(LAYERS)):
        matrices = layer_mats(ids_all)
        grad_hidden, matrix_grads, gain_grads = layer_backward(
            grad_hidden,
            matrices,
            small_params[4 * layer_index : 4 * layer_index + 4],
            states_kept[layer_index],
            seqs_here,
        )
        block_parts[layer_index] = jnp.concatenate([to_blocks(piece) for piece in matrix_grads], 0)
        small_parts[layer_index] = gain_grads
    grad_lat_table = dot_cols(latent_hot, grad_hidden.astype(jnp.bfloat16))
    grad_act_table = lax.dot_general(
        action_hot, grad_hidden, (((0,), (0,)), ((), ())), precision=HIGHEST
    )
    grad_ids = block_parts[0]
    grad_maps = jnp.concatenate([grad_lat_table, grad_dyn_table], 0)
    small_local = jnp.concatenate(
        small_parts + [final_gain[None], final_bias[None], grad_act_table], 0
    )
    head_local = jnp.concatenate([grad_head_matrix, grad_head_bias[None]], 0)
    local_sums = jnp.stack([loss_local, jnp.sum(now)])
    block_grad, maps_grad, packed_grad, square, sums = reduced_grads(
        grad_ids, grad_maps, pack_heads(head_local, small_local), owner_order, local_sums, dp, fsdp
    )
    head_grad, small_grad = unpack_heads(packed_grad, head_weights.shape, small_params.shape[0])
    counted = sums[1]
    loss_value = sums[0] / counted
    grad_norm = jnp.sqrt(square) / counted
    factor = jnp.minimum(1.0, clip_norm / grad_norm) / counted
    soap_out = soap_update(
        blocks,
        block_first,
        block_second,
        left_stat,
        right_stat,
        left_basis,
        right_basis,
        block_grad * factor,
    )
    maps_out = adam_update(
        latent_maps, latent_first, latent_second, maps_grad * factor, weight_decay, learn_rate
    )
    heads_out = adam_update(
        head_weights, head_first, head_second, head_grad * factor, weight_decay, learn_rate
    )
    small_out = adam_update(
        small_params, small_first, small_second, small_grad * factor, 0.0, small_rate
    )
    ema_new = ema_rate * ema_critic + (1.0 - ema_rate) * heads_out[0][:, BINS : 2 * BINS]
    return (
        loss_value,
        grad_norm,
        soap_out[0],
        soap_out[1],
        soap_out[2],
        soap_out[3],
        soap_out[4],
        soap_out[5],
        soap_out[6],
        maps_out[0],
        maps_out[1],
        maps_out[2],
        heads_out[0],
        heads_out[1],
        heads_out[2],
        small_out[0],
        small_out[1],
        small_out[2],
        ema_new,
    )


def solution(mesh):
    placed = (
        P(("dp", "fsdp"), None, None),
        P(("dp", "fsdp"), None),
        P(("dp", "fsdp")),
        P(),
        P(("dp", "fsdp"), None),
        P(("dp", "fsdp"), None, None),
        P(("dp", "fsdp"), None, None),
        P(("dp", "fsdp"), None),
        P(),
        P("fsdp", None, None),
        P("fsdp", None, None),
        P("fsdp", None, None),
        P("fsdp", None, None),
        P("fsdp", None, None),
        P("fsdp", None, None),
        P("fsdp", None, None),
        P("fsdp", None),
        P("fsdp", None),
        P("fsdp", None),
        P(),
        P(),
        P(),
        P(),
        P(),
        P(),
        P(),
    )
    return jax.shard_map(
        functools.partial(shards, dp=mesh.shape["dp"], fsdp=mesh.shape["fsdp"]),
        mesh=mesh,
        in_specs=placed,
        out_specs=(
            P(),
            P(),
            P("fsdp", None, None),
            P("fsdp", None, None),
            P("fsdp", None, None),
            P("fsdp", None, None),
            P("fsdp", None, None),
            P("fsdp", None, None),
            P("fsdp", None, None),
            P("fsdp", None),
            P("fsdp", None),
            P("fsdp", None),
            P(),
            P(),
            P(),
            P(),
            P(),
            P(),
            P(),
        ),
        check_vma=False,
    )
```

```python
import functools
import math

import jax
import jax.numpy as jnp
from jax import lax
from jax.experimental import pallas as pl
from jax.experimental.pallas import tpu as pltpu
from jax.sharding import PartitionSpec as P

D = 512
NH = 8
DH = 64
FF = 2048
GROUPS = 32
CLASSES = 32
LAT = 1024
BINS = 255
NA = 18
LAYERS = 1
F = 64
NGAME = 26
BS = 128
STEP = 10
PAN = 16
PACK = 8
HEAD_COLS = 640
PACK_ROWS = 3072
MAP_CHUNKS = ((0, 1), (2,), (3,))
PART_ROWS = (384, 368, 368)
TM = 256
GELU_A = math.sqrt(2.0 / math.pi)
GELU_B = 0.044715


HIGHEST = lax.Precision.HIGHEST
beta_one = 0.9
beta_two = 0.99
epsilon = 1e-08
learn_rate = 0.03
small_rate = 0.15
weight_decay = 0.01
clip_norm = 0.05
ema_rate = 0.98
norm_eps = 1e-05


def positions(frames, width):
    frame_index = jnp.arange(frames).astype(jnp.float32)[:, None]
    feature = jnp.arange(width)
    freq = jnp.exp(-(feature // 2 * 2).astype(jnp.float32) * (math.log(10000.0) / width))
    angle = frame_index * freq[None, :]
    return jnp.where(feature % 2 == 0, jnp.sin(angle), jnp.cos(angle))


def halves(size):
    return [1 << bit for bit in reversed(range(size.bit_length() - 1))]


def swap(value, axis, size, bit):
    return lax.ppermute(value, axis, [(i, i ^ bit) for i in range(size)])


def sum_small(value, dp, fsdp):
    for axis, size in (("dp", dp), ("fsdp", fsdp)):
        for bit in reversed(halves(size)):
            value = value + swap(value, axis, size, bit)
    return value


def part_orders(dp, fsdp):
    core, tall = [("dp", dp, bit) for bit in reversed(halves(dp))]
    deep, near, side = [("fsdp", fsdp, bit) for bit in halves(fsdp)]
    return (
        (core, tall, side, near, deep),
        (core, side, near, deep, tall),
        (core, near, tall, side, deep),
    )


def order_index(order, dp_here, fsdp_here):
    dp_index = jnp.zeros((), jnp.int32)
    fsdp_index = jnp.zeros((), jnp.int32)
    spot = jnp.arange(1 << len(order))
    for place, (axis, _, bit) in enumerate(order):
        flag = (spot >> (len(order) - 1 - place)) & 1
        if axis == "dp":
            dp_index = dp_index + flag * bit
        else:
            fsdp_index = fsdp_index + flag * bit
    return dp_index ^ dp_here, fsdp_index ^ fsdp_here


def scatter_sum(held, sent, order, wide_stages):
    for place, (axis, size, bit) in enumerate(order):
        got = swap(sent, axis, size, bit)
        held = held + got.astype(jnp.float32)
        half = held.shape[0] // 2
        if half:
            held, sent = held[:half], held[half:]
            if place + 1 < len(order) - wide_stages:
                sent = sent.astype(jnp.bfloat16)
    return held[0]


def gather_doubling(value, order):
    held = value[None]
    for axis, size, bit in reversed(order):
        held = jnp.concatenate([held, swap(held, axis, size, bit)], 0)
    return held


def inverse_place(order, dp, fsdp, dp_here, fsdp_here):
    dp_id = jnp.arange(dp)[None, :] ^ dp_here
    fsdp_id = jnp.arange(fsdp)[:, None] ^ fsdp_here
    spot = jnp.zeros((fsdp, dp), jnp.int32)
    for place, (axis, _, bit) in enumerate(order):
        source = dp_id if axis == "dp" else fsdp_id
        flag = (source & bit) // bit
        spot = spot + flag * (1 << (len(order) - 1 - place))
    return spot


def placed_units(dp, fsdp):
    dp_here = lax.axis_index("dp")
    fsdp_here = lax.axis_index("fsdp")
    units = []
    spots = []
    for order in part_orders(dp, fsdp):
        dp_index, fsdp_index = order_index(order, dp_here, fsdp_here)
        units.append(fsdp_index * dp + dp_index)
        spots.append(inverse_place(order, dp, fsdp, dp_here, fsdp_here).reshape(-1))
    return jnp.stack(units), jnp.stack(spots)


def gathered_pieces(blocks_low, maps_low, dp, fsdp):
    dp_here = lax.axis_index("dp")
    quarter = blocks_low.shape[0] // dp
    piece_rows = maps_low.shape[0] // dp
    own_blocks = lax.dynamic_slice_in_dim(blocks_low, dp_here * quarter, quarter, 0)
    own_maps = lax.dynamic_slice_in_dim(maps_low, dp_here * piece_rows, piece_rows, 0)
    pieces = []
    for part, order in enumerate(part_orders(dp, fsdp)):
        piece = jnp.concatenate(
            [own_blocks[2 * part], own_blocks[2 * part + 1]]
            + [own_maps[:, c * BS : (c + 1) * BS] for c in MAP_CHUNKS[part]],
            0,
        )
        held = gather_doubling(piece, order[2:])
        both = [held, swap(held, *order[1])]
        pieces += both + [swap(piece, *order[0]) for piece in both]
    return pieces


def reduced_grads(outs, sums, slots, map_rows, dp, fsdp):
    if (dp, fsdp) != (4, 8):
        both = ("dp", "fsdp")
        block_grad = lax.psum(
            lax.psum_scatter(outs[0], "fsdp", scatter_dimension=0, tiled=True), "dp"
        )
        maps_grad = lax.psum(
            lax.psum_scatter(outs[1], "fsdp", scatter_dimension=0, tiled=True), "dp"
        )
        heads = lax.psum(outs[2], both)
        sums = lax.psum(sums, both)
        held = lax.psum(jnp.sum(block_grad * block_grad) + jnp.sum(maps_grad * maps_grad), "fsdp")
        return block_grad, maps_grad, heads, held + jnp.sum(heads * heads), sums
    dp_here = lax.axis_index("dp")
    fsdp_here = lax.axis_index("fsdp")
    parts = [
        scatter_sum(outs[2 * part], outs[2 * part + 1], order, 2)
        for part, order in enumerate(part_orders(dp, fsdp))
    ]
    cut = 2 * BS
    own_blocks = jnp.concatenate([part[:cut] for part in parts], 0)
    own_maps = jnp.concatenate([parts[0][cut:], parts[1][cut : cut + 64], parts[2][cut : cut + 64]], 0)
    own_heads = jnp.concatenate([parts[1][cut + 64 :], parts[2][cut + 64 :]], 0)
    own_square = sum(jnp.sum(part * part) for part in parts)
    sums = sum_small(jnp.concatenate([sums, own_square[None]]), dp, fsdp)
    dp_order = [("dp", dp, bit) for bit in reversed(halves(dp))]
    spot = inverse_place(dp_order, dp, 1, dp_here, 0).reshape(-1)
    shard = gather_doubling(jnp.concatenate([own_blocks, own_maps], 0), dp_order)
    shard = shard[spot]
    count = slots // dp * BS
    piece_rows = map_rows // dp
    block_grad = shard[:, :count].reshape(slots, BS, BS)
    maps_grad = (
        shard[:, count:]
        .reshape(dp, D // BS, piece_rows, BS)
        .transpose(0, 2, 1, 3)
        .reshape(map_rows, D)
    )
    full_order = part_orders(dp, fsdp)[0]
    all_heads = gather_doubling(own_heads, full_order)
    spot = inverse_place(full_order, dp, fsdp, dp_here, fsdp_here).reshape(-1)
    return block_grad, maps_grad, all_heads[spot].reshape(-1, BS), sums[-1], sums[:-1]


def norm_rows(inputs, gain_row, bias_row):
    center = inputs - jnp.mean(inputs, -1, keepdims=True)
    rstd = lax.rsqrt(jnp.mean(center * center, -1, keepdims=True) + norm_eps)
    scaled = center * rstd
    return scaled * gain_row + bias_row, scaled, rstd


def norm_rows_back(grad_out, scaled, rstd, gain_row):
    grad_scaled = grad_out * gain_row
    return rstd * (
        grad_scaled
        - jnp.mean(grad_scaled, -1, keepdims=True)
        - scaled * jnp.mean(grad_scaled * scaled, -1, keepdims=True)
    )


def dot32(left, right, ca, cb):
    return lax.dot_general(
        left, right, (((ca,), (cb,)), ((), ())), preferred_element_type=jnp.float32
    )


def model_kernel(fast, rows_of, *refs):
    refs = list(refs)
    take = lambda count: [refs.pop(0) for _ in range(count)]
    (owner, units, block_place, unit_place) = take(4)
    sources = take(12 if fast else 2)
    (hot, target, later_row, base, facts, legal, next_hot, act_hot, gains, head_w, head_b) = take(11)
    outs = take(6 if fast else 3)
    (sums_out,) = take(1)
    (wall, maps) = take(2)
    (normed1, qkv, probs, mixed, normed2, slope, act, final, grad_dyn, grad_head) = take(10)
    (grad_low, grad_pre, grad_mid, grad_qkv, grad_hid, small, bias_sum) = take(7)
    if fast:
        keep, send = take(2)
    wall_sem, maps_sem, out_sem = take(3)
    tokens = base.shape[0]
    tile = D // BS
    wide = FF // BS
    out_at = 3 * tile * tile
    expand_at = out_at + tile * tile
    contract_at = expand_at + tile * wide

    if fast:
        for part in range(3):
            for piece in range(4):
                source = sources[part * 4 + piece]

                def fetch(j, carry, part=part, piece=piece, source=source):
                    unit = units[part * 32 + piece * 8 + j]
                    for k in range(2):
                        block = owner[unit * 6 + part * 2 + k]
                        pltpu.make_async_copy(
                            source.at[j, k * BS : (k + 1) * BS, :], wall.at[block], wall_sem
                        ).start()
                    for i, chunk in enumerate(MAP_CHUNKS[part]):
                        pltpu.make_async_copy(
                            source.at[j, 2 * BS + i * 64 : 2 * BS + (i + 1) * 64, :],
                            maps.at[
                                pl.ds(pl.multiple_of(unit * 64, 64), 64),
                                chunk * BS : (chunk + 1) * BS,
                            ],
                            maps_sem,
                        ).start()
                    return carry

                lax.fori_loop(0, 8, fetch, 0)
    else:

        def fetch(j, carry):
            pltpu.make_async_copy(sources[0].at[j], wall.at[owner[j]], wall_sem).start()
            return carry

        lax.fori_loop(0, wall.shape[0], fetch, 0)
        pltpu.make_async_copy(sources[1], maps, maps_sem).start()
    small[...] = jnp.zeros_like(small)
    bias_sum[...] = jnp.zeros_like(bias_sum)
    sums_out[...] = jnp.zeros_like(sums_out)
    pltpu.make_async_copy(wall, wall, wall_sem).wait()
    pltpu.make_async_copy(maps, maps, maps_sem).wait()

    def grid_of(start, stride, row_count, col_count):
        return jnp.concatenate(
            [
                jnp.concatenate([wall[start + r * stride + c] for c in range(col_count)], 1)
                for r in range(row_count)
            ],
            0,
        )

    def chunk(step, carry):
        rows = pl.ds(pl.multiple_of(step * TM, TM), TM)
        hidden = dot32(hot[:, rows], maps[:LAT, :], 0, 0) + base[rows, :]
        normed, scaled1, rstd1 = norm_rows(hidden, gains[0:1], gains[1:2])
        normed1[rows, :] = normed.astype(jnp.bfloat16)

        def joint_strip(s, c):
            cols = pl.ds(pl.multiple_of(s * 256, 256), 256)
            weight = grid_of(2 * s, 3 * tile, tile, 2)
            qkv[rows, cols] = dot32(normed1[rows, :], weight, 1, 0).astype(jnp.bfloat16)
            return c

        lax.fori_loop(0, 6, joint_strip, 0)
        lane = lax.broadcasted_iota(jnp.int32, (BS, BS), 1)
        line = lax.broadcasted_iota(jnp.int32, (BS, BS), 0)
        allowed = (line >= lane) & (line // F == lane // F)
        low_half = lane < DH
        halves_of = [mask.astype(jnp.float32).astype(jnp.bfloat16) for mask in (low_half, ~low_half)]

        def attend(s, c):
            sub = pl.ds(pl.multiple_of(step * TM + s * BS, BS), BS)
            for pair in range(NH // 2):
                spans = [slice(part * D + pair * BS, part * D + (pair + 1) * BS) for part in range(3)]
                query, key, value = [qkv[sub, span] for span in spans]
                mixes = []
                for side in range(2):
                    half = halves_of[side]
                    scores = dot32(query * half, key, 1, 1) * DH ** (-0.5)
                    scores = jnp.where(allowed, scores, -1e30)
                    shifted = scores - jnp.max(scores, -1, keepdims=True)
                    power = jnp.exp(shifted)
                    prob = power / jnp.sum(power, -1, keepdims=True)
                    probs[2 * pair + side, sub, :] = prob
                    mixes.append(dot32(prob.astype(jnp.bfloat16), value, 1, 0))
                mixed[sub, pair * BS : (pair + 1) * BS] = jnp.where(low_half, *mixes).astype(
                    jnp.bfloat16
                )
            return c

        lax.fori_loop(0, TM // BS, attend, 0)
        out_map = grid_of(out_at, tile, tile, tile)
        middle = hidden + dot32(mixed[rows, :], out_map, 1, 0)
        normed, scaled2, rstd2 = norm_rows(middle, gains[2:3], gains[3:4])
        normed2[rows, :] = normed.astype(jnp.bfloat16)

        def expand_strip(s, c):
            cols = pl.ds(pl.multiple_of(s * 256, 256), 256)
            weight = grid_of(expand_at + 2 * s, wide, tile, 2)
            pre = dot32(normed2[rows, :], weight, 1, 0)
            square = pre * pre
            curve = jnp.tanh(GELU_A * (pre + GELU_B * (square * pre)))
            act[rows, cols] = (0.5 * pre * (1.0 + curve)).astype(jnp.bfloat16)
            slope[:, cols] = 0.5 * (1.0 + curve) + 0.5 * pre * (1.0 - curve * curve) * (
                GELU_A * (1.0 + 3.0 * GELU_B * square)
            )
            return c

        lax.fori_loop(0, FF // 256, expand_strip, 0)

        def contract_strip(s, total):
            cols = pl.ds(pl.multiple_of(s * 512, 512), 512)
            weight = grid_of(contract_at + s * 4 * tile, tile, 4, tile)
            return total + dot32(act[rows, cols], weight, 1, 0)

        top = lax.fori_loop(0, FF // 512, contract_strip, middle)
        normed, scaled3, rstd3 = norm_rows(top, gains[4:5], gains[5:6])
        final[rows, :] = normed.astype(jnp.bfloat16)
        late = later_row[0:1, rows]

        def dyn_strip(s, total):
            span = pl.ds(pl.multiple_of(s * 256, 256), 256)
            below = pl.ds(pl.multiple_of(LAT + s * 256, 256), 256)
            logits = dot32(maps[below, :], final[rows, :], 1, 1)
            logits = logits.reshape(256 // CLASSES, CLASSES, TM)
            shifted = logits - jnp.max(logits, 1, keepdims=True)
            power = jnp.exp(shifted)
            norm = jnp.sum(power, 1, keepdims=True)
            wanted = target[span, rows].astype(jnp.float32).reshape(256 // CLASSES, CLASSES, TM)
            spent = jnp.sum(wanted * (jnp.log(norm) - shifted), 0)
            grad = (power / norm - wanted) * late[None]
            grad_dyn[span, rows] = grad.reshape(256, TM).astype(jnp.bfloat16)
            return total + jnp.sum(spent, 0, keepdims=True) * late

        dyn_loss = lax.fori_loop(0, LAT // 256, dyn_strip, jnp.zeros((1, TM), jnp.float32))
        heads = dot32(final[rows, :], head_w[...], 1, 0) + head_b[0:1]
        now = facts[rows, 0:1]
        late_col = facts[rows, 1:2]
        spot = lax.broadcasted_iota(jnp.int32, (TM, 256), 1).astype(jnp.float32)
        frame_loss = jnp.zeros((TM, 1), jnp.float32)
        for which in range(2):
            logits = heads[:, which * 256 : (which + 1) * 256]
            bin_low = facts[rows, 2 + which : 3 + which]
            upper = facts[rows, 4 + which : 5 + which]
            weights = jnp.where(spot == bin_low, 1.0 - upper, 0.0)
            weights = weights + jnp.where(spot == bin_low + 1.0, upper, 0.0)
            shifted = logits - jnp.max(logits, -1, keepdims=True)
            power = jnp.exp(shifted)
            norm = jnp.sum(power, -1, keepdims=True)
            frame_loss = frame_loss + jnp.sum(
                weights * jnp.where(weights > 0.0, jnp.log(norm) - shifted, 0.0), -1, keepdims=True
            )
            grad = (power / norm - weights) * now
            grad_head[rows, which * 256 : (which + 1) * 256] = grad.astype(jnp.bfloat16)
            bias_sum[0:1, which * 256 : (which + 1) * 256] += jnp.sum(
                grad.astype(jnp.bfloat16).astype(jnp.float32), 0, keepdims=True
            )
        tail = heads[:, 512:640]
        logit = tail[:, 0:1]
        goal = facts[rows, 6:7]
        soft = jnp.maximum(logit, 0.0) + jnp.log1p(jnp.exp(-jnp.abs(logit)))
        frame_loss = (frame_loss + soft - goal * logit) * now
        may = legal[rows, :]
        chosen = next_hot[rows, :]
        masked = jnp.where(may > 0.5, tail, -1e30)
        shifted = masked - jnp.max(masked, -1, keepdims=True)
        power = jnp.exp(shifted)
        norm = jnp.sum(power, -1, keepdims=True)
        actor = jnp.sum(
            jnp.where(chosen > 0.5, jnp.log(norm) - shifted, 0.0), -1, keepdims=True
        )
        frame_loss = frame_loss + actor * late_col
        grad = (power / norm - chosen) * late_col
        column = lax.broadcasted_iota(jnp.int32, (TM, BS), 1)
        grad = jnp.where(column == 0, (jax.nn.sigmoid(logit) - goal) * now, grad)
        grad_head[rows, 512:640] = grad.astype(jnp.bfloat16)
        bias_sum[0:1, 512:640] += jnp.sum(
            grad.astype(jnp.bfloat16).astype(jnp.float32), 0, keepdims=True
        )
        sums_out[0:1, :] += jnp.broadcast_to(
            jnp.sum(dyn_loss, -1, keepdims=True) + jnp.sum(frame_loss, 0, keepdims=True), (1, BS)
        )
        sums_out[1:2, :] += jnp.broadcast_to(jnp.sum(now, 0, keepdims=True), (1, BS))

        grad_final = dot32(grad_dyn[:, rows], maps[LAT:, :], 0, 0) + dot32(
            grad_head[rows, :], head_w[...], 1, 1
        )
        small[4:5, :] += jnp.sum(grad_final * scaled3, 0, keepdims=True)
        small[5:6, :] += jnp.sum(grad_final, 0, keepdims=True)
        grad_top = norm_rows_back(grad_final, scaled3, rstd3, gains[4:5])
        grad_low[rows, :] = grad_top.astype(jnp.bfloat16)

        def act_strip(s, total):
            cols = pl.ds(pl.multiple_of(s * 256, 256), 256)
            weight = grid_of(contract_at + s * 2 * tile, tile, 2, tile)
            grad = dot32(grad_low[rows, :], weight, 1, 1) * slope[:, cols]
            grad = grad.astype(jnp.bfloat16)
            grad_pre[rows, cols] = grad
            weight = grid_of(expand_at + 2 * s, wide, tile, 2)
            return total + dot32(grad, weight, 1, 1)

        grad_normed = lax.fori_loop(
            0, FF // 256, act_strip, jnp.zeros((TM, D), jnp.float32)
        )
        small[2:3, :] += jnp.sum(grad_normed * scaled2, 0, keepdims=True)
        small[3:4, :] += jnp.sum(grad_normed, 0, keepdims=True)
        grad_middle = grad_top + norm_rows_back(grad_normed, scaled2, rstd2, gains[2:3])
        grad_mid[rows, :] = grad_middle.astype(jnp.bfloat16)
        out_map = grid_of(out_at, tile, tile, tile)
        mixed_grad = dot32(grad_mid[rows, :], out_map, 1, 1).astype(jnp.bfloat16)
        grad_hid[rows, :] = mixed_grad

        def attend_back(s, c):
            sub = pl.ds(pl.multiple_of(step * TM + s * BS, BS), BS)
            for pair in range(NH // 2):
                spans = [slice(part * D + pair * BS, part * D + (pair + 1) * BS) for part in range(3)]
                query, key, value = [qkv[sub, span] for span in spans]
                grad_out = grad_hid[sub, pair * BS : (pair + 1) * BS]
                totals = [jnp.zeros((BS, BS), jnp.float32) for _ in range(3)]
                for side in range(2):
                    half = halves_of[side]
                    prob = probs[2 * pair + side, sub, :]
                    out_half = grad_out * half
                    grad_prob = dot32(out_half, value, 1, 1)
                    dots = jnp.sum(grad_prob * prob, -1, keepdims=True)
                    grad_score = (prob * (grad_prob - dots)).astype(jnp.bfloat16)
                    totals[0] += dot32(grad_score, key * half, 1, 0)
                    totals[1] += dot32(grad_score, query * half, 0, 0)
                    totals[2] += dot32(prob.astype(jnp.bfloat16), out_half, 0, 0)
                for part, (span, total) in enumerate(zip(spans, totals)):
                    scale = DH ** (-0.5) if part < 2 else 1.0
                    grad_qkv[sub, span] = (total * scale).astype(jnp.bfloat16)
            return c

        lax.fori_loop(0, TM // BS, attend_back, 0)

        def joint_back(s, total):
            cols = pl.ds(pl.multiple_of(s * 512, 512), 512)
            weight = grid_of(4 * s, 3 * tile, tile, 4)
            return total + dot32(grad_qkv[rows, cols], weight, 1, 1)

        grad_normed = lax.fori_loop(0, 3, joint_back, jnp.zeros((TM, D), jnp.float32))
        small[0:1, :] += jnp.sum(grad_normed * scaled1, 0, keepdims=True)
        small[1:2, :] += jnp.sum(grad_normed, 0, keepdims=True)
        grad_in = grad_middle + norm_rows_back(grad_normed, scaled1, rstd1, gains[0:1])
        grad_hid[rows, :] = grad_in.astype(jnp.bfloat16)
        pieces = thirds(grad_in)
        small[...] += sum(dot32(act_hot[:, rows], piece, 1, 0) for piece in pieces)
        return carry

    lax.fori_loop(0, tokens // TM, chunk, 0)

    def put(place, rows, first, value):
        part = (place >> 8) & 3
        spot = place & 15
        dest = pl.ds(first, rows)

        @pl.when(((place >> 4) & 1) == 0)
        def _():
            keep[part, spot, dest, :] = value

        @pl.when(((place >> 4) & 1) == 1)
        def _():
            send[part, spot, dest, :] = value.astype(jnp.bfloat16)

    def put_block(block, value):
        place = block_place[block]
        if fast:
            put(place, BS, pl.multiple_of(((place >> 10) & 1) * BS, BS), value)
        else:
            outs[0][place] = value

    def block_grads(start, stride, left, right, row_count, col_steps):
        def strip(s, c):
            cols = pl.ds(pl.multiple_of(s * 256, 256), 256)
            grads = dot32(left, right[:, cols], 0, 0)
            for r in range(row_count):
                for k in range(2):
                    put_block(
                        start + r * stride + 2 * s + k,
                        grads[r * BS : (r + 1) * BS, k * BS : (k + 1) * BS],
                    )
            return c

        lax.fori_loop(0, col_steps, strip, 0)

    block_grads(0, 3 * tile, normed1[...], grad_qkv, tile, 6)
    block_grads(out_at, tile, mixed[...], grad_mid, tile, 2)
    block_grads(expand_at, wide, normed2[...], grad_pre, tile, FF // 256)

    def contract_rows(m, c):
        cols = pl.ds(pl.multiple_of(m * D, D), D)
        for s in range(2):
            grads = dot32(act[:, cols], grad_low[:, s * 256 : (s + 1) * 256], 0, 0)
            for r in range(tile):
                for k in range(2):
                    put_block(
                        contract_at + (m * tile + r) * tile + 2 * s + k,
                        grads[r * BS : (r + 1) * BS, k * BS : (k + 1) * BS],
                    )
        return c

    lax.fori_loop(0, FF // D, contract_rows, 0)

    def map_rows(m, c):
        span = pl.ds(pl.multiple_of(m * 256, 256), 256)
        for table in range(2):
            source, other = ((hot, grad_hid), (grad_dyn, final))[table]
            grads = dot32(source[span, :], other[...], 1, 0)
            if not fast:
                outs[1][pl.ds(pl.multiple_of(table * LAT + m * 256, 256), 256), :] = grads
                continue
            for u in range(4):
                unit = table * (LAT // 64) + m * 4 + u
                for part in range(3):
                    place = unit_place[part * 32 + unit]
                    for i, piece in enumerate(MAP_CHUNKS[part]):
                        put(
                            place,
                            64,
                            2 * BS + i * 64,
                            grads[u * 64 : (u + 1) * 64, piece * BS : (piece + 1) * BS],
                        )
        return c

    lax.fori_loop(0, LAT // 256, map_rows, 0)
    pieces = []
    for c in range(5):
        pieces.append(dot32(final[...], grad_head[:, c * BS : (c + 1) * BS], 0, 0))
    packed = jnp.concatenate(
        pieces
        + [
            bias_sum[0:1, c * BS : (c + 1) * BS] if c < 5 else jnp.zeros((3, BS), jnp.float32)
            for c in range(6)
        ]
        + [small[:, c * BS : (c + 1) * BS] for c in range(tile)]
        + [jnp.zeros((PACK_ROWS - 5 * D - 8 - tile * small.shape[0], BS), jnp.float32)],
        0,
    )
    if not fast:
        outs[2][...] = packed
        return
    for unit in range(32):
        for half in range(2):
            part = 1 + half
            place = unit_place[part * 32 + unit]
            first = unit * 96 + half * 48
            put(place, 48, 2 * BS + 64, packed[first : first + 48])
    copies = []
    for part in range(3):
        for which, scratch in enumerate((keep, send)):
            copies.append(
                pltpu.make_async_copy(
                    scratch.at[part, :, 0 : rows_of[part], :],
                    outs[part * 2 + which],
                    out_sem.at[part * 2 + which],
                )
            )
    for copy in copies:
        copy.start()
    for copy in copies:
        copy.wait()


def spread_cols(head):
    gap = jnp.zeros((head.shape[0], 1), head.dtype)
    rest = jnp.zeros((head.shape[0], BS - 1 - NA), head.dtype)
    return jnp.concatenate(
        [head[:, :BINS], gap, head[:, BINS : 2 * BINS], gap, head[:, 2 * BINS :], rest], 1
    )


def unpack_heads(packed, small_rows):
    chunks = [packed[c * D : (c + 1) * D] for c in range(5)]
    bias = jnp.concatenate([packed[5 * D + c : 5 * D + c + 1] for c in range(5)], 1)
    head = jnp.concatenate([jnp.concatenate(chunks, 1), bias], 0)
    head = jnp.concatenate(
        [head[:, :BINS], head[:, 256 : 256 + BINS], head[:, 512 : 513 + NA]], 1
    )
    start = 5 * D + 8
    small = jnp.concatenate(
        [packed[start + c * small_rows : start + (c + 1) * small_rows] for c in range(D // BS)], 1
    )
    return head, small


def model_grads(
    latents, actions, game_ids, action_masks, valid_steps, target_bins, target_fracs, continues,
    owner_order, blocks, latent_maps, head_weights, small_params, dp, fsdp,
):
    fast = (dp, fsdp) == (4, 8)
    seqs_here = latents.shape[0]
    tokens = seqs_here * F
    blocks_low = blocks.astype(jnp.bfloat16)
    maps_low = latent_maps.astype(jnp.bfloat16)
    inverse = jnp.argsort(owner_order).astype(jnp.int32)
    if fast:
        sources = gathered_pieces(blocks_low, maps_low, dp, fsdp)
        units, spots = placed_units(dp, fsdp)
        part_ids = jnp.arange(3)[:, None]
        unit_place = (part_ids << 8) + spots
        slot_unit = inverse // 6
        slot_part = inverse % 6 // 2
        block_place = ((inverse % 2) << 10) + unit_place.reshape(-1)[slot_part * (dp * fsdp) + slot_unit]
        units = units.reshape(-1).astype(jnp.int32)
        unit_place = unit_place.reshape(-1).astype(jnp.int32)
        block_place = block_place.astype(jnp.int32)
    else:
        sources = [
            lax.all_gather(blocks_low, "fsdp", axis=0, tiled=True),
            lax.all_gather(maps_low, "fsdp", axis=0, tiled=True),
        ]
        units = unit_place = jnp.zeros((96,), jnp.int32)
        block_place = inverse
    class_ids = jnp.arange(CLASSES)[None, :, None]

    def one_hot_rows(values):
        rows = values.reshape(tokens, GROUPS).T
        return (rows[:, None, :] == class_ids).astype(jnp.bfloat16).reshape(LAT, tokens)

    frame_last = (jnp.arange(F) < F - 1).astype(jnp.float32)[None, :]
    later = (jnp.roll(valid_steps, -1, axis=1).astype(jnp.float32) * frame_last).reshape(tokens)
    now = valid_steps.astype(jnp.float32).reshape(tokens)
    action_hot = (actions.reshape(tokens, 1) == jnp.arange(NA)[None, :]).astype(jnp.float32)
    base = jnp.dot(action_hot, small_params[4 * LAYERS + 2 :], precision=HIGHEST)
    base = (base.reshape(seqs_here, F, D) + positions(F, D)[None]).reshape(tokens, D)
    facts = jnp.concatenate(
        [
            now[:, None],
            later[:, None],
            target_bins.reshape(tokens, 2).astype(jnp.float32),
            target_fracs.reshape(tokens, 2),
            continues.reshape(tokens, 1).astype(jnp.float32),
            jnp.zeros((tokens, BS - 7), jnp.float32),
        ],
        1,
    )
    game_hot = (game_ids[:, None] == jnp.arange(NGAME)[None, :]).astype(jnp.float32)
    legal_rows = jnp.dot(game_hot, action_masks.astype(jnp.float32), precision=HIGHEST)
    legal = jnp.broadcast_to(legal_rows[:, None, :], (seqs_here, F, NA)).reshape(tokens, NA)
    legal = jnp.pad(legal, ((0, 0), (1, BS - 1 - NA)))
    next_hot = (
        jnp.roll(actions, -1, axis=1).reshape(tokens, 1) == jnp.arange(BS)[None, :] - 1
    ).astype(jnp.float32)
    small_rows = small_params.shape[0]
    act_hot = (
        jnp.arange(small_rows)[:, None] - (4 * LAYERS + 2) == actions.reshape(1, tokens)
    ).astype(jnp.bfloat16)
    gains = jnp.pad(small_params[: 4 * LAYERS + 2], ((0, 2), (0, 0)))
    head_wide = spread_cols(head_weights[:D].astype(jnp.bfloat16))
    column = jnp.arange(HEAD_COLS)[None, :]
    head_bias = jnp.where(
        (column == BINS) | (column == 256 + BINS), -1e30, spread_cols(head_weights[D:])
    )
    vmem = pl.BlockSpec(memory_space=pltpu.VMEM)
    smem = pl.BlockSpec(memory_space=pltpu.SMEM)
    away = pl.BlockSpec(memory_space=pl.ANY)
    low = jnp.bfloat16
    wide_type = jnp.float32
    if fast:
        shapes = []
        for rows in PART_ROWS:
            shapes += [((16, rows, BS), wide_type), ((16, rows, BS), low)]
        out_specs = [away] * 6 + [vmem]
    else:
        shapes = [
            (( 192, BS, BS), wide_type), ((2 * LAT, D), wide_type), ((PACK_ROWS, BS), wide_type)
        ]
        out_specs = [vmem] * 4
    shapes.append(((8, BS), wide_type))
    scratch = [
        pltpu.VMEM((owner_order.shape[0], BS, BS), low),
        pltpu.VMEM((2 * LAT, D), low),
        pltpu.VMEM((tokens, D), low),
        pltpu.VMEM((tokens, 3 * D), low),
        pltpu.VMEM((NH, tokens, BS), wide_type),
        pltpu.VMEM((tokens, D), low),
        pltpu.VMEM((tokens, D), low),
        pltpu.VMEM((TM, FF), wide_type),
        pltpu.VMEM((tokens, FF), low),
        pltpu.VMEM((tokens, D), low),
        pltpu.VMEM((LAT, tokens), low),
        pltpu.VMEM((tokens, HEAD_COLS), low),
        pltpu.VMEM((tokens, D), low),
        pltpu.VMEM((tokens, FF), low),
        pltpu.VMEM((tokens, D), low),
        pltpu.VMEM((tokens, 3 * D), low),
        pltpu.VMEM((tokens, D), low),
        pltpu.VMEM((small_rows, D), wide_type),
        pltpu.VMEM((8, HEAD_COLS), wide_type),
    ]
    if fast:
        scratch += [
            pltpu.VMEM((3, 16, PART_ROWS[0], BS), wide_type),
            pltpu.VMEM((3, 16, PART_ROWS[0], BS), low),
        ]
    scratch += [
        pltpu.SemaphoreType.DMA,
        pltpu.SemaphoreType.DMA,
        pltpu.SemaphoreType.DMA((6,)),
    ]
    *outs, sums = pl.pallas_call(
        functools.partial(model_kernel, fast, PART_ROWS),
        out_shape=[jax.ShapeDtypeStruct(shape, kind) for shape, kind in shapes],
        in_specs=[smem] * 4 + [away] * len(sources) + [vmem] * 11,
        out_specs=out_specs,
        scratch_shapes=scratch,
        compiler_params=pltpu.CompilerParams(vmem_limit_bytes=66 * 1000 * 1000),
        name="model",
    )(
        owner_order, units, block_place, unit_place, *sources,
        one_hot_rows(latents), one_hot_rows(jnp.roll(latents, -1, axis=1)),
        jnp.broadcast_to(later[None], (8, tokens)), base, facts, legal, next_hot, act_hot, gains,
        head_wide, jnp.broadcast_to(head_bias, (8, HEAD_COLS)),
    )
    return reduced_grads(outs, sums[:2, 0], blocks.shape[0], latent_maps.shape[0], dp, fsdp)


def thirds(value):
    first = value.astype(jnp.bfloat16)
    rest = value - first.astype(jnp.float32)
    second = rest.astype(jnp.bfloat16)
    third = (rest - second.astype(jnp.float32)).astype(jnp.bfloat16)
    return first, second, third


def stack_left(value, axis):
    a, b, c = thirds(value)
    return jnp.concatenate([a, a, b, a, b, c], axis)


def stack_right(value, axis):
    a, b, c = thirds(value)
    return jnp.concatenate([a, b, a, c, b, a], axis)


def fdot(left, right, ca, cb):
    return lax.dot_general(
        stack_left(left, ca),
        stack_right(right, cb),
        (((ca,), (cb,)), ((), ())),
        preferred_element_type=jnp.float32,
    )


def qr_kernel(count, stat_ref, basis_ref, out_ref, work):
    tiles = -(-count // PACK)
    rows = PACK * PAN
    panels = BS // PAN

    batch = next(size for size in (8, 6, 4, 3, 2, 1) if count % size == 0)

    def start(step, _):
        ids = [step * batch + c for c in range(batch)]
        stats = [stat_ref[b] for b in ids]
        bases = [basis_ref[b] for b in ids]
        scales = [
            1.0 / jnp.max(jnp.sum(jnp.abs(stat), -1, keepdims=True), 0, keepdims=True)
            for stat in stats
        ]
        xts = [fdot(base, stat, 0, 0) * scale for base, stat, scale in zip(bases, stats, scales)]
        grams = [fdot(xt, xt, 1, 1) for xt in xts]
        for b, xt, gram in zip(ids, xts, grams):
            for p in range(panels):
                work[p, pl.ds(b * PAN, PAN), :BS] = gram[p * PAN : (p + 1) * PAN]
                work[p, pl.ds(b * PAN, PAN), BS:] = xt[p * PAN : (p + 1) * PAN]
        return _

    lax.fori_loop(0, count // batch, start, 0)
    row_id = lax.broadcasted_iota(jnp.int32, (PAN, BS), 0)
    lane_id = lax.broadcasted_iota(jnp.int32, (PAN, BS), 1)
    group = lane_id // PAN
    for p in range(panels):
        packed = []
        for t in range(tiles):
            tile = jnp.zeros((PAN, BS), jnp.float32)
            for c in range(PACK):
                b = t * PACK + c
                if b < count:
                    diag = work[p, b * PAN : (b + 1) * PAN, :BS]
                    shift = (c - p) * PAN % BS
                    if shift:
                        diag = pltpu.roll(diag, shift, 1)
                    tile = jnp.where(group == c, diag, tile)
                else:
                    tile = jnp.where((group == c) & (lane_id % PAN == row_id), 1.0, tile)
            packed.append(tile)
        inverse = [jnp.where(lane_id % PAN == row_id, 1.0, 0.0) for _ in range(tiles)]
        scales = [jnp.ones((PAN, BS), jnp.float32) for _ in range(tiles)]
        for k in range(PAN):
            index = group * PAN + k
            for t in range(tiles):
                tile = packed[t]
                column = jnp.take_along_axis(tile, index, axis=1, mode="promise_in_bounds")
                pivot = column[k : k + 1]
                scales[t] = jnp.where(row_id == k, lax.rsqrt(pivot), scales[t])
                if k < PAN - 1:
                    factor = jnp.where(row_id > k, column * (1.0 / pivot), 0.0)
                    packed[t] = tile - factor * tile[k : k + 1]
                    inverse[t] = inverse[t] - factor * inverse[t][k : k + 1]
        for t in range(tiles):
            low = inverse[t] * scales[t]
            spread = jnp.concatenate([jnp.where(group == c, low, 0.0) for c in range(PACK)], 0)
            here = min(rows, (count - t * PACK) * PAN)
            spread = spread[:here]
            if here < rows:
                spread = spread[:, :here]
            span = slice(t * rows, t * rows + here)
            work[p, span, :] = fdot(spread, work[p, span, :], 1, 0)
        if p < panels - 1:

            def trail(step, _, p=p):
                ids = [step * batch + c for c in range(batch)]
                uppers = [work[p, pl.ds(b * PAN, PAN), :] for b in ids]
                changes = [fdot(upper[:, :BS], upper, 0, 0) for upper in uppers]
                for b, change in zip(ids, changes):
                    for q in range(p + 1, panels):
                        work[q, pl.ds(b * PAN, PAN), :] -= change[q * PAN : (q + 1) * PAN]
                return _

            lax.fori_loop(0, count // batch, trail, 0)

    def finish(b, _):
        rows_q = jnp.concatenate([work[p, pl.ds(b * PAN, PAN), BS:] for p in range(panels)], 0)
        out_ref[b] = rows_q.T
        return _

    lax.fori_loop(0, count, finish, 0, unroll=2)


def renew_all(stats, bases):
    count = stats.shape[0]
    return pl.pallas_call(
        functools.partial(qr_kernel, count),
        out_shape=jax.ShapeDtypeStruct((count, BS, BS), jnp.float32),
        in_specs=[pl.BlockSpec(memory_space=pltpu.VMEM)] * 2,
        out_specs=pl.BlockSpec(memory_space=pltpu.VMEM),
        scratch_shapes=[pltpu.VMEM((BS // PAN, count * PAN, 2 * BS), jnp.float32)],
        name="renew",
    )(stats, bases)


def soap_update(weight, first_moment, second_moment, left, right, left_rot, right_rot, grad):
    left = beta_two * left + (1.0 - beta_two) * jnp.einsum(
        "bij,bkj->bik", grad, grad, precision=HIGHEST
    )
    right = beta_two * right + (1.0 - beta_two) * jnp.einsum(
        "bji,bjk->bik", grad, grad, precision=HIGHEST
    )
    rotated = jnp.einsum("bji,bjk->bik", left_rot, grad, precision=HIGHEST)
    rotated = jnp.einsum("bij,bjk->bik", rotated, right_rot, precision=HIGHEST)
    first_moment = beta_one * first_moment + (1.0 - beta_one) * rotated
    second_moment = beta_two * second_moment + (1.0 - beta_two) * rotated * rotated
    direction = (
        first_moment
        / (1.0 - beta_one**STEP)
        / (jnp.sqrt(second_moment / (1.0 - beta_two**STEP)) + epsilon)
    )
    direction = jnp.einsum("bij,bjk->bik", left_rot, direction, precision=HIGHEST)
    direction = jnp.einsum("bij,bkj->bik", direction, right_rot, precision=HIGHEST)
    weight = weight - learn_rate * (direction + weight_decay * weight)
    count = weight.shape[0]
    renewed = renew_all(
        jnp.concatenate([left, right], 0), jnp.concatenate([left_rot, right_rot], 0)
    )
    return (
        weight,
        first_moment,
        second_moment,
        left,
        right,
        renewed[:count],
        renewed[count:],
    )


def adam_update(weight, first_moment, second_moment, grad, decay_rate, rate):
    first_moment = beta_one * first_moment + (1.0 - beta_one) * grad
    second_moment = beta_two * second_moment + (1.0 - beta_two) * grad * grad
    direction = (
        first_moment
        / (1.0 - beta_one**STEP)
        / (jnp.sqrt(second_moment / (1.0 - beta_two**STEP)) + epsilon)
    )
    return (weight - rate * (direction + decay_rate * weight), first_moment, second_moment)


def shards(
    latents,
    actions,
    game_ids,
    action_masks,
    valid_steps,
    target_bins,
    target_fracs,
    continues,
    owner_order,
    blocks,
    block_first,
    block_second,
    left_stat,
    right_stat,
    left_basis,
    right_basis,
    latent_maps,
    latent_first,
    latent_second,
    head_weights,
    head_first,
    head_second,
    small_params,
    small_first,
    small_second,
    ema_critic,
    dp,
    fsdp,
):
    block_grad, maps_grad, packed_grad, square, sums = model_grads(
        latents, actions, game_ids, action_masks, valid_steps, target_bins, target_fracs, continues,
        owner_order, blocks, latent_maps, head_weights, small_params, dp, fsdp,
    )
    head_grad, small_grad = unpack_heads(packed_grad, small_params.shape[0])
    counted = sums[1]
    loss_value = sums[0] / counted
    grad_norm = jnp.sqrt(square) / counted
    factor = jnp.minimum(1.0, clip_norm / grad_norm) / counted
    soap_out = soap_update(
        blocks,
        block_first,
        block_second,
        left_stat,
        right_stat,
        left_basis,
        right_basis,
        block_grad * factor,
    )
    maps_out = adam_update(
        latent_maps, latent_first, latent_second, maps_grad * factor, weight_decay, learn_rate
    )
    heads_out = adam_update(
        head_weights, head_first, head_second, head_grad * factor, weight_decay, learn_rate
    )
    small_out = adam_update(
        small_params, small_first, small_second, small_grad * factor, 0.0, small_rate
    )
    ema_new = ema_rate * ema_critic + (1.0 - ema_rate) * heads_out[0][:, BINS : 2 * BINS]
    return (
        loss_value,
        grad_norm,
        soap_out[0],
        soap_out[1],
        soap_out[2],
        soap_out[3],
        soap_out[4],
        soap_out[5],
        soap_out[6],
        maps_out[0],
        maps_out[1],
        maps_out[2],
        heads_out[0],
        heads_out[1],
        heads_out[2],
        small_out[0],
        small_out[1],
        small_out[2],
        ema_new,
    )


def solution(mesh):
    placed = (
        P(("dp", "fsdp"), None, None),
        P(("dp", "fsdp"), None),
        P(("dp", "fsdp")),
        P(),
        P(("dp", "fsdp"), None),
        P(("dp", "fsdp"), None, None),
        P(("dp", "fsdp"), None, None),
        P(("dp", "fsdp"), None),
        P(),
        P("fsdp", None, None),
        P("fsdp", None, None),
        P("fsdp", None, None),
        P("fsdp", None, None),
        P("fsdp", None, None),
        P("fsdp", None, None),
        P("fsdp", None, None),
        P("fsdp", None),
        P("fsdp", None),
        P("fsdp", None),
        P(),
        P(),
        P(),
        P(),
        P(),
        P(),
        P(),
    )
    return jax.shard_map(
        functools.partial(shards, dp=mesh.shape["dp"], fsdp=mesh.shape["fsdp"]),
        mesh=mesh,
        in_specs=placed,
        out_specs=(
            P(),
            P(),
            P("fsdp", None, None),
            P("fsdp", None, None),
            P("fsdp", None, None),
            P("fsdp", None, None),
            P("fsdp", None, None),
            P("fsdp", None, None),
            P("fsdp", None, None),
            P("fsdp", None),
            P("fsdp", None),
            P("fsdp", None),
            P(),
            P(),
            P(),
            P(),
            P(),
            P(),
            P(),
        ),
        check_vma=False,
    )
```

```python
import functools
import math

import jax
import jax.numpy as jnp
from jax import lax
from jax.experimental import pallas as pl
from jax.experimental.pallas import tpu as pltpu
from jax.sharding import PartitionSpec as P

D = 512
NH = 8
DH = 64
FF = 2048
GROUPS = 32
CLASSES = 32
LAT = 1024
BINS = 255
NA = 18
LAYERS = 1
F = 64
NGAME = 26
BS = 128
STEP = 10
PAN = 16
PACK = 8
HEAD_COLS = 640
PACK_ROWS = 3072
MAP_CHUNKS = ((0, 1), (2,), (3,))
PART_ROWS = (384, 368, 368)
TM = 256
GELU_A = math.sqrt(2.0 / math.pi)
GELU_B = 0.044715


HIGHEST = lax.Precision.HIGHEST
beta_one = 0.9
beta_two = 0.99
epsilon = 1e-08
learn_rate = 0.03
small_rate = 0.15
weight_decay = 0.01
clip_norm = 0.05
ema_rate = 0.98
norm_eps = 1e-05


def positions(frames, width):
    frame_index = jnp.arange(frames).astype(jnp.float32)[:, None]
    feature = jnp.arange(width)
    freq = jnp.exp(-(feature // 2 * 2).astype(jnp.float32) * (math.log(10000.0) / width))
    angle = frame_index * freq[None, :]
    return jnp.where(feature % 2 == 0, jnp.sin(angle), jnp.cos(angle))


def halves(size):
    return [1 << bit for bit in reversed(range(size.bit_length() - 1))]


def swap(value, axis, size, bit):
    return lax.ppermute(value, axis, [(i, i ^ bit) for i in range(size)])


def part_orders(dp, fsdp):
    core, tall = [("dp", dp, bit) for bit in reversed(halves(dp))]
    deep, near, side = [("fsdp", fsdp, bit) for bit in halves(fsdp)]
    return (
        (core, tall, side, near, deep),
        (core, side, near, deep, tall),
        (core, near, tall, side, deep),
    )


def order_index(order, dp_here, fsdp_here):
    dp_index = jnp.zeros((), jnp.int32)
    fsdp_index = jnp.zeros((), jnp.int32)
    spot = jnp.arange(1 << len(order))
    for place, (axis, _, bit) in enumerate(order):
        flag = (spot >> (len(order) - 1 - place)) & 1
        if axis == "dp":
            dp_index = dp_index + flag * bit
        else:
            fsdp_index = fsdp_index + flag * bit
    return dp_index ^ dp_here, fsdp_index ^ fsdp_here


def scatter_sum(held, sent, order, wide_stages):
    for place, (axis, size, bit) in enumerate(order):
        got = swap(sent, axis, size, bit)
        held = held + got.astype(jnp.float32)
        half = held.shape[0] // 2
        if half:
            held, sent = held[:half], held[half:]
            if place + 1 < len(order) - wide_stages:
                sent = sent.astype(jnp.bfloat16)
    return held[0]


def gather_doubling(value, order):
    held = value[None]
    for axis, size, bit in reversed(order):
        held = jnp.concatenate([held, swap(held, axis, size, bit)], 0)
    return held


def inverse_place(order, dp, fsdp, dp_here, fsdp_here):
    dp_id = jnp.arange(dp)[None, :] ^ dp_here
    fsdp_id = jnp.arange(fsdp)[:, None] ^ fsdp_here
    spot = jnp.zeros((fsdp, dp), jnp.int32)
    for place, (axis, _, bit) in enumerate(order):
        source = dp_id if axis == "dp" else fsdp_id
        flag = (source & bit) // bit
        spot = spot + flag * (1 << (len(order) - 1 - place))
    return spot


def placed_units(dp, fsdp):
    dp_here = lax.axis_index("dp")
    fsdp_here = lax.axis_index("fsdp")
    units = []
    spots = []
    for order in part_orders(dp, fsdp):
        dp_index, fsdp_index = order_index(order, dp_here, fsdp_here)
        units.append(fsdp_index * dp + dp_index)
        spots.append(inverse_place(order, dp, fsdp, dp_here, fsdp_here).reshape(-1))
    return jnp.stack(units), jnp.stack(spots)


def gathered_pieces(blocks_low, maps_low, ready, dp, fsdp):
    dp_here = lax.axis_index("dp")
    quarter = blocks_low.shape[0] // dp
    piece_rows = maps_low.shape[0] // dp
    own_blocks = lax.dynamic_slice_in_dim(blocks_low, dp_here * quarter, quarter, 0)
    own_maps = lax.dynamic_slice_in_dim(maps_low, dp_here * piece_rows, piece_rows, 0)
    pieces = []
    for part, order in enumerate(part_orders(dp, fsdp)):
        piece = jnp.concatenate(
            [own_blocks[2 * part], own_blocks[2 * part + 1]]
            + [own_maps[:, c * BS : (c + 1) * BS] for c in MAP_CHUNKS[part]],
            0,
        )
        held = gather_doubling(piece, order[2:])
        pieces.append([held, swap(held, *order[1])])
    pieces[-1][1], ready = lax.optimization_barrier((pieces[-1][1], ready))
    return [
        piece
        for both, order in zip(pieces, part_orders(dp, fsdp))
        for piece in both + [swap(piece, *order[0]) for piece in both]
    ], ready


def reduced_grads(outs, sums, slots, map_rows, dp, fsdp):
    if (dp, fsdp) != (4, 8):
        both = ("dp", "fsdp")
        block_grad = lax.psum(
            lax.psum_scatter(outs[0], "fsdp", scatter_dimension=0, tiled=True), "dp"
        )
        maps_grad = lax.psum(
            lax.psum_scatter(outs[1], "fsdp", scatter_dimension=0, tiled=True), "dp"
        )
        heads = lax.psum(outs[2], both)
        sums = lax.psum(sums, both)
        held = lax.psum(jnp.sum(block_grad * block_grad) + jnp.sum(maps_grad * maps_grad), "fsdp")
        return block_grad, maps_grad, heads, held + jnp.sum(heads * heads), sums
    dp_here = lax.axis_index("dp")
    fsdp_here = lax.axis_index("fsdp")
    parts = [
        scatter_sum(outs[2 * part], outs[2 * part + 1], order, 2)
        for part, order in enumerate(part_orders(dp, fsdp))
    ]
    cut = 2 * BS
    own_blocks = jnp.concatenate([part[:cut] for part in parts], 0)
    own_maps = jnp.concatenate([parts[0][cut:], parts[1][cut : cut + 64], parts[2][cut : cut + 64]], 0)
    own_heads = jnp.concatenate([parts[1][cut + 64 :], parts[2][cut + 64 :]], 0)
    own_square = sum(jnp.sum(part * part) for part in parts)
    totals = jnp.concatenate([sums, own_square[None]])
    totals = jnp.pad(totals[None], ((0, 7), (0, BS - totals.shape[0])))
    own_heads = jnp.concatenate([own_heads, totals], 0)
    dp_order = [("dp", dp, bit) for bit in reversed(halves(dp))]
    spot = inverse_place(dp_order, dp, 1, dp_here, 0).reshape(-1)
    shard = gather_doubling(jnp.concatenate([own_blocks, own_maps], 0), dp_order)
    shard = shard[spot]
    count = slots // dp * BS
    piece_rows = map_rows // dp
    block_grad = shard[:, :count].reshape(slots, BS, BS)
    maps_grad = (
        shard[:, count:]
        .reshape(dp, D // BS, piece_rows, BS)
        .transpose(0, 2, 1, 3)
        .reshape(map_rows, D)
    )
    core, tall, side, near, deep = part_orders(dp, fsdp)[0]
    full_order = (core, deep, side, near, tall)
    all_heads = gather_doubling(own_heads, full_order)
    spot = inverse_place(full_order, dp, fsdp, dp_here, fsdp_here).reshape(-1)
    all_heads = all_heads[spot]
    sums = jnp.sum(all_heads[:, -8, :3], 0)
    return block_grad, maps_grad, all_heads[:, :-8].reshape(-1, BS), sums[-1], sums[:-1]


def norm_rows(inputs, gain_row, bias_row):
    center = inputs - jnp.mean(inputs, -1, keepdims=True)
    rstd = lax.rsqrt(jnp.mean(center * center, -1, keepdims=True) + norm_eps)
    scaled = center * rstd
    return scaled * gain_row + bias_row, scaled, rstd


def norm_rows_back(grad_out, scaled, rstd, gain_row):
    grad_scaled = grad_out * gain_row
    return rstd * (
        grad_scaled
        - jnp.mean(grad_scaled, -1, keepdims=True)
        - scaled * jnp.mean(grad_scaled * scaled, -1, keepdims=True)
    )


def dot32(left, right, ca, cb):
    return lax.dot_general(
        left, right, (((ca,), (cb,)), ((), ())), preferred_element_type=jnp.float32
    )


def model_kernel(fast, rows_of, *refs):
    refs = list(refs)
    take = lambda count: [refs.pop(0) for _ in range(count)]
    (owner, units, block_place, unit_place) = take(4)
    sources = take(12 if fast else 2)
    (hot, target, later_row, base, facts, legal, next_hot, act_hot, gains, head_w, head_b) = take(11)
    outs = take(6 if fast else 3)
    (sums_out,) = take(1)
    (wall, maps) = take(2)
    (normed1, qkv, probs, mixed, normed2, slope, act, final, grad_dyn, grad_head) = take(10)
    (grad_low, grad_pre, grad_mid, grad_qkv, grad_hid, small, bias_sum) = take(7)
    if fast:
        keep, send = take(2)
    wall_sem, maps_sem, out_sem = take(3)
    tokens = base.shape[0]
    tile = D // BS
    wide = FF // BS
    out_at = 3 * tile * tile
    expand_at = out_at + tile * tile
    contract_at = expand_at + tile * wide

    if fast:
        for part in range(3):
            for piece in range(4):
                source = sources[part * 4 + piece]

                def fetch(j, carry, part=part, piece=piece, source=source):
                    unit = units[part * 32 + piece * 8 + j]
                    for k in range(2):
                        block = owner[unit * 6 + part * 2 + k]
                        pltpu.make_async_copy(
                            source.at[j, k * BS : (k + 1) * BS, :], wall.at[block], wall_sem
                        ).start()
                    for i, chunk in enumerate(MAP_CHUNKS[part]):
                        pltpu.make_async_copy(
                            source.at[j, 2 * BS + i * 64 : 2 * BS + (i + 1) * 64, :],
                            maps.at[
                                pl.ds(pl.multiple_of(unit * 64, 64), 64),
                                chunk * BS : (chunk + 1) * BS,
                            ],
                            maps_sem,
                        ).start()
                    return carry

                lax.fori_loop(0, 8, fetch, 0)
    else:

        def fetch(j, carry):
            pltpu.make_async_copy(sources[0].at[j], wall.at[owner[j]], wall_sem).start()
            return carry

        lax.fori_loop(0, wall.shape[0], fetch, 0)
        pltpu.make_async_copy(sources[1], maps, maps_sem).start()
    small[...] = jnp.zeros_like(small)
    bias_sum[...] = jnp.zeros_like(bias_sum)
    sums_out[...] = jnp.zeros_like(sums_out)
    pltpu.make_async_copy(wall, wall, wall_sem).wait()
    pltpu.make_async_copy(maps, maps, maps_sem).wait()

    def grid_of(start, stride, row_count, col_count):
        return jnp.concatenate(
            [
                jnp.concatenate([wall[start + r * stride + c] for c in range(col_count)], 1)
                for r in range(row_count)
            ],
            0,
        )

    def chunk(step, carry):
        rows = pl.ds(pl.multiple_of(step * TM, TM), TM)
        hidden = dot32(hot[:, rows], maps[:LAT, :], 0, 0) + base[rows, :]
        normed, scaled1, rstd1 = norm_rows(hidden, gains[0:1], gains[1:2])
        normed1[rows, :] = normed.astype(jnp.bfloat16)

        def joint_strip(s, c):
            cols = pl.ds(pl.multiple_of(s * 256, 256), 256)
            weight = grid_of(2 * s, 3 * tile, tile, 2)
            qkv[rows, cols] = dot32(normed1[rows, :], weight, 1, 0).astype(jnp.bfloat16)
            return c

        lax.fori_loop(0, 6, joint_strip, 0)
        lane = lax.broadcasted_iota(jnp.int32, (BS, BS), 1)
        line = lax.broadcasted_iota(jnp.int32, (BS, BS), 0)
        allowed = (line >= lane) & (line // F == lane // F)
        low_half = lane < DH
        halves_of = [mask.astype(jnp.float32).astype(jnp.bfloat16) for mask in (low_half, ~low_half)]

        def attend(s, c):
            sub = pl.ds(pl.multiple_of(step * TM + s * BS, BS), BS)
            for pair in range(NH // 2):
                spans = [slice(part * D + pair * BS, part * D + (pair + 1) * BS) for part in range(3)]
                query, key, value = [qkv[sub, span] for span in spans]
                mixes = []
                for side in range(2):
                    half = halves_of[side]
                    scores = dot32(query * half, key, 1, 1) * DH ** (-0.5)
                    scores = jnp.where(allowed, scores, -1e30)
                    shifted = scores - jnp.max(scores, -1, keepdims=True)
                    power = jnp.exp(shifted)
                    prob = power / jnp.sum(power, -1, keepdims=True)
                    probs[2 * pair + side, sub, :] = prob
                    mixes.append(dot32(prob.astype(jnp.bfloat16), value, 1, 0))
                mixed[sub, pair * BS : (pair + 1) * BS] = jnp.where(low_half, *mixes).astype(
                    jnp.bfloat16
                )
            return c

        lax.fori_loop(0, TM // BS, attend, 0)
        out_map = grid_of(out_at, tile, tile, tile)
        middle = hidden + dot32(mixed[rows, :], out_map, 1, 0)
        normed, scaled2, rstd2 = norm_rows(middle, gains[2:3], gains[3:4])
        normed2[rows, :] = normed.astype(jnp.bfloat16)

        def expand_strip(s, c):
            cols = pl.ds(pl.multiple_of(s * 256, 256), 256)
            weight = grid_of(expand_at + 2 * s, wide, tile, 2)
            pre = dot32(normed2[rows, :], weight, 1, 0)
            square = pre * pre
            curve = jnp.tanh(GELU_A * (pre + GELU_B * (square * pre)))
            act[rows, cols] = (0.5 * pre * (1.0 + curve)).astype(jnp.bfloat16)
            slope[:, cols] = 0.5 * (1.0 + curve) + 0.5 * pre * (1.0 - curve * curve) * (
                GELU_A * (1.0 + 3.0 * GELU_B * square)
            )
            return c

        lax.fori_loop(0, FF // 256, expand_strip, 0)

        def contract_strip(s, total):
            cols = pl.ds(pl.multiple_of(s * 512, 512), 512)
            weight = grid_of(contract_at + s * 4 * tile, tile, 4, tile)
            return total + dot32(act[rows, cols], weight, 1, 0)

        top = lax.fori_loop(0, FF // 512, contract_strip, middle)
        normed, scaled3, rstd3 = norm_rows(top, gains[4:5], gains[5:6])
        final[rows, :] = normed.astype(jnp.bfloat16)
        late = later_row[0:1, rows]

        def dyn_strip(s, total):
            span = pl.ds(pl.multiple_of(s * 256, 256), 256)
            below = pl.ds(pl.multiple_of(LAT + s * 256, 256), 256)
            logits = dot32(maps[below, :], final[rows, :], 1, 1)
            logits = logits.reshape(256 // CLASSES, CLASSES, TM)
            shifted = logits - jnp.max(logits, 1, keepdims=True)
            power = jnp.exp(shifted)
            norm = jnp.sum(power, 1, keepdims=True)
            wanted = target[span, rows].astype(jnp.float32).reshape(256 // CLASSES, CLASSES, TM)
            spent = jnp.sum(wanted * (jnp.log(norm) - shifted), 0)
            grad = (power / norm - wanted) * late[None]
            grad_dyn[span, rows] = grad.reshape(256, TM).astype(jnp.bfloat16)
            return total + jnp.sum(spent, 0, keepdims=True) * late

        dyn_loss = lax.fori_loop(0, LAT // 256, dyn_strip, jnp.zeros((1, TM), jnp.float32))
        heads = dot32(final[rows, :], head_w[...], 1, 0) + head_b[0:1]
        now = facts[rows, 0:1]
        late_col = facts[rows, 1:2]
        spot = lax.broadcasted_iota(jnp.int32, (TM, 256), 1).astype(jnp.float32)
        frame_loss = jnp.zeros((TM, 1), jnp.float32)
        for which in range(2):
            logits = heads[:, which * 256 : (which + 1) * 256]
            bin_low = facts[rows, 2 + which : 3 + which]
            upper = facts[rows, 4 + which : 5 + which]
            weights = jnp.where(spot == bin_low, 1.0 - upper, 0.0)
            weights = weights + jnp.where(spot == bin_low + 1.0, upper, 0.0)
            shifted = logits - jnp.max(logits, -1, keepdims=True)
            power = jnp.exp(shifted)
            norm = jnp.sum(power, -1, keepdims=True)
            frame_loss = frame_loss + jnp.sum(
                weights * jnp.where(weights > 0.0, jnp.log(norm) - shifted, 0.0), -1, keepdims=True
            )
            grad = (power / norm - weights) * now
            grad_head[rows, which * 256 : (which + 1) * 256] = grad.astype(jnp.bfloat16)
            bias_sum[0:1, which * 256 : (which + 1) * 256] += jnp.sum(
                grad.astype(jnp.bfloat16).astype(jnp.float32), 0, keepdims=True
            )
        tail = heads[:, 512:640]
        logit = tail[:, 0:1]
        goal = facts[rows, 6:7]
        soft = jnp.maximum(logit, 0.0) + jnp.log1p(jnp.exp(-jnp.abs(logit)))
        frame_loss = (frame_loss + soft - goal * logit) * now
        may = legal[rows, :]
        chosen = next_hot[rows, :]
        masked = jnp.where(may > 0.5, tail, -1e30)
        shifted = masked - jnp.max(masked, -1, keepdims=True)
        power = jnp.exp(shifted)
        norm = jnp.sum(power, -1, keepdims=True)
        actor = jnp.sum(
            jnp.where(chosen > 0.5, jnp.log(norm) - shifted, 0.0), -1, keepdims=True
        )
        frame_loss = frame_loss + actor * late_col
        grad = (power / norm - chosen) * late_col
        column = lax.broadcasted_iota(jnp.int32, (TM, BS), 1)
        grad = jnp.where(column == 0, (jax.nn.sigmoid(logit) - goal) * now, grad)
        grad_head[rows, 512:640] = grad.astype(jnp.bfloat16)
        bias_sum[0:1, 512:640] += jnp.sum(
            grad.astype(jnp.bfloat16).astype(jnp.float32), 0, keepdims=True
        )
        sums_out[0:1, :] += jnp.broadcast_to(
            jnp.sum(dyn_loss, -1, keepdims=True) + jnp.sum(frame_loss, 0, keepdims=True), (1, BS)
        )
        sums_out[1:2, :] += jnp.broadcast_to(jnp.sum(now, 0, keepdims=True), (1, BS))

        grad_final = dot32(grad_dyn[:, rows], maps[LAT:, :], 0, 0) + dot32(
            grad_head[rows, :], head_w[...], 1, 1
        )
        small[4:5, :] += jnp.sum(grad_final * scaled3, 0, keepdims=True)
        small[5:6, :] += jnp.sum(grad_final, 0, keepdims=True)
        grad_top = norm_rows_back(grad_final, scaled3, rstd3, gains[4:5])
        grad_low[rows, :] = grad_top.astype(jnp.bfloat16)

        def act_strip(s, total):
            cols = pl.ds(pl.multiple_of(s * 256, 256), 256)
            weight = grid_of(contract_at + s * 2 * tile, tile, 2, tile)
            grad = dot32(grad_low[rows, :], weight, 1, 1) * slope[:, cols]
            grad = grad.astype(jnp.bfloat16)
            grad_pre[rows, cols] = grad
            weight = grid_of(expand_at + 2 * s, wide, tile, 2)
            return total + dot32(grad, weight, 1, 1)

        grad_normed = lax.fori_loop(
            0, FF // 256, act_strip, jnp.zeros((TM, D), jnp.float32)
        )
        small[2:3, :] += jnp.sum(grad_normed * scaled2, 0, keepdims=True)
        small[3:4, :] += jnp.sum(grad_normed, 0, keepdims=True)
        grad_middle = grad_top + norm_rows_back(grad_normed, scaled2, rstd2, gains[2:3])
        grad_mid[rows, :] = grad_middle.astype(jnp.bfloat16)
        out_map = grid_of(out_at, tile, tile, tile)
        mixed_grad = dot32(grad_mid[rows, :], out_map, 1, 1).astype(jnp.bfloat16)
        grad_hid[rows, :] = mixed_grad

        def attend_back(s, c):
            sub = pl.ds(pl.multiple_of(step * TM + s * BS, BS), BS)
            for pair in range(NH // 2):
                spans = [slice(part * D + pair * BS, part * D + (pair + 1) * BS) for part in range(3)]
                query, key, value = [qkv[sub, span] for span in spans]
                grad_out = grad_hid[sub, pair * BS : (pair + 1) * BS]
                totals = [jnp.zeros((BS, BS), jnp.float32) for _ in range(3)]
                for side in range(2):
                    half = halves_of[side]
                    prob = probs[2 * pair + side, sub, :]
                    out_half = grad_out * half
                    grad_prob = dot32(out_half, value, 1, 1)
                    dots = jnp.sum(grad_prob * prob, -1, keepdims=True)
                    grad_score = (prob * (grad_prob - dots)).astype(jnp.bfloat16)
                    totals[0] += dot32(grad_score, key * half, 1, 0)
                    totals[1] += dot32(grad_score, query * half, 0, 0)
                    totals[2] += dot32(prob.astype(jnp.bfloat16), out_half, 0, 0)
                for part, (span, total) in enumerate(zip(spans, totals)):
                    scale = DH ** (-0.5) if part < 2 else 1.0
                    grad_qkv[sub, span] = (total * scale).astype(jnp.bfloat16)
            return c

        lax.fori_loop(0, TM // BS, attend_back, 0)

        def joint_back(s, total):
            cols = pl.ds(pl.multiple_of(s * 512, 512), 512)
            weight = grid_of(4 * s, 3 * tile, tile, 4)
            return total + dot32(grad_qkv[rows, cols], weight, 1, 1)

        grad_normed = lax.fori_loop(0, 3, joint_back, jnp.zeros((TM, D), jnp.float32))
        small[0:1, :] += jnp.sum(grad_normed * scaled1, 0, keepdims=True)
        small[1:2, :] += jnp.sum(grad_normed, 0, keepdims=True)
        grad_in = grad_middle + norm_rows_back(grad_normed, scaled1, rstd1, gains[0:1])
        grad_hid[rows, :] = grad_in.astype(jnp.bfloat16)
        pieces = thirds(grad_in)
        small[...] += sum(dot32(act_hot[:, rows], piece, 1, 0) for piece in pieces)
        return carry

    lax.fori_loop(0, tokens // TM, chunk, 0)

    def put(place, rows, first, value):
        part = (place >> 8) & 3
        spot = place & 15
        dest = pl.ds(first, rows)

        @pl.when(((place >> 4) & 1) == 0)
        def _():
            keep[part, spot, dest, :] = value

        @pl.when(((place >> 4) & 1) == 1)
        def _():
            send[part, spot, dest, :] = value.astype(jnp.bfloat16)

    def put_block(block, value):
        place = block_place[block]
        if fast:
            put(place, BS, pl.multiple_of(((place >> 10) & 1) * BS, BS), value)
        else:
            outs[0][place] = value

    def block_grads(start, stride, left, right, row_count, col_steps):
        def strip(s, c):
            cols = pl.ds(pl.multiple_of(s * 256, 256), 256)
            grads = dot32(left, right[:, cols], 0, 0)
            for r in range(row_count):
                for k in range(2):
                    put_block(
                        start + r * stride + 2 * s + k,
                        grads[r * BS : (r + 1) * BS, k * BS : (k + 1) * BS],
                    )
            return c

        lax.fori_loop(0, col_steps, strip, 0)

    block_grads(0, 3 * tile, normed1[...], grad_qkv, tile, 6)
    block_grads(out_at, tile, mixed[...], grad_mid, tile, 2)
    block_grads(expand_at, wide, normed2[...], grad_pre, tile, FF // 256)

    def contract_rows(m, c):
        cols = pl.ds(pl.multiple_of(m * D, D), D)
        for s in range(2):
            grads = dot32(act[:, cols], grad_low[:, s * 256 : (s + 1) * 256], 0, 0)
            for r in range(tile):
                for k in range(2):
                    put_block(
                        contract_at + (m * tile + r) * tile + 2 * s + k,
                        grads[r * BS : (r + 1) * BS, k * BS : (k + 1) * BS],
                    )
        return c

    lax.fori_loop(0, FF // D, contract_rows, 0)

    def map_rows(m, c):
        span = pl.ds(pl.multiple_of(m * 256, 256), 256)
        for table in range(2):
            source, other = ((hot, grad_hid), (grad_dyn, final))[table]
            grads = dot32(source[span, :], other[...], 1, 0)
            if not fast:
                outs[1][pl.ds(pl.multiple_of(table * LAT + m * 256, 256), 256), :] = grads
                continue
            for u in range(4):
                unit = table * (LAT // 64) + m * 4 + u
                for part in range(3):
                    place = unit_place[part * 32 + unit]
                    for i, piece in enumerate(MAP_CHUNKS[part]):
                        put(
                            place,
                            64,
                            2 * BS + i * 64,
                            grads[u * 64 : (u + 1) * 64, piece * BS : (piece + 1) * BS],
                        )
        return c

    lax.fori_loop(0, LAT // 256, map_rows, 0)
    pieces = []
    for c in range(5):
        pieces.append(dot32(final[...], grad_head[:, c * BS : (c + 1) * BS], 0, 0))
    packed = jnp.concatenate(
        pieces
        + [
            bias_sum[0:1, c * BS : (c + 1) * BS] if c < 5 else jnp.zeros((3, BS), jnp.float32)
            for c in range(6)
        ]
        + [small[:, c * BS : (c + 1) * BS] for c in range(tile)]
        + [jnp.zeros((PACK_ROWS - 5 * D - 8 - tile * small.shape[0], BS), jnp.float32)],
        0,
    )
    if not fast:
        outs[2][...] = packed
        return
    for unit in range(32):
        for half in range(2):
            part = 1 + half
            place = unit_place[part * 32 + unit]
            first = unit * 96 + half * 48
            put(place, 48, 2 * BS + 64, packed[first : first + 48])
    copies = []
    for part in range(3):
        for which, scratch in enumerate((keep, send)):
            copies.append(
                pltpu.make_async_copy(
                    scratch.at[part, :, 0 : rows_of[part], :],
                    outs[part * 2 + which],
                    out_sem.at[part * 2 + which],
                )
            )
    for copy in copies:
        copy.start()
    for copy in copies:
        copy.wait()


def spread_cols(head):
    gap = jnp.zeros((head.shape[0], 1), head.dtype)
    rest = jnp.zeros((head.shape[0], BS - 1 - NA), head.dtype)
    return jnp.concatenate(
        [head[:, :BINS], gap, head[:, BINS : 2 * BINS], gap, head[:, 2 * BINS :], rest], 1
    )


def unpack_heads(packed, small_rows):
    chunks = [packed[c * D : (c + 1) * D] for c in range(5)]
    bias = jnp.concatenate([packed[5 * D + c : 5 * D + c + 1] for c in range(5)], 1)
    head = jnp.concatenate([jnp.concatenate(chunks, 1), bias], 0)
    head = jnp.concatenate(
        [head[:, :BINS], head[:, 256 : 256 + BINS], head[:, 512 : 513 + NA]], 1
    )
    start = 5 * D + 8
    small = jnp.concatenate(
        [packed[start + c * small_rows : start + (c + 1) * small_rows] for c in range(D // BS)], 1
    )
    return head, small


def model_grads(
    latents, actions, game_ids, action_masks, valid_steps, target_bins, target_fracs, continues,
    owner_order, blocks, latent_maps, head_weights, small_params, dp, fsdp,
):
    fast = (dp, fsdp) == (4, 8)
    seqs_here = latents.shape[0]
    tokens = seqs_here * F
    blocks_low = blocks.astype(jnp.bfloat16)
    maps_low = latent_maps.astype(jnp.bfloat16)
    slot_ids = jnp.arange(owner_order.shape[0], dtype=jnp.int32)
    inverse = jnp.sum(jnp.where(owner_order[None, :] == slot_ids[:, None], slot_ids[None, :], 0), 1)
    if fast:
        units, spots = placed_units(dp, fsdp)
        part_ids = jnp.arange(3)[:, None]
        unit_place = (part_ids << 8) + spots
        slot_unit = inverse // 6
        slot_part = inverse % 6 // 2
        block_place = ((inverse % 2) << 10) + unit_place.reshape(-1)[slot_part * (dp * fsdp) + slot_unit]
        units = units.reshape(-1).astype(jnp.int32)
        unit_place = unit_place.reshape(-1).astype(jnp.int32)
        block_place = block_place.astype(jnp.int32)
    else:
        sources = [
            lax.all_gather(blocks_low, "fsdp", axis=0, tiled=True),
            lax.all_gather(maps_low, "fsdp", axis=0, tiled=True),
        ]
        units = unit_place = jnp.zeros((96,), jnp.int32)
        block_place = inverse
    class_ids = jnp.arange(CLASSES)[None, :, None]

    def one_hot_rows(values):
        rows = values.reshape(tokens, GROUPS).T
        return (rows[:, None, :] == class_ids).astype(jnp.bfloat16).reshape(LAT, tokens)

    frame_last = (jnp.arange(F) < F - 1).astype(jnp.float32)[None, :]
    later = (jnp.roll(valid_steps, -1, axis=1).astype(jnp.float32) * frame_last).reshape(tokens)
    now = valid_steps.astype(jnp.float32).reshape(tokens)
    action_hot = (actions.reshape(tokens, 1) == jnp.arange(NA)[None, :]).astype(jnp.float32)
    base = jnp.dot(action_hot, small_params[4 * LAYERS + 2 :], precision=HIGHEST)
    base = (base.reshape(seqs_here, F, D) + positions(F, D)[None]).reshape(tokens, D)
    facts = jnp.concatenate(
        [
            now[:, None],
            later[:, None],
            target_bins.reshape(tokens, 2).astype(jnp.float32),
            target_fracs.reshape(tokens, 2),
            continues.reshape(tokens, 1).astype(jnp.float32),
            jnp.zeros((tokens, BS - 7), jnp.float32),
        ],
        1,
    )
    game_hot = (game_ids[:, None] == jnp.arange(NGAME)[None, :]).astype(jnp.float32)
    legal_rows = jnp.dot(game_hot, action_masks.astype(jnp.float32), precision=HIGHEST)
    legal = jnp.broadcast_to(legal_rows[:, None, :], (seqs_here, F, NA)).reshape(tokens, NA)
    legal = jnp.pad(legal, ((0, 0), (1, BS - 1 - NA)))
    next_hot = (
        jnp.roll(actions, -1, axis=1).reshape(tokens, 1) == jnp.arange(BS)[None, :] - 1
    ).astype(jnp.float32)
    small_rows = small_params.shape[0]
    act_hot = (
        jnp.arange(small_rows)[:, None] - (4 * LAYERS + 2) == actions.reshape(1, tokens)
    ).astype(jnp.bfloat16)
    gains = jnp.pad(small_params[: 4 * LAYERS + 2], ((0, 2), (0, 0)))
    head_wide = spread_cols(head_weights[:D].astype(jnp.bfloat16))
    column = jnp.arange(HEAD_COLS)[None, :]
    head_bias = jnp.where(
        (column == BINS) | (column == 256 + BINS), -1e30, spread_cols(head_weights[D:])
    )
    vmem = pl.BlockSpec(memory_space=pltpu.VMEM)
    smem = pl.BlockSpec(memory_space=pltpu.SMEM)
    away = pl.BlockSpec(memory_space=pl.ANY)
    low = jnp.bfloat16
    wide_type = jnp.float32
    if fast:
        shapes = []
        for rows in PART_ROWS:
            shapes += [((16, rows, BS), wide_type), ((16, rows, BS), low)]
        out_specs = [away] * 6 + [vmem]
    else:
        shapes = [
            (( 192, BS, BS), wide_type), ((2 * LAT, D), wide_type), ((PACK_ROWS, BS), wide_type)
        ]
        out_specs = [vmem] * 4
    shapes.append(((8, BS), wide_type))
    scratch = [
        pltpu.VMEM((owner_order.shape[0], BS, BS), low),
        pltpu.VMEM((2 * LAT, D), low),
        pltpu.VMEM((tokens, D), low),
        pltpu.VMEM((tokens, 3 * D), low),
        pltpu.VMEM((NH, tokens, BS), wide_type),
        pltpu.VMEM((tokens, D), low),
        pltpu.VMEM((tokens, D), low),
        pltpu.VMEM((TM, FF), wide_type),
        pltpu.VMEM((tokens, FF), low),
        pltpu.VMEM((tokens, D), low),
        pltpu.VMEM((LAT, tokens), low),
        pltpu.VMEM((tokens, HEAD_COLS), low),
        pltpu.VMEM((tokens, D), low),
        pltpu.VMEM((tokens, FF), low),
        pltpu.VMEM((tokens, D), low),
        pltpu.VMEM((tokens, 3 * D), low),
        pltpu.VMEM((tokens, D), low),
        pltpu.VMEM((small_rows, D), wide_type),
        pltpu.VMEM((8, HEAD_COLS), wide_type),
    ]
    if fast:
        scratch += [
            pltpu.VMEM((3, 16, PART_ROWS[0], BS), wide_type),
            pltpu.VMEM((3, 16, PART_ROWS[0], BS), low),
        ]
    scratch += [
        pltpu.SemaphoreType.DMA,
        pltpu.SemaphoreType.DMA,
        pltpu.SemaphoreType.DMA((6,)),
    ]
    inputs = (
        owner_order, units, block_place, unit_place,
        one_hot_rows(latents), one_hot_rows(jnp.roll(latents, -1, axis=1)),
        jnp.broadcast_to(later[None], (8, tokens)), base, facts, legal, next_hot, act_hot, gains,
        head_wide, jnp.broadcast_to(head_bias, (8, HEAD_COLS)),
    )
    if fast:
        sources, inputs = gathered_pieces(blocks_low, maps_low, inputs, dp, fsdp)
    *outs, sums = pl.pallas_call(
        functools.partial(model_kernel, fast, PART_ROWS),
        out_shape=[jax.ShapeDtypeStruct(shape, kind) for shape, kind in shapes],
        in_specs=[smem] * 4 + [away] * len(sources) + [vmem] * 11,
        out_specs=out_specs,
        scratch_shapes=scratch,
        compiler_params=pltpu.CompilerParams(vmem_limit_bytes=66 * 1000 * 1000),
        name="model",
    )(*inputs[:4], *sources, *inputs[4:])
    return reduced_grads(outs, sums[:2, 0], blocks.shape[0], latent_maps.shape[0], dp, fsdp)


def thirds(value):
    first = value.astype(jnp.bfloat16)
    rest = value - first.astype(jnp.float32)
    second = rest.astype(jnp.bfloat16)
    third = (rest - second.astype(jnp.float32)).astype(jnp.bfloat16)
    return first, second, third


def stack_left(value, axis):
    a, b, c = thirds(value)
    return jnp.concatenate([a, a, b, a, b, c], axis)


def stack_right(value, axis):
    a, b, c = thirds(value)
    return jnp.concatenate([a, b, a, c, b, a], axis)


def fdot(left, right, ca, cb):
    return lax.dot_general(
        stack_left(left, ca),
        stack_right(right, cb),
        (((ca,), (cb,)), ((), ())),
        preferred_element_type=jnp.float32,
    )


def qr_kernel(count, stat_ref, basis_ref, out_ref, work):
    tiles = -(-count // PACK)
    rows = PACK * PAN
    panels = BS // PAN

    batch = next(size for size in (8, 6, 4, 3, 2, 1) if count % size == 0)

    def start(step, _):
        ids = [step * batch + c for c in range(batch)]
        stats = [stat_ref[b] for b in ids]
        bases = [basis_ref[b] for b in ids]
        scales = [
            1.0 / jnp.max(jnp.sum(jnp.abs(stat), -1, keepdims=True), 0, keepdims=True)
            for stat in stats
        ]
        xts = [fdot(base, stat, 0, 0) * scale for base, stat, scale in zip(bases, stats, scales)]
        grams = [fdot(xt, xt, 1, 1) for xt in xts]
        for b, xt, gram in zip(ids, xts, grams):
            for p in range(panels):
                work[p, pl.ds(b * PAN, PAN), :BS] = gram[p * PAN : (p + 1) * PAN]
                work[p, pl.ds(b * PAN, PAN), BS:] = xt[p * PAN : (p + 1) * PAN]
        return _

    lax.fori_loop(0, count // batch, start, 0)
    row_id = lax.broadcasted_iota(jnp.int32, (PAN, BS), 0)
    lane_id = lax.broadcasted_iota(jnp.int32, (PAN, BS), 1)
    group = lane_id // PAN
    for p in range(panels):
        packed = []
        for t in range(tiles):
            tile = jnp.zeros((PAN, BS), jnp.float32)
            for c in range(PACK):
                b = t * PACK + c
                if b < count:
                    diag = work[p, b * PAN : (b + 1) * PAN, :BS]
                    shift = (c - p) * PAN % BS
                    if shift:
                        diag = pltpu.roll(diag, shift, 1)
                    tile = jnp.where(group == c, diag, tile)
                else:
                    tile = jnp.where((group == c) & (lane_id % PAN == row_id), 1.0, tile)
            packed.append(tile)
        inverse = [jnp.where(lane_id % PAN == row_id, 1.0, 0.0) for _ in range(tiles)]
        scales = [jnp.ones((PAN, BS), jnp.float32) for _ in range(tiles)]
        for k in range(PAN):
            index = group * PAN + k
            for t in range(tiles):
                tile = packed[t]
                column = jnp.take_along_axis(tile, index, axis=1, mode="promise_in_bounds")
                pivot = column[k : k + 1]
                scales[t] = jnp.where(row_id == k, lax.rsqrt(pivot), scales[t])
                if k < PAN - 1:
                    factor = jnp.where(row_id > k, column * (1.0 / pivot), 0.0)
                    packed[t] = tile - factor * tile[k : k + 1]
                    inverse[t] = inverse[t] - factor * inverse[t][k : k + 1]
        for t in range(tiles):
            low = inverse[t] * scales[t]
            spread = jnp.concatenate([jnp.where(group == c, low, 0.0) for c in range(PACK)], 0)
            here = min(rows, (count - t * PACK) * PAN)
            spread = spread[:here]
            if here < rows:
                spread = spread[:, :here]
            span = slice(t * rows, t * rows + here)
            work[p, span, :] = fdot(spread, work[p, span, :], 1, 0)
        if p < panels - 1:

            def trail(step, _, p=p):
                ids = [step * batch + c for c in range(batch)]
                uppers = [work[p, pl.ds(b * PAN, PAN), :] for b in ids]
                changes = [fdot(upper[:, :BS], upper, 0, 0) for upper in uppers]
                for b, change in zip(ids, changes):
                    for q in range(p + 1, panels):
                        work[q, pl.ds(b * PAN, PAN), :] -= change[q * PAN : (q + 1) * PAN]
                return _

            lax.fori_loop(0, count // batch, trail, 0)

    def finish(b, _):
        rows_q = jnp.concatenate([work[p, pl.ds(b * PAN, PAN), BS:] for p in range(panels)], 0)
        out_ref[b] = rows_q.T
        return _

    lax.fori_loop(0, count, finish, 0, unroll=2)


def renew_all(stats, bases):
    count = stats.shape[0]
    return pl.pallas_call(
        functools.partial(qr_kernel, count),
        out_shape=jax.ShapeDtypeStruct((count, BS, BS), jnp.float32),
        in_specs=[pl.BlockSpec(memory_space=pltpu.VMEM)] * 2,
        out_specs=pl.BlockSpec(memory_space=pltpu.VMEM),
        scratch_shapes=[pltpu.VMEM((BS // PAN, count * PAN, 2 * BS), jnp.float32)],
        name="renew",
    )(stats, bases)


def soap_update(weight, first_moment, second_moment, left, right, left_rot, right_rot, grad, dp):
    left = beta_two * left + (1.0 - beta_two) * jnp.einsum(
        "bij,bkj->bik", grad, grad, precision=HIGHEST
    )
    right = beta_two * right + (1.0 - beta_two) * jnp.einsum(
        "bji,bjk->bik", grad, grad, precision=HIGHEST
    )
    rotated = jnp.einsum("bji,bjk->bik", left_rot, grad, precision=HIGHEST)
    rotated = jnp.einsum("bij,bjk->bik", rotated, right_rot, precision=HIGHEST)
    first_moment = beta_one * first_moment + (1.0 - beta_one) * rotated
    second_moment = beta_two * second_moment + (1.0 - beta_two) * rotated * rotated
    direction = (
        first_moment
        / (1.0 - beta_one**STEP)
        / (jnp.sqrt(second_moment / (1.0 - beta_two**STEP)) + epsilon)
    )
    direction = jnp.einsum("bij,bjk->bik", left_rot, direction, precision=HIGHEST)
    direction = jnp.einsum("bij,bkj->bik", direction, right_rot, precision=HIGHEST)
    weight = weight - learn_rate * (direction + weight_decay * weight)
    is_left = lax.axis_index("dp") % 2 == 0
    renewed = renew_all(jnp.where(is_left, left, right), jnp.where(is_left, left_rot, right_rot))
    other = swap(renewed, "dp", dp, 1)
    return (
        weight,
        first_moment,
        second_moment,
        left,
        right,
        jnp.where(is_left, renewed, other),
        jnp.where(is_left, other, renewed),
    )


def adam_update(weight, first_moment, second_moment, grad, decay_rate, rate):
    first_moment = beta_one * first_moment + (1.0 - beta_one) * grad
    second_moment = beta_two * second_moment + (1.0 - beta_two) * grad * grad
    direction = (
        first_moment
        / (1.0 - beta_one**STEP)
        / (jnp.sqrt(second_moment / (1.0 - beta_two**STEP)) + epsilon)
    )
    return (weight - rate * (direction + decay_rate * weight), first_moment, second_moment)


def shards(
    latents,
    actions,
    game_ids,
    action_masks,
    valid_steps,
    target_bins,
    target_fracs,
    continues,
    owner_order,
    blocks,
    block_first,
    block_second,
    left_stat,
    right_stat,
    left_basis,
    right_basis,
    latent_maps,
    latent_first,
    latent_second,
    head_weights,
    head_first,
    head_second,
    small_params,
    small_first,
    small_second,
    ema_critic,
    dp,
    fsdp,
):
    block_grad, maps_grad, packed_grad, square, sums = model_grads(
        latents, actions, game_ids, action_masks, valid_steps, target_bins, target_fracs, continues,
        owner_order, blocks, latent_maps, head_weights, small_params, dp, fsdp,
    )
    head_grad, small_grad = unpack_heads(packed_grad, small_params.shape[0])
    counted = sums[1]
    loss_value = sums[0] / counted
    grad_norm = jnp.sqrt(square) / counted
    factor = jnp.minimum(1.0, clip_norm / grad_norm) / counted
    soap_out = soap_update(
        blocks,
        block_first,
        block_second,
        left_stat,
        right_stat,
        left_basis,
        right_basis,
        block_grad * factor,
        dp,
    )
    maps_out = adam_update(
        latent_maps, latent_first, latent_second, maps_grad * factor, weight_decay, learn_rate
    )
    heads_out = adam_update(
        head_weights, head_first, head_second, head_grad * factor, weight_decay, learn_rate
    )
    small_out = adam_update(
        small_params, small_first, small_second, small_grad * factor, 0.0, small_rate
    )
    ema_new = ema_rate * ema_critic + (1.0 - ema_rate) * heads_out[0][:, BINS : 2 * BINS]
    return (
        loss_value,
        grad_norm,
        soap_out[0],
        soap_out[1],
        soap_out[2],
        soap_out[3],
        soap_out[4],
        soap_out[5],
        soap_out[6],
        maps_out[0],
        maps_out[1],
        maps_out[2],
        heads_out[0],
        heads_out[1],
        heads_out[2],
        small_out[0],
        small_out[1],
        small_out[2],
        ema_new,
    )


def solution(mesh):
    placed = (
        P(("dp", "fsdp"), None, None),
        P(("dp", "fsdp"), None),
        P(("dp", "fsdp")),
        P(),
        P(("dp", "fsdp"), None),
        P(("dp", "fsdp"), None, None),
        P(("dp", "fsdp"), None, None),
        P(("dp", "fsdp"), None),
        P(),
        P("fsdp", None, None),
        P("fsdp", None, None),
        P("fsdp", None, None),
        P("fsdp", None, None),
        P("fsdp", None, None),
        P("fsdp", None, None),
        P("fsdp", None, None),
        P("fsdp", None),
        P("fsdp", None),
        P("fsdp", None),
        P(),
        P(),
        P(),
        P(),
        P(),
        P(),
        P(),
    )
    return jax.shard_map(
        functools.partial(shards, dp=mesh.shape["dp"], fsdp=mesh.shape["fsdp"]),
        mesh=mesh,
        in_specs=placed,
        out_specs=(
            P(),
            P(),
            P("fsdp", None, None),
            P("fsdp", None, None),
            P("fsdp", None, None),
            P("fsdp", None, None),
            P("fsdp", None, None),
            P("fsdp", None, None),
            P("fsdp", None, None),
            P("fsdp", None),
            P("fsdp", None),
            P("fsdp", None),
            P(),
            P(),
            P(),
            P(),
            P(),
            P(),
            P(),
        ),
        check_vma=False,
    )
```

```python
import functools
import math

import jax
import jax.numpy as jnp
from jax import lax
from jax.experimental import pallas as pl
from jax.experimental.pallas import tpu as pltpu
from jax.sharding import PartitionSpec as P

D = 512
NH = 8
DH = 64
FF = 2048
GROUPS = 32
CLASSES = 32
LAT = 1024
BINS = 255
NA = 18
LAYERS = 1
F = 64
NGAME = 26
BS = 128
STEP = 10
PAN = 16
PACK = 8
HEAD_COLS = 640
PACK_ROWS = 3072
MAP_CHUNKS = ((0, 1), (2,), (3,))
PART_ROWS = (384, 368, 368)
TM = 256
GELU_A = math.sqrt(2.0 / math.pi)
GELU_B = 0.044715


HIGHEST = lax.Precision.HIGHEST
beta_one = 0.9
beta_two = 0.99
epsilon = 1e-08
learn_rate = 0.03
small_rate = 0.15
weight_decay = 0.01
clip_norm = 0.05
ema_rate = 0.98
norm_eps = 1e-05


def positions(frames, width):
    frame_index = jnp.arange(frames).astype(jnp.float32)[:, None]
    feature = jnp.arange(width)
    freq = jnp.exp(-(feature // 2 * 2).astype(jnp.float32) * (math.log(10000.0) / width))
    angle = frame_index * freq[None, :]
    return jnp.where(feature % 2 == 0, jnp.sin(angle), jnp.cos(angle))


def halves(size):
    return [1 << bit for bit in reversed(range(size.bit_length() - 1))]


def swap(value, axis, size, bit):
    return lax.ppermute(value, axis, [(i, i ^ bit) for i in range(size)])


def part_orders(dp, fsdp):
    core, tall = [("dp", dp, bit) for bit in reversed(halves(dp))]
    deep, near, side = [("fsdp", fsdp, bit) for bit in halves(fsdp)]
    return (
        (core, tall, side, near, deep),
        (core, side, near, deep, tall),
        (core, near, tall, side, deep),
    )


def order_index(order, dp_here, fsdp_here):
    dp_index = jnp.zeros((), jnp.int32)
    fsdp_index = jnp.zeros((), jnp.int32)
    spot = jnp.arange(1 << len(order))
    for place, (axis, _, bit) in enumerate(order):
        flag = (spot >> (len(order) - 1 - place)) & 1
        if axis == "dp":
            dp_index = dp_index + flag * bit
        else:
            fsdp_index = fsdp_index + flag * bit
    return dp_index ^ dp_here, fsdp_index ^ fsdp_here


def scatter_sum(held, sent, order, wide_stages):
    for place, (axis, size, bit) in enumerate(order):
        got = swap(sent, axis, size, bit)
        held = held + got.astype(jnp.float32)
        half = held.shape[0] // 2
        if half:
            held, sent = held[:half], held[half:]
            if place + 1 < len(order) - wide_stages:
                sent = sent.astype(jnp.bfloat16)
    return held[0]


def gather_doubling(value, order):
    held = value[None]
    for axis, size, bit in reversed(order):
        held = jnp.concatenate([held, swap(held, axis, size, bit)], 0)
    return held


def inverse_place(order, dp, fsdp, dp_here, fsdp_here):
    dp_id = jnp.arange(dp)[None, :] ^ dp_here
    fsdp_id = jnp.arange(fsdp)[:, None] ^ fsdp_here
    spot = jnp.zeros((fsdp, dp), jnp.int32)
    for place, (axis, _, bit) in enumerate(order):
        source = dp_id if axis == "dp" else fsdp_id
        flag = (source & bit) // bit
        spot = spot + flag * (1 << (len(order) - 1 - place))
    return spot


def placed_units(dp, fsdp):
    dp_here = lax.axis_index("dp")
    fsdp_here = lax.axis_index("fsdp")
    units = []
    spots = []
    for order in part_orders(dp, fsdp):
        dp_index, fsdp_index = order_index(order, dp_here, fsdp_here)
        units.append(fsdp_index * dp + dp_index)
        spots.append(inverse_place(order, dp, fsdp, dp_here, fsdp_here).reshape(-1))
    return jnp.stack(units), jnp.stack(spots)


def gathered_pieces(blocks_low, maps_low, dp, fsdp):
    dp_here = lax.axis_index("dp")
    quarter = blocks_low.shape[0] // dp
    piece_rows = maps_low.shape[0] // dp
    own_blocks = lax.dynamic_slice_in_dim(blocks_low, dp_here * quarter, quarter, 0)
    own_maps = lax.dynamic_slice_in_dim(maps_low, dp_here * piece_rows, piece_rows, 0)
    pieces = []
    for part, order in enumerate(part_orders(dp, fsdp)):
        piece = jnp.concatenate(
            [own_blocks[2 * part], own_blocks[2 * part + 1]]
            + [own_maps[:, c * BS : (c + 1) * BS] for c in MAP_CHUNKS[part]],
            0,
        )
        held = gather_doubling(piece, order[2:])
        both = [held, swap(held, *order[1])]
        pieces += both + [swap(piece, *order[0]) for piece in both]
    return pieces


def reduced_grads(outs, sums, slots, map_rows, dp, fsdp):
    if (dp, fsdp) != (4, 8):
        both = ("dp", "fsdp")
        block_grad = lax.psum(
            lax.psum_scatter(outs[0], "fsdp", scatter_dimension=0, tiled=True), "dp"
        )
        maps_grad = lax.psum(
            lax.psum_scatter(outs[1], "fsdp", scatter_dimension=0, tiled=True), "dp"
        )
        heads = lax.psum(outs[2], both)
        sums = lax.psum(sums, both)
        held = lax.psum(jnp.sum(block_grad * block_grad) + jnp.sum(maps_grad * maps_grad), "fsdp")
        return block_grad, maps_grad, heads, held + jnp.sum(heads * heads), sums
    dp_here = lax.axis_index("dp")
    fsdp_here = lax.axis_index("fsdp")
    parts = [
        scatter_sum(outs[2 * part], outs[2 * part + 1], order, 1)
        for part, order in enumerate(part_orders(dp, fsdp))
    ]
    cut = 2 * BS
    own_blocks = jnp.concatenate([part[:cut] for part in parts], 0)
    own_maps = jnp.concatenate([parts[0][cut:], parts[1][cut : cut + 64], parts[2][cut : cut + 64]], 0)
    own_heads = jnp.concatenate([parts[1][cut + 64 :], parts[2][cut + 64 :]], 0)
    own_square = sum(jnp.sum(part * part) for part in parts)
    totals = jnp.concatenate([sums, own_square[None]])
    totals = jnp.pad(totals[None], ((0, 7), (0, BS - totals.shape[0])))
    own_heads = jnp.concatenate([own_heads, totals], 0)
    dp_order = [("dp", dp, bit) for bit in reversed(halves(dp))]
    spot = inverse_place(dp_order, dp, 1, dp_here, 0).reshape(-1)
    shard = gather_doubling(jnp.concatenate([own_blocks, own_maps], 0), dp_order)
    shard = shard[spot]
    count = slots // dp * BS
    piece_rows = map_rows // dp
    block_grad = shard[:, :count].reshape(slots, BS, BS)
    maps_grad = (
        shard[:, count:]
        .reshape(dp, D // BS, piece_rows, BS)
        .transpose(0, 2, 1, 3)
        .reshape(map_rows, D)
    )
    core, tall, side, near, deep = part_orders(dp, fsdp)[0]
    full_order = (core, deep, side, near, tall)
    all_heads = gather_doubling(own_heads, full_order)
    spot = inverse_place(full_order, dp, fsdp, dp_here, fsdp_here).reshape(-1)
    all_heads = all_heads[spot]
    sums = jnp.sum(all_heads[:, -8, :3], 0)
    return block_grad, maps_grad, all_heads[:, :-8].reshape(-1, BS), sums[-1], sums[:-1]


def norm_rows(inputs, gain_row, bias_row):
    center = inputs - jnp.mean(inputs, -1, keepdims=True)
    rstd = lax.rsqrt(jnp.mean(center * center, -1, keepdims=True) + norm_eps)
    scaled = center * rstd
    return scaled * gain_row + bias_row, scaled, rstd


def norm_rows_back(grad_out, scaled, rstd, gain_row):
    grad_scaled = grad_out * gain_row
    return rstd * (
        grad_scaled
        - jnp.mean(grad_scaled, -1, keepdims=True)
        - scaled * jnp.mean(grad_scaled * scaled, -1, keepdims=True)
    )


def dot32(left, right, ca, cb):
    return lax.dot_general(
        left, right, (((ca,), (cb,)), ((), ())), preferred_element_type=jnp.float32
    )


def model_kernel(fast, rows_of, *refs):
    refs = list(refs)
    take = lambda count: [refs.pop(0) for _ in range(count)]
    (owner, units, block_place, unit_place) = take(4)
    sources = take(12 if fast else 2)
    (hot, target, later_row, base, facts, legal, next_hot, act_hot, gains, head_w, head_b) = take(11)
    outs = take(6 if fast else 3)
    (sums_out,) = take(1)
    (wall, maps) = take(2)
    (normed1, qkv, probs, mixed, normed2, slope, act, final, grad_dyn, grad_head) = take(10)
    (grad_low, grad_pre, grad_mid, grad_qkv, grad_hid, small, bias_sum) = take(7)
    if fast:
        keep, send = take(2)
    wall_sem, maps_sem, out_sem = take(3)
    tokens = base.shape[0]
    tile = D // BS
    wide = FF // BS
    out_at = 3 * tile * tile
    expand_at = out_at + tile * tile
    contract_at = expand_at + tile * wide

    if fast:
        for part in range(3):
            for piece in range(4):
                source = sources[part * 4 + piece]

                def fetch(j, carry, part=part, piece=piece, source=source):
                    unit = units[part * 32 + piece * 8 + j]
                    for k in range(2):
                        block = owner[unit * 6 + part * 2 + k]
                        pltpu.make_async_copy(
                            source.at[j, k * BS : (k + 1) * BS, :], wall.at[block], wall_sem
                        ).start()
                    for i, chunk in enumerate(MAP_CHUNKS[part]):
                        pltpu.make_async_copy(
                            source.at[j, 2 * BS + i * 64 : 2 * BS + (i + 1) * 64, :],
                            maps.at[
                                pl.ds(pl.multiple_of(unit * 64, 64), 64),
                                chunk * BS : (chunk + 1) * BS,
                            ],
                            maps_sem,
                        ).start()
                    return carry

                lax.fori_loop(0, 8, fetch, 0)
    else:

        def fetch(j, carry):
            pltpu.make_async_copy(sources[0].at[j], wall.at[owner[j]], wall_sem).start()
            return carry

        lax.fori_loop(0, wall.shape[0], fetch, 0)
        pltpu.make_async_copy(sources[1], maps, maps_sem).start()
    small[...] = jnp.zeros_like(small)
    bias_sum[...] = jnp.zeros_like(bias_sum)
    sums_out[...] = jnp.zeros_like(sums_out)
    pltpu.make_async_copy(wall, wall, wall_sem).wait()
    pltpu.make_async_copy(maps, maps, maps_sem).wait()

    def grid_of(start, stride, row_count, col_count):
        return jnp.concatenate(
            [
                jnp.concatenate([wall[start + r * stride + c] for c in range(col_count)], 1)
                for r in range(row_count)
            ],
            0,
        )

    def chunk(step, carry):
        rows = pl.ds(pl.multiple_of(step * TM, TM), TM)
        hidden = dot32(hot[:, rows], maps[:LAT, :], 0, 0) + base[rows, :]
        normed, scaled1, rstd1 = norm_rows(hidden, gains[0:1], gains[1:2])
        normed1[rows, :] = normed.astype(jnp.bfloat16)

        def joint_strip(s, c):
            cols = pl.ds(pl.multiple_of(s * 256, 256), 256)
            weight = grid_of(2 * s, 3 * tile, tile, 2)
            qkv[rows, cols] = dot32(normed1[rows, :], weight, 1, 0).astype(jnp.bfloat16)
            return c

        lax.fori_loop(0, 6, joint_strip, 0)
        lane = lax.broadcasted_iota(jnp.int32, (BS, BS), 1)
        line = lax.broadcasted_iota(jnp.int32, (BS, BS), 0)
        allowed = (line >= lane) & (line // F == lane // F)
        low_half = lane < DH
        halves_of = [mask.astype(jnp.float32).astype(jnp.bfloat16) for mask in (low_half, ~low_half)]

        def attend(s, c):
            sub = pl.ds(pl.multiple_of(step * TM + s * BS, BS), BS)
            for pair in range(NH // 2):
                spans = [slice(part * D + pair * BS, part * D + (pair + 1) * BS) for part in range(3)]
                query, key, value = [qkv[sub, span] for span in spans]
                mixes = []
                for side in range(2):
                    half = halves_of[side]
                    scores = dot32(query * half, key, 1, 1) * DH ** (-0.5)
                    scores = jnp.where(allowed, scores, -1e30)
                    shifted = scores - jnp.max(scores, -1, keepdims=True)
                    power = jnp.exp(shifted)
                    prob = power / jnp.sum(power, -1, keepdims=True)
                    probs[2 * pair + side, sub, :] = prob
                    mixes.append(dot32(prob.astype(jnp.bfloat16), value, 1, 0))
                mixed[sub, pair * BS : (pair + 1) * BS] = jnp.where(low_half, *mixes).astype(
                    jnp.bfloat16
                )
            return c

        lax.fori_loop(0, TM // BS, attend, 0)
        out_map = grid_of(out_at, tile, tile, tile)
        middle = hidden + dot32(mixed[rows, :], out_map, 1, 0)
        normed, scaled2, rstd2 = norm_rows(middle, gains[2:3], gains[3:4])
        normed2[rows, :] = normed.astype(jnp.bfloat16)

        def expand_strip(s, c):
            cols = pl.ds(pl.multiple_of(s * 256, 256), 256)
            weight = grid_of(expand_at + 2 * s, wide, tile, 2)
            pre = dot32(normed2[rows, :], weight, 1, 0)
            square = pre * pre
            curve = jnp.tanh(GELU_A * (pre + GELU_B * (square * pre)))
            act[rows, cols] = (0.5 * pre * (1.0 + curve)).astype(jnp.bfloat16)
            slope[:, cols] = 0.5 * (1.0 + curve) + 0.5 * pre * (1.0 - curve * curve) * (
                GELU_A * (1.0 + 3.0 * GELU_B * square)
            )
            return c

        lax.fori_loop(0, FF // 256, expand_strip, 0)

        def contract_strip(s, total):
            cols = pl.ds(pl.multiple_of(s * 512, 512), 512)
            weight = grid_of(contract_at + s * 4 * tile, tile, 4, tile)
            return total + dot32(act[rows, cols], weight, 1, 0)

        top = lax.fori_loop(0, FF // 512, contract_strip, middle)
        normed, scaled3, rstd3 = norm_rows(top, gains[4:5], gains[5:6])
        final[rows, :] = normed.astype(jnp.bfloat16)
        late = later_row[0:1, rows]

        def dyn_strip(s, total):
            span = pl.ds(pl.multiple_of(s * 256, 256), 256)
            below = pl.ds(pl.multiple_of(LAT + s * 256, 256), 256)
            logits = dot32(maps[below, :], final[rows, :], 1, 1)
            logits = logits.reshape(256 // CLASSES, CLASSES, TM)
            shifted = logits - jnp.max(logits, 1, keepdims=True)
            power = jnp.exp(shifted)
            norm = jnp.sum(power, 1, keepdims=True)
            wanted = target[span, rows].astype(jnp.float32).reshape(256 // CLASSES, CLASSES, TM)
            spent = jnp.sum(wanted * (jnp.log(norm) - shifted), 0)
            grad = (power / norm - wanted) * late[None]
            grad_dyn[span, rows] = grad.reshape(256, TM).astype(jnp.bfloat16)
            return total + jnp.sum(spent, 0, keepdims=True) * late

        dyn_loss = lax.fori_loop(0, LAT // 256, dyn_strip, jnp.zeros((1, TM), jnp.float32))
        heads = dot32(final[rows, :], head_w[...], 1, 0) + head_b[0:1]
        now = facts[rows, 0:1]
        late_col = facts[rows, 1:2]
        spot = lax.broadcasted_iota(jnp.int32, (TM, 256), 1).astype(jnp.float32)
        frame_loss = jnp.zeros((TM, 1), jnp.float32)
        for which in range(2):
            logits = heads[:, which * 256 : (which + 1) * 256]
            bin_low = facts[rows, 2 + which : 3 + which]
            upper = facts[rows, 4 + which : 5 + which]
            weights = jnp.where(spot == bin_low, 1.0 - upper, 0.0)
            weights = weights + jnp.where(spot == bin_low + 1.0, upper, 0.0)
            shifted = logits - jnp.max(logits, -1, keepdims=True)
            power = jnp.exp(shifted)
            norm = jnp.sum(power, -1, keepdims=True)
            frame_loss = frame_loss + jnp.sum(
                weights * jnp.where(weights > 0.0, jnp.log(norm) - shifted, 0.0), -1, keepdims=True
            )
            grad = (power / norm - weights) * now
            grad_head[rows, which * 256 : (which + 1) * 256] = grad.astype(jnp.bfloat16)
            bias_sum[0:1, which * 256 : (which + 1) * 256] += jnp.sum(
                grad.astype(jnp.bfloat16).astype(jnp.float32), 0, keepdims=True
            )
        tail = heads[:, 512:640]
        logit = tail[:, 0:1]
        goal = facts[rows, 6:7]
        soft = jnp.maximum(logit, 0.0) + jnp.log1p(jnp.exp(-jnp.abs(logit)))
        frame_loss = (frame_loss + soft - goal * logit) * now
        may = legal[rows, :]
        chosen = next_hot[rows, :]
        masked = jnp.where(may > 0.5, tail, -1e30)
        shifted = masked - jnp.max(masked, -1, keepdims=True)
        power = jnp.exp(shifted)
        norm = jnp.sum(power, -1, keepdims=True)
        actor = jnp.sum(
            jnp.where(chosen > 0.5, jnp.log(norm) - shifted, 0.0), -1, keepdims=True
        )
        frame_loss = frame_loss + actor * late_col
        grad = (power / norm - chosen) * late_col
        column = lax.broadcasted_iota(jnp.int32, (TM, BS), 1)
        grad = jnp.where(column == 0, (jax.nn.sigmoid(logit) - goal) * now, grad)
        grad_head[rows, 512:640] = grad.astype(jnp.bfloat16)
        bias_sum[0:1, 512:640] += jnp.sum(
            grad.astype(jnp.bfloat16).astype(jnp.float32), 0, keepdims=True
        )
        sums_out[0:1, :] += jnp.broadcast_to(
            jnp.sum(dyn_loss, -1, keepdims=True) + jnp.sum(frame_loss, 0, keepdims=True), (1, BS)
        )
        sums_out[1:2, :] += jnp.broadcast_to(jnp.sum(now, 0, keepdims=True), (1, BS))

        grad_final = dot32(grad_dyn[:, rows], maps[LAT:, :], 0, 0) + dot32(
            grad_head[rows, :], head_w[...], 1, 1
        )
        small[4:5, :] += jnp.sum(grad_final * scaled3, 0, keepdims=True)
        small[5:6, :] += jnp.sum(grad_final, 0, keepdims=True)
        grad_top = norm_rows_back(grad_final, scaled3, rstd3, gains[4:5])
        grad_low[rows, :] = grad_top.astype(jnp.bfloat16)

        def act_strip(s, total):
            cols = pl.ds(pl.multiple_of(s * 256, 256), 256)
            weight = grid_of(contract_at + s * 2 * tile, tile, 2, tile)
            grad = dot32(grad_low[rows, :], weight, 1, 1) * slope[:, cols]
            grad = grad.astype(jnp.bfloat16)
            grad_pre[rows, cols] = grad
            weight = grid_of(expand_at + 2 * s, wide, tile, 2)
            return total + dot32(grad, weight, 1, 1)

        grad_normed = lax.fori_loop(
            0, FF // 256, act_strip, jnp.zeros((TM, D), jnp.float32)
        )
        small[2:3, :] += jnp.sum(grad_normed * scaled2, 0, keepdims=True)
        small[3:4, :] += jnp.sum(grad_normed, 0, keepdims=True)
        grad_middle = grad_top + norm_rows_back(grad_normed, scaled2, rstd2, gains[2:3])
        grad_mid[rows, :] = grad_middle.astype(jnp.bfloat16)
        out_map = grid_of(out_at, tile, tile, tile)
        mixed_grad = dot32(grad_mid[rows, :], out_map, 1, 1).astype(jnp.bfloat16)
        grad_hid[rows, :] = mixed_grad

        def attend_back(s, c):
            sub = pl.ds(pl.multiple_of(step * TM + s * BS, BS), BS)
            for pair in range(NH // 2):
                spans = [slice(part * D + pair * BS, part * D + (pair + 1) * BS) for part in range(3)]
                query, key, value = [qkv[sub, span] for span in spans]
                grad_out = grad_hid[sub, pair * BS : (pair + 1) * BS]
                totals = [jnp.zeros((BS, BS), jnp.float32) for _ in range(3)]
                for side in range(2):
                    half = halves_of[side]
                    prob = probs[2 * pair + side, sub, :]
                    out_half = grad_out * half
                    grad_prob = dot32(out_half, value, 1, 1)
                    dots = jnp.sum(grad_prob * prob, -1, keepdims=True)
                    grad_score = (prob * (grad_prob - dots)).astype(jnp.bfloat16)
                    totals[0] += dot32(grad_score, key * half, 1, 0)
                    totals[1] += dot32(grad_score, query * half, 0, 0)
                    totals[2] += dot32(prob.astype(jnp.bfloat16), out_half, 0, 0)
                for part, (span, total) in enumerate(zip(spans, totals)):
                    scale = DH ** (-0.5) if part < 2 else 1.0
                    grad_qkv[sub, span] = (total * scale).astype(jnp.bfloat16)
            return c

        lax.fori_loop(0, TM // BS, attend_back, 0)

        def joint_back(s, total):
            cols = pl.ds(pl.multiple_of(s * 512, 512), 512)
            weight = grid_of(4 * s, 3 * tile, tile, 4)
            return total + dot32(grad_qkv[rows, cols], weight, 1, 1)

        grad_normed = lax.fori_loop(0, 3, joint_back, jnp.zeros((TM, D), jnp.float32))
        small[0:1, :] += jnp.sum(grad_normed * scaled1, 0, keepdims=True)
        small[1:2, :] += jnp.sum(grad_normed, 0, keepdims=True)
        grad_in = grad_middle + norm_rows_back(grad_normed, scaled1, rstd1, gains[0:1])
        grad_hid[rows, :] = grad_in.astype(jnp.bfloat16)
        pieces = thirds(grad_in)
        small[...] += sum(dot32(act_hot[:, rows], piece, 1, 0) for piece in pieces)
        return carry

    lax.fori_loop(0, tokens // TM, chunk, 0)

    def put(place, rows, first, value):
        part = (place >> 8) & 3
        spot = place & 15
        dest = pl.ds(first, rows)

        @pl.when(((place >> 4) & 1) == 0)
        def _():
            keep[part, spot, dest, :] = value

        @pl.when(((place >> 4) & 1) == 1)
        def _():
            send[part, spot, dest, :] = value.astype(jnp.bfloat16)

    def put_block(block, value):
        place = block_place[block]
        if fast:
            put(place, BS, pl.multiple_of(((place >> 10) & 1) * BS, BS), value)
        else:
            outs[0][place] = value

    def block_grads(start, stride, left, right, row_count, col_steps):
        def strip(s, c):
            cols = pl.ds(pl.multiple_of(s * 256, 256), 256)
            grads = dot32(left, right[:, cols], 0, 0)
            for r in range(row_count):
                for k in range(2):
                    put_block(
                        start + r * stride + 2 * s + k,
                        grads[r * BS : (r + 1) * BS, k * BS : (k + 1) * BS],
                    )
            return c

        lax.fori_loop(0, col_steps, strip, 0)

    block_grads(0, 3 * tile, normed1[...], grad_qkv, tile, 6)
    block_grads(out_at, tile, mixed[...], grad_mid, tile, 2)
    block_grads(expand_at, wide, normed2[...], grad_pre, tile, FF // 256)

    def contract_rows(m, c):
        cols = pl.ds(pl.multiple_of(m * D, D), D)
        for s in range(2):
            grads = dot32(act[:, cols], grad_low[:, s * 256 : (s + 1) * 256], 0, 0)
            for r in range(tile):
                for k in range(2):
                    put_block(
                        contract_at + (m * tile + r) * tile + 2 * s + k,
                        grads[r * BS : (r + 1) * BS, k * BS : (k + 1) * BS],
                    )
        return c

    lax.fori_loop(0, FF // D, contract_rows, 0)

    def map_rows(m, c):
        span = pl.ds(pl.multiple_of(m * 256, 256), 256)
        for table in range(2):
            source, other = ((hot, grad_hid), (grad_dyn, final))[table]
            grads = dot32(source[span, :], other[...], 1, 0)
            if not fast:
                outs[1][pl.ds(pl.multiple_of(table * LAT + m * 256, 256), 256), :] = grads
                continue
            for u in range(4):
                unit = table * (LAT // 64) + m * 4 + u
                for part in range(3):
                    place = unit_place[part * 32 + unit]
                    for i, piece in enumerate(MAP_CHUNKS[part]):
                        put(
                            place,
                            64,
                            2 * BS + i * 64,
                            grads[u * 64 : (u + 1) * 64, piece * BS : (piece + 1) * BS],
                        )
        return c

    lax.fori_loop(0, LAT // 256, map_rows, 0)
    pieces = []
    for c in range(5):
        pieces.append(dot32(final[...], grad_head[:, c * BS : (c + 1) * BS], 0, 0))
    packed = jnp.concatenate(
        pieces
        + [
            bias_sum[0:1, c * BS : (c + 1) * BS] if c < 5 else jnp.zeros((3, BS), jnp.float32)
            for c in range(6)
        ]
        + [small[:, c * BS : (c + 1) * BS] for c in range(tile)]
        + [jnp.zeros((PACK_ROWS - 5 * D - 8 - tile * small.shape[0], BS), jnp.float32)],
        0,
    )
    if not fast:
        outs[2][...] = packed
        return
    for unit in range(32):
        for half in range(2):
            part = 1 + half
            place = unit_place[part * 32 + unit]
            first = unit * 96 + half * 48
            put(place, 48, 2 * BS + 64, packed[first : first + 48])
    copies = []
    for part in range(3):
        for which, scratch in enumerate((keep, send)):
            copies.append(
                pltpu.make_async_copy(
                    scratch.at[part, :, 0 : rows_of[part], :],
                    outs[part * 2 + which],
                    out_sem.at[part * 2 + which],
                )
            )
    for copy in copies:
        copy.start()
    for copy in copies:
        copy.wait()


def spread_cols(head):
    gap = jnp.zeros((head.shape[0], 1), head.dtype)
    rest = jnp.zeros((head.shape[0], BS - 1 - NA), head.dtype)
    return jnp.concatenate(
        [head[:, :BINS], gap, head[:, BINS : 2 * BINS], gap, head[:, 2 * BINS :], rest], 1
    )


def unpack_heads(packed, small_rows):
    chunks = [packed[c * D : (c + 1) * D] for c in range(5)]
    bias = jnp.concatenate([packed[5 * D + c : 5 * D + c + 1] for c in range(5)], 1)
    head = jnp.concatenate([jnp.concatenate(chunks, 1), bias], 0)
    head = jnp.concatenate(
        [head[:, :BINS], head[:, 256 : 256 + BINS], head[:, 512 : 513 + NA]], 1
    )
    start = 5 * D + 8
    small = jnp.concatenate(
        [packed[start + c * small_rows : start + (c + 1) * small_rows] for c in range(D // BS)], 1
    )
    return head, small


def model_grads(
    latents, actions, game_ids, action_masks, valid_steps, target_bins, target_fracs, continues,
    owner_order, blocks, latent_maps, head_weights, small_params, dp, fsdp,
):
    fast = (dp, fsdp) == (4, 8)
    seqs_here = latents.shape[0]
    tokens = seqs_here * F
    blocks_low = blocks.astype(jnp.bfloat16)
    maps_low = latent_maps.astype(jnp.bfloat16)
    slot_ids = jnp.arange(owner_order.shape[0], dtype=jnp.int32)
    inverse = jnp.sum(jnp.where(owner_order[None, :] == slot_ids[:, None], slot_ids[None, :], 0), 1)
    if fast:
        units, spots = placed_units(dp, fsdp)
        part_ids = jnp.arange(3)[:, None]
        unit_place = (part_ids << 8) + spots
        slot_unit = inverse // 6
        slot_part = inverse % 6 // 2
        block_place = ((inverse % 2) << 10) + unit_place.reshape(-1)[slot_part * (dp * fsdp) + slot_unit]
        units = units.reshape(-1).astype(jnp.int32)
        unit_place = unit_place.reshape(-1).astype(jnp.int32)
        block_place = block_place.astype(jnp.int32)
    else:
        sources = [
            lax.all_gather(blocks_low, "fsdp", axis=0, tiled=True),
            lax.all_gather(maps_low, "fsdp", axis=0, tiled=True),
        ]
        units = unit_place = jnp.zeros((96,), jnp.int32)
        block_place = inverse
    class_ids = jnp.arange(CLASSES)[None, :, None]

    def one_hot_rows(values):
        rows = values.reshape(tokens, GROUPS).T
        return (rows[:, None, :] == class_ids).astype(jnp.bfloat16).reshape(LAT, tokens)

    frame_last = (jnp.arange(F) < F - 1).astype(jnp.float32)[None, :]
    later = (jnp.roll(valid_steps, -1, axis=1).astype(jnp.float32) * frame_last).reshape(tokens)
    now = valid_steps.astype(jnp.float32).reshape(tokens)
    action_hot = (actions.reshape(tokens, 1) == jnp.arange(NA)[None, :]).astype(jnp.float32)
    base = jnp.dot(action_hot, small_params[4 * LAYERS + 2 :], precision=HIGHEST)
    base = (base.reshape(seqs_here, F, D) + positions(F, D)[None]).reshape(tokens, D)
    facts = jnp.concatenate(
        [
            now[:, None],
            later[:, None],
            target_bins.reshape(tokens, 2).astype(jnp.float32),
            target_fracs.reshape(tokens, 2),
            continues.reshape(tokens, 1).astype(jnp.float32),
            jnp.zeros((tokens, BS - 7), jnp.float32),
        ],
        1,
    )
    game_hot = (game_ids[:, None] == jnp.arange(NGAME)[None, :]).astype(jnp.float32)
    legal_rows = jnp.dot(game_hot, action_masks.astype(jnp.float32), precision=HIGHEST)
    legal = jnp.broadcast_to(legal_rows[:, None, :], (seqs_here, F, NA)).reshape(tokens, NA)
    legal = jnp.pad(legal, ((0, 0), (1, BS - 1 - NA)))
    next_hot = (
        jnp.roll(actions, -1, axis=1).reshape(tokens, 1) == jnp.arange(BS)[None, :] - 1
    ).astype(jnp.float32)
    small_rows = small_params.shape[0]
    act_hot = (
        jnp.arange(small_rows)[:, None] - (4 * LAYERS + 2) == actions.reshape(1, tokens)
    ).astype(jnp.bfloat16)
    gains = jnp.pad(small_params[: 4 * LAYERS + 2], ((0, 2), (0, 0)))
    head_wide = spread_cols(head_weights[:D].astype(jnp.bfloat16))
    column = jnp.arange(HEAD_COLS)[None, :]
    head_bias = jnp.where(
        (column == BINS) | (column == 256 + BINS), -1e30, spread_cols(head_weights[D:])
    )
    vmem = pl.BlockSpec(memory_space=pltpu.VMEM)
    smem = pl.BlockSpec(memory_space=pltpu.SMEM)
    away = pl.BlockSpec(memory_space=pl.ANY)
    low = jnp.bfloat16
    wide_type = jnp.float32
    if fast:
        shapes = []
        for rows in PART_ROWS:
            shapes += [((16, rows, BS), wide_type), ((16, rows, BS), low)]
        out_specs = [away] * 6 + [vmem]
    else:
        shapes = [
            (( 192, BS, BS), wide_type), ((2 * LAT, D), wide_type), ((PACK_ROWS, BS), wide_type)
        ]
        out_specs = [vmem] * 4
    shapes.append(((8, BS), wide_type))
    scratch = [
        pltpu.VMEM((owner_order.shape[0], BS, BS), low),
        pltpu.VMEM((2 * LAT, D), low),
        pltpu.VMEM((tokens, D), low),
        pltpu.VMEM((tokens, 3 * D), low),
        pltpu.VMEM((NH, tokens, BS), wide_type),
        pltpu.VMEM((tokens, D), low),
        pltpu.VMEM((tokens, D), low),
        pltpu.VMEM((TM, FF), wide_type),
        pltpu.VMEM((tokens, FF), low),
        pltpu.VMEM((tokens, D), low),
        pltpu.VMEM((LAT, tokens), low),
        pltpu.VMEM((tokens, HEAD_COLS), low),
        pltpu.VMEM((tokens, D), low),
        pltpu.VMEM((tokens, FF), low),
        pltpu.VMEM((tokens, D), low),
        pltpu.VMEM((tokens, 3 * D), low),
        pltpu.VMEM((tokens, D), low),
        pltpu.VMEM((small_rows, D), wide_type),
        pltpu.VMEM((8, HEAD_COLS), wide_type),
    ]
    if fast:
        scratch += [
            pltpu.VMEM((3, 16, PART_ROWS[0], BS), wide_type),
            pltpu.VMEM((3, 16, PART_ROWS[0], BS), low),
        ]
    scratch += [
        pltpu.SemaphoreType.DMA,
        pltpu.SemaphoreType.DMA,
        pltpu.SemaphoreType.DMA((6,)),
    ]
    inputs = (
        owner_order, units, block_place, unit_place,
        one_hot_rows(latents), one_hot_rows(jnp.roll(latents, -1, axis=1)),
        jnp.broadcast_to(later[None], (8, tokens)), base, facts, legal, next_hot, act_hot, gains,
        head_wide, jnp.broadcast_to(head_bias, (8, HEAD_COLS)),
    )
    if fast:
        sources = gathered_pieces(blocks_low, maps_low, dp, fsdp)
    *outs, sums = pl.pallas_call(
        functools.partial(model_kernel, fast, PART_ROWS),
        out_shape=[jax.ShapeDtypeStruct(shape, kind) for shape, kind in shapes],
        in_specs=[smem] * 4 + [away] * len(sources) + [vmem] * 11,
        out_specs=out_specs,
        scratch_shapes=scratch,
        compiler_params=pltpu.CompilerParams(vmem_limit_bytes=66 * 1000 * 1000),
        name="model",
    )(*inputs[:4], *sources, *inputs[4:])
    return reduced_grads(outs, sums[:2, 0], blocks.shape[0], latent_maps.shape[0], dp, fsdp)


def thirds(value):
    first = value.astype(jnp.bfloat16)
    rest = value - first.astype(jnp.float32)
    second = rest.astype(jnp.bfloat16)
    third = (rest - second.astype(jnp.float32)).astype(jnp.bfloat16)
    return first, second, third


def stack_left(value, axis):
    a, b, c = thirds(value)
    return jnp.concatenate([a, a, b, a, b, c], axis)


def stack_right(value, axis):
    a, b, c = thirds(value)
    return jnp.concatenate([a, b, a, c, b, a], axis)


def fdot(left, right, ca, cb):
    return lax.dot_general(
        stack_left(left, ca),
        stack_right(right, cb),
        (((ca,), (cb,)), ((), ())),
        preferred_element_type=jnp.float32,
    )


def qr_kernel(count, stat_ref, basis_ref, out_ref, work):
    tiles = -(-count // PACK)
    rows = PACK * PAN
    panels = BS // PAN

    batch = next(size for size in (8, 6, 4, 3, 2, 1) if count % size == 0)

    def start(step, _):
        ids = [step * batch + c for c in range(batch)]
        stats = [stat_ref[b] for b in ids]
        bases = [basis_ref[b] for b in ids]
        scales = [
            1.0 / jnp.max(jnp.sum(jnp.abs(stat), -1, keepdims=True), 0, keepdims=True)
            for stat in stats
        ]
        xts = [fdot(base, stat, 0, 0) * scale for base, stat, scale in zip(bases, stats, scales)]
        grams = [fdot(xt, xt, 1, 1) for xt in xts]
        for b, xt, gram in zip(ids, xts, grams):
            for p in range(panels):
                work[p, pl.ds(b * PAN, PAN), :BS] = gram[p * PAN : (p + 1) * PAN]
                work[p, pl.ds(b * PAN, PAN), BS:] = xt[p * PAN : (p + 1) * PAN]
        return _

    lax.fori_loop(0, count // batch, start, 0)
    row_id = lax.broadcasted_iota(jnp.int32, (PAN, BS), 0)
    lane_id = lax.broadcasted_iota(jnp.int32, (PAN, BS), 1)
    group = lane_id // PAN
    for p in range(panels):
        packed = []
        for t in range(tiles):
            tile = jnp.zeros((PAN, BS), jnp.float32)
            for c in range(PACK):
                b = t * PACK + c
                if b < count:
                    diag = work[p, b * PAN : (b + 1) * PAN, :BS]
                    shift = (c - p) * PAN % BS
                    if shift:
                        diag = pltpu.roll(diag, shift, 1)
                    tile = jnp.where(group == c, diag, tile)
                else:
                    tile = jnp.where((group == c) & (lane_id % PAN == row_id), 1.0, tile)
            packed.append(tile)
        inverse = [jnp.where(lane_id % PAN == row_id, 1.0, 0.0) for _ in range(tiles)]
        scales = [jnp.ones((PAN, BS), jnp.float32) for _ in range(tiles)]
        for k in range(PAN):
            index = group * PAN + k
            for t in range(tiles):
                tile = packed[t]
                column = jnp.take_along_axis(tile, index, axis=1, mode="promise_in_bounds")
                pivot = column[k : k + 1]
                scales[t] = jnp.where(row_id == k, lax.rsqrt(pivot), scales[t])
                if k < PAN - 1:
                    factor = jnp.where(row_id > k, column * (1.0 / pivot), 0.0)
                    packed[t] = tile - factor * tile[k : k + 1]
                    inverse[t] = inverse[t] - factor * inverse[t][k : k + 1]
        for t in range(tiles):
            low = inverse[t] * scales[t]
            spread = jnp.concatenate([jnp.where(group == c, low, 0.0) for c in range(PACK)], 0)
            here = min(rows, (count - t * PACK) * PAN)
            spread = spread[:here]
            if here < rows:
                spread = spread[:, :here]
            span = slice(t * rows, t * rows + here)
            work[p, span, :] = fdot(spread, work[p, span, :], 1, 0)
        if p < panels - 1:

            def trail(step, _, p=p):
                ids = [step * batch + c for c in range(batch)]
                uppers = [work[p, pl.ds(b * PAN, PAN), :] for b in ids]
                changes = [fdot(upper[:, :BS], upper, 0, 0) for upper in uppers]
                for b, change in zip(ids, changes):
                    for q in range(p + 1, panels):
                        work[q, pl.ds(b * PAN, PAN), :] -= change[q * PAN : (q + 1) * PAN]
                return _

            lax.fori_loop(0, count // batch, trail, 0)

    def finish(b, _):
        rows_q = jnp.concatenate([work[p, pl.ds(b * PAN, PAN), BS:] for p in range(panels)], 0)
        out_ref[b] = rows_q.T
        return _

    lax.fori_loop(0, count, finish, 0, unroll=2)


def renew_all(stats, bases):
    count = stats.shape[0]
    return pl.pallas_call(
        functools.partial(qr_kernel, count),
        out_shape=jax.ShapeDtypeStruct((count, BS, BS), jnp.float32),
        in_specs=[pl.BlockSpec(memory_space=pltpu.VMEM)] * 2,
        out_specs=pl.BlockSpec(memory_space=pltpu.VMEM),
        scratch_shapes=[pltpu.VMEM((BS // PAN, count * PAN, 2 * BS), jnp.float32)],
        name="renew",
    )(stats, bases)


def soap_update(weight, first_moment, second_moment, left, right, left_rot, right_rot, grad, dp):
    left = beta_two * left + (1.0 - beta_two) * jnp.einsum(
        "bij,bkj->bik", grad, grad, precision=HIGHEST
    )
    right = beta_two * right + (1.0 - beta_two) * jnp.einsum(
        "bji,bjk->bik", grad, grad, precision=HIGHEST
    )
    rotated = jnp.einsum("bji,bjk->bik", left_rot, grad, precision=HIGHEST)
    rotated = jnp.einsum("bij,bjk->bik", rotated, right_rot, precision=HIGHEST)
    first_moment = beta_one * first_moment + (1.0 - beta_one) * rotated
    second_moment = beta_two * second_moment + (1.0 - beta_two) * rotated * rotated
    direction = (
        first_moment
        / (1.0 - beta_one**STEP)
        / (jnp.sqrt(second_moment / (1.0 - beta_two**STEP)) + epsilon)
    )
    direction = jnp.einsum("bij,bjk->bik", left_rot, direction, precision=HIGHEST)
    direction = jnp.einsum("bij,bkj->bik", direction, right_rot, precision=HIGHEST)
    weight = weight - learn_rate * (direction + weight_decay * weight)
    is_left = lax.axis_index("dp") % 2 == 0
    renewed = renew_all(jnp.where(is_left, left, right), jnp.where(is_left, left_rot, right_rot))
    other = swap(renewed, "dp", dp, 1)
    return (
        weight,
        first_moment,
        second_moment,
        left,
        right,
        jnp.where(is_left, renewed, other),
        jnp.where(is_left, other, renewed),
    )


def adam_update(weight, first_moment, second_moment, grad, decay_rate, rate):
    first_moment = beta_one * first_moment + (1.0 - beta_one) * grad
    second_moment = beta_two * second_moment + (1.0 - beta_two) * grad * grad
    direction = (
        first_moment
        / (1.0 - beta_one**STEP)
        / (jnp.sqrt(second_moment / (1.0 - beta_two**STEP)) + epsilon)
    )
    return (weight - rate * (direction + decay_rate * weight), first_moment, second_moment)


def shards(
    latents,
    actions,
    game_ids,
    action_masks,
    valid_steps,
    target_bins,
    target_fracs,
    continues,
    owner_order,
    blocks,
    block_first,
    block_second,
    left_stat,
    right_stat,
    left_basis,
    right_basis,
    latent_maps,
    latent_first,
    latent_second,
    head_weights,
    head_first,
    head_second,
    small_params,
    small_first,
    small_second,
    ema_critic,
    dp,
    fsdp,
):
    block_grad, maps_grad, packed_grad, square, sums = model_grads(
        latents, actions, game_ids, action_masks, valid_steps, target_bins, target_fracs, continues,
        owner_order, blocks, latent_maps, head_weights, small_params, dp, fsdp,
    )
    head_grad, small_grad = unpack_heads(packed_grad, small_params.shape[0])
    counted = sums[1]
    loss_value = sums[0] / counted
    grad_norm = jnp.sqrt(square) / counted
    factor = jnp.minimum(1.0, clip_norm / grad_norm) / counted
    soap_out = soap_update(
        blocks,
        block_first,
        block_second,
        left_stat,
        right_stat,
        left_basis,
        right_basis,
        block_grad * factor,
        dp,
    )
    maps_out = adam_update(
        latent_maps, latent_first, latent_second, maps_grad * factor, weight_decay, learn_rate
    )
    heads_out = adam_update(
        head_weights, head_first, head_second, head_grad * factor, weight_decay, learn_rate
    )
    small_out = adam_update(
        small_params, small_first, small_second, small_grad * factor, 0.0, small_rate
    )
    ema_new = ema_rate * ema_critic + (1.0 - ema_rate) * heads_out[0][:, BINS : 2 * BINS]
    return (
        loss_value,
        grad_norm,
        soap_out[0],
        soap_out[1],
        soap_out[2],
        soap_out[3],
        soap_out[4],
        soap_out[5],
        soap_out[6],
        maps_out[0],
        maps_out[1],
        maps_out[2],
        heads_out[0],
        heads_out[1],
        heads_out[2],
        small_out[0],
        small_out[1],
        small_out[2],
        ema_new,
    )


def solution(mesh):
    placed = (
        P(("dp", "fsdp"), None, None),
        P(("dp", "fsdp"), None),
        P(("dp", "fsdp")),
        P(),
        P(("dp", "fsdp"), None),
        P(("dp", "fsdp"), None, None),
        P(("dp", "fsdp"), None, None),
        P(("dp", "fsdp"), None),
        P(),
        P("fsdp", None, None),
        P("fsdp", None, None),
        P("fsdp", None, None),
        P("fsdp", None, None),
        P("fsdp", None, None),
        P("fsdp", None, None),
        P("fsdp", None, None),
        P("fsdp", None),
        P("fsdp", None),
        P("fsdp", None),
        P(),
        P(),
        P(),
        P(),
        P(),
        P(),
        P(),
    )
    return jax.shard_map(
        functools.partial(shards, dp=mesh.shape["dp"], fsdp=mesh.shape["fsdp"]),
        mesh=mesh,
        in_specs=placed,
        out_specs=(
            P(),
            P(),
            P("fsdp", None, None),
            P("fsdp", None, None),
            P("fsdp", None, None),
            P("fsdp", None, None),
            P("fsdp", None, None),
            P("fsdp", None, None),
            P("fsdp", None, None),
            P("fsdp", None),
            P("fsdp", None),
            P("fsdp", None),
            P(),
            P(),
            P(),
            P(),
            P(),
            P(),
            P(),
        ),
        check_vma=False,
    )
```
